512 devices in a mesh: row: 16 (over y, x), col: 32 (over z, core).
Axes of the slice: x: 4, y: 4, z: 16, core: 2. Of those that a mesh axis runs over, the one named last changes fastest.
Arguments:
- queries: bfloat16 [16, 1024, 3840], P('row', 'col'), may hold values from -240 to 240
- tree_latent: bfloat16 [16, 1024, 288], P('row', 'col'), may hold values from -6 to 6
- parents: int32 [16, 32, 32], P('row', 'col'), may hold values from -1 to 30, as said below
- cache: bfloat16 [16, 32, 256, 288], P('row', 'col'), may hold values from -6 to 6
- cache_lengths: int32 [16, 32], P('row', 'col'), may hold values from 1 to 256, 6144 in all within a row
- accepted: int32 [16, 32, 8], P('row', 'col'), may hold values from 0 to 31
- residual: bfloat16 [16, 1024, 2560], P(None, 'col', 'row'), may hold values from -6 to 6
- long_queries: bfloat16 [32, 32, 3840], P('col'), may hold values from -240 to 240
- long_tree_latent: bfloat16 [32, 32, 288], P('col'), may hold values from -6 to 6
- long_parents: int32 [32, 32], P('col'), may hold values from -1 to 30, as said below
- long_cache: bfloat16 [32, 4096, 288], P('col', 'row'), may hold values from -6 to 6
- long_plan: int32 [32, 16], P('col', 'row'), may hold values from 1 to 256, 3072 in all within a row
- long_residual: bfloat16 [32, 32, 2560], P('col', None, 'row'), may hold values from -6 to 6
- key_up: bfloat16 [2560, 256], P('col'), may hold values from -0.75 to 0.75
- value_up: bfloat16 [2560, 256], P('col'), may hold values from -0.375 to 0.375
- out_weight: bfloat16 [2560, 2560], P('col', 'row'), may hold values from -0.125 to 0.125
Outputs:
- hidden: bfloat16 [16, 1024, 2560], P(None, 'col', 'row')
- accepted_cache: bfloat16 [16, 32, 8, 288], P('row', 'col')
- long_hidden: bfloat16 [32, 32, 2560], P('col', None, 'row')
The draws below stay inside these ranges and needn't reach their ends.
Inputs may be any that keep to these rules, and one draw needn't show every extreme that they name: parents[..., 0] = -1 (the root); every other position's parent lies before it. long_parents[..., 0] = -1 (the root); every other position's parent lies before it.
All inputs are finite; a program needn't handle non-finite values. No bound on the sum of `cache_lengths` or of `long_plan` on one device may be relied on, other than what follows from the above.
Results may differ from the reference program's by a relative error of at most 0.0095.
Values may be sent and summed in bfloat16 or wider, within the bound.
No kernel may reach another device: no remote copies, remote signals or barrier semaphores. Data moves between devices by JAX's collectives and lax.ppermute only.
A program may use at most 128 MiB of HBM per device.

```python
import math
import jax
import jax.numpy as jnp
import numpy as np
from jax import lax

D = 2560
HEADS = 40
NOPE = 64
ROPE = 32
VDIM = 64
KVR = 256
TREE = 32
CACHE = 256
PIECE = 256
ACC = 8
REQ_C = 32
TOK_C = 1024
LONGS = 32
LONG_LEN = 4096
N_ROW = 16


def query_values(key, shape):
    base_draw = jax.random.normal(key, shape, jnp.float32)
    return jnp.clip(base_draw, -6.0, 6.0).astype(jnp.bfloat16)


def tree_parents(key, shape):
    positions = jnp.arange(TREE, dtype=jnp.int32)
    upper = jnp.maximum(positions, 1)
    drawn = jax.random.randint(key, shape, 0, upper)
    return jnp.where(positions == 0, -1, drawn).astype(jnp.int32)


def draw_queries(key, part):
    return query_values(key, (N_ROW, TOK_C, HEADS * (NOPE + ROPE)))


def draw_long_queries(key, part):
    return query_values(key, (LONGS, TREE, HEADS * (NOPE + ROPE)))


def draw_parents(key, part):
    return tree_parents(key, (N_ROW, REQ_C, TREE))


def draw_long_parents(key, part):
    return tree_parents(key, (LONGS, TREE))


def place_ends(values, own_key, smallest, high):
    extent = values.shape
    spot = [jax.random.randint(jax.random.fold_in(own_key, axis), (), 0, extent[axis]) for axis in range(len(extent))]
    values = values.at[tuple(spot)].set(smallest)
    longest = extent.index(max(extent))
    spot[longest] = (spot[longest] + 1) % extent[longest]
    return values.at[tuple(spot)].set(high)


def block_levels(key, dims, cuts, smallest, largest):
    factor_of, own = 1.0, jax.random.fold_in(key, 6)
    for axis_at, shards_of in cuts:
        steps = jnp.exp(jax.random.uniform(jax.random.fold_in(own, axis_at), (shards_of,), jnp.float32, smallest / len(cuts), largest / len(cuts)))
        factor_of = factor_of * jnp.repeat(steps, dims[axis_at] // shards_of).reshape([-1 if axis == axis_at else 1 for axis in range(len(dims))])
    return factor_of


def length_profile(amount, total, reach, skew):
    loads = [(1 << 20) // math.isqrt(grade ** skew) + 1 for grade in range(2, amount + 1)]
    surplus, given = total - reach - (amount - 1), [1] * (amount - 1)
    while surplus > 0:
        movable = [i for i in range(amount - 1) if given[i] < reach]
        mass, remaining = sum([loads[i] for i in movable]), surplus
        for i in movable:
            addition = min(reach - given[i], max(1, remaining * loads[i] // mass), surplus)
            given[i] = given[i] + addition
            surplus = surplus - addition
    return np.array([reach] + given)


def ragged(key, count, total, reach, skew):
    if count == 2:
        one = jax.random.randint(key, (), max(1, total - reach), min(reach, total - 1) + 1)
        return jnp.stack([one, total - one])
    tallies = jnp.asarray(length_profile(count, total, reach, skew), jnp.int32)
    pairs = (count - 1) // 2
    donor, receiver = tallies[1:1 + 2 * pairs:2], tallies[2:2 + 2 * pairs:2]
    room = jnp.minimum(donor - 1, reach - receiver)
    passed = jax.random.randint(jax.random.fold_in(key, 1), (pairs,), 0, 1 << 20) % (room + 1)
    tallies = tallies.at[1:1 + 2 * pairs:2].set(donor - passed).at[2:2 + 2 * pairs:2].set(receiver + passed)
    return tallies[jax.random.permutation(jax.random.fold_in(key, 2), count)]


def gaussian(key, shape, scale, limit, shards=(), kind=jnp.bfloat16):
    values = scale * jax.random.normal(key, shape, jnp.float32)
    if shards:
        values = values * block_levels(key, shape, shards, -0.22, 0.18)
    return jnp.clip(values, -limit, limit).astype(kind)


def setup_inputs(seed: int = 0) -> dict:
    splits = jax.random.split(jax.random.key(seed), 17)
    return {
        "queries": draw_queries(jax.random.fold_in(splits[16], 71), 0),
        "tree_latent": gaussian(splits[1], (N_ROW, TOK_C, KVR + ROPE), 1.0, 6.0, ((0, 16), (1, 32))),
        "parents": draw_parents(jax.random.fold_in(splits[16], 71), 0),
        "cache": gaussian(splits[3], (N_ROW, REQ_C, CACHE, KVR + ROPE), 1.0, 6.0, ((0, 16), (1, 32))),
        "cache_lengths": jax.vmap(lambda own: ragged(own, REQ_C, REQ_C * CACHE * 3 // 4, CACHE, 1))(jax.random.split(splits[4], N_ROW)).reshape((N_ROW, REQ_C)).astype(jnp.int32),
        "accepted": place_ends(jax.random.randint(splits[5], (N_ROW, REQ_C, ACC), 0, TREE), jax.random.fold_in(splits[5], 1), 0, TREE - 1).astype(jnp.int32),
        "residual": gaussian(splits[6], (N_ROW, TOK_C, D), 1.0, 6.0, ((1, 32), (2, 16))),
        "long_queries": draw_long_queries(jax.random.fold_in(splits[16], 71), 0),
        "long_tree_latent": gaussian(splits[8], (LONGS, TREE, KVR + ROPE), 1.0, 6.0, ((0, 32),)),
        "long_parents": draw_long_parents(jax.random.fold_in(splits[16], 71), 0),
        "long_cache": gaussian(splits[10], (LONGS, LONG_LEN, KVR + ROPE), 1.0, 6.0, ((0, 32), (1, 16))),
        "long_plan": jax.vmap(lambda own: ragged(own, N_ROW, PIECE * N_ROW * 3 // 4, PIECE, 1))(jax.random.split(splits[11], LONGS)).reshape((LONGS, N_ROW)).astype(jnp.int32),
        "long_residual": gaussian(splits[12], (LONGS, TREE, D), 1.0, 6.0, ((0, 32), (2, 16))),
        "key_up": gaussian(splits[13], (HEADS * NOPE, KVR), NOPE ** -0.5, 0.75, ((0, 32),)),
        "value_up": gaussian(splits[14], (HEADS * VDIM, KVR), KVR ** -0.5, 0.375, ((0, 32),)),
        "out_weight": gaussian(splits[15], (HEADS * VDIM, D), (HEADS * VDIM) ** -0.5, 0.125, ((0, 32), (1, 16))),
    }


def tree_reach(parent_ids):
    tree_count = parent_ids.shape[-1]
    positions = jnp.arange(tree_count, dtype=jnp.int32)
    reach_mat = (parent_ids[..., :, None] == positions).astype(jnp.float32)
    reach_mat = reach_mat + (positions[:, None] == positions[None, :]).astype(jnp.float32)
    for square_turn in range(max(1, (tree_count - 1).bit_length())):
        product = jnp.einsum("...ij,...jk->...ik", reach_mat, reach_mat, precision=lax.Precision.HIGHEST)
        reach_mat = jnp.minimum(reach_mat + product, 1.0)
    return reach_mat > 0.5


def query_cat(query_rows, key_up):
    per_head = query_rows.reshape(query_rows.shape[:-1] + (HEADS, NOPE + ROPE))
    nope_part = per_head[..., :NOPE].astype(jnp.float32)
    rope_part = per_head[..., NOPE:]
    key_heads = key_up.reshape(HEADS, NOPE, KVR).astype(jnp.float32)
    latent = jnp.einsum("...hd,hdk->...hk", nope_part, key_heads).astype(jnp.bfloat16)
    return jnp.concatenate([latent, rope_part], axis=-1)


def block_terms(query_block, key_rows, allowed):
    score_scale = (NOPE + ROPE) ** -0.5
    scores = jnp.einsum("thc,pc->thp", query_block.astype(jnp.float32), key_rows.astype(jnp.float32)) * score_scale
    scores = jnp.where(allowed[:, None, :], scores, -jnp.inf)
    row_max = jnp.max(scores, axis=-1)
    weights_row = jnp.where(allowed[:, None, :], jnp.exp(scores - row_max[..., None]), 0.0).astype(jnp.bfloat16)
    row_total = jnp.sum(weights_row.astype(jnp.float32), axis=-1)
    row_acc = jnp.einsum("thp,pk->thk", weights_row.astype(jnp.float32), key_rows[:, :KVR].astype(jnp.float32))
    return row_max, row_total, row_acc


def reference(queries, tree_latent, parents, cache, cache_lengths, accepted, residual, long_queries, long_tree_latent, long_parents, long_cache, long_plan, long_residual, key_up, value_up, out_weight):
    score_scale = (NOPE + ROPE) ** -0.5
    row_width = KVR + ROPE
    flat_count = N_ROW * REQ_C
    value_heads = value_up.reshape(HEADS, VDIM, KVR).astype(jnp.float32)

    def one_request(request_inputs):
        query_rows, latent_rows, parent_ids, cache_rows, length = request_inputs
        query_block = query_cat(query_rows, key_up)
        key_rows = jnp.concatenate([cache_rows, latent_rows], axis=0)
        cache_ok = jnp.broadcast_to((jnp.arange(CACHE, dtype=jnp.int32) < length)[None, :], (TREE, CACHE))
        allowed = jnp.concatenate([cache_ok, tree_reach(parent_ids)], axis=1)
        scores = jnp.einsum("thc,pc->thp", query_block.astype(jnp.float32), key_rows.astype(jnp.float32)) * score_scale
        scores = jnp.where(allowed[:, None, :], scores, -jnp.inf)
        row_max = jnp.max(scores, axis=-1, keepdims=True)
        exponent = jnp.exp(scores - row_max)
        probability = (exponent / jnp.sum(exponent, axis=-1, keepdims=True)).astype(jnp.bfloat16)
        latent = jnp.einsum("thp,pk->thk", probability.astype(jnp.float32), key_rows[:, :KVR].astype(jnp.float32)).astype(jnp.bfloat16)
        head_out = jnp.einsum("thk,hek->the", latent.astype(jnp.float32), value_heads).astype(jnp.bfloat16)
        return head_out.reshape(TREE, HEADS * VDIM)

    short_heads = lax.map(one_request, (
        queries.reshape(flat_count, TREE, HEADS * (NOPE + ROPE)),
        tree_latent.reshape(flat_count, TREE, row_width),
        parents.reshape(flat_count, TREE),
        cache.reshape(flat_count, CACHE, row_width),
        cache_lengths.reshape(flat_count)))
    projected = jnp.dot(short_heads.reshape(flat_count * TREE, HEADS * VDIM), out_weight, preferred_element_type=jnp.float32)
    hidden = (residual.astype(jnp.float32) + projected.reshape(N_ROW, TOK_C, D)).astype(jnp.bfloat16)

    latent_table = tree_latent.reshape(N_ROW, REQ_C, TREE, row_width)
    accepted_cache = jnp.take_along_axis(latent_table, accepted[..., None], axis=2)

    def one_long(long_inputs):
        query_rows, latent_rows, parent_ids, cache_rows, plan_len = long_inputs
        query_block = query_cat(query_rows, key_up)
        pieces = cache_rows.reshape(N_ROW, PIECE, row_width)
        valid_mask = jnp.arange(PIECE, dtype=jnp.int32)[None, :] < plan_len[:, None]

        def piece_terms(piece_rows, piece_ok):
            return block_terms(query_block, piece_rows, jnp.broadcast_to(piece_ok[None, :], (TREE, PIECE)))

        piece_max, piece_total, piece_acc = jax.vmap(piece_terms)(pieces, valid_mask)
        tree_max, tree_total, tree_acc = block_terms(query_block, latent_rows, tree_reach(parent_ids))
        overall = jnp.maximum(jnp.max(piece_max, axis=0), tree_max)
        piece_factor = jnp.exp(piece_max - overall[None])
        tree_factor = jnp.exp(tree_max - overall)
        denominator = jnp.sum(piece_total * piece_factor, axis=0) + tree_total * tree_factor
        numerator = jnp.sum(piece_acc * piece_factor[..., None], axis=0) + tree_acc * tree_factor[..., None]
        head_out = jnp.einsum("thk,hek->the", numerator, value_heads, precision=lax.Precision.HIGHEST) / denominator[..., None]
        return head_out.astype(jnp.bfloat16).reshape(TREE, HEADS * VDIM)

    long_heads = lax.map(one_long, (long_queries, long_tree_latent, long_parents, long_cache, long_plan))
    long_projected = jnp.dot(long_heads.reshape(LONGS * TREE, HEADS * VDIM), out_weight, preferred_element_type=jnp.float32)
    long_hidden = (long_residual.astype(jnp.float32) + long_projected.reshape(LONGS, TREE, D)).astype(jnp.bfloat16)
    return hidden, accepted_cache, long_hidden
```

```python
import jax
import jax.numpy as jnp
from jax import lax
from jax.experimental import pallas as pl
from jax.experimental.pallas import tpu as pltpu
from jax.sharding import Mesh, PartitionSpec as P

HEADS = 40
NOPE = 64
ROPE = 32
VDIM = 64
KVR = 256
TREE = 32
ROWS = ("y", "x")
COLS = ("z", "c")
SWAP = [(0, 1), (1, 0)]
BF = jnp.bfloat16
F32 = jnp.float32


def tree_reach(parent_ids):
    tree_count = parent_ids.shape[-1]
    positions = jnp.arange(tree_count, dtype=jnp.int32)
    reach = (parent_ids[..., :, None] == positions).astype(F32)
    reach = reach + (positions[:, None] == positions[None, :]).astype(F32)
    for _ in range(max(1, (tree_count - 1).bit_length())):
        product = jnp.einsum("...ij,...jk->...ik", reach, reach, preferred_element_type=F32)
        reach = jnp.minimum(reach + product, 1.0)
    return reach > 0.5


def spread(value, axes, count):
    return lax.all_to_all(jnp.broadcast_to(value[None], (count,) + value.shape), axes, 0, 0)


def split3(value):
    high = value.astype(BF)
    rest = value - high.astype(F32)
    mid = rest.astype(BF)
    return high, mid, (rest - mid.astype(F32)).astype(BF)


def attend_kernel(place, qn, qr, keys, bias, mine, twin, out, kv, lat, sems):
    z, c = place[0], place[1]
    nz, shard = mine.shape[0], mine.shape[1]
    copies = []
    for i in range(nz):
        for k, (source, part) in enumerate(((mine, c), (twin, 1 - c))):
            row = pl.multiple_of(lax.rem(z + i, nz) * (2 * shard) + part * shard, 16)
            copies.append(pltpu.make_async_copy(source.at[i], kv.at[pl.ds(row, shard)], sems.at[k * nz + i]))
    for copy in copies:
        copy.start()
    for copy in copies:
        copy.wait()
    for h in range(HEADS):
        part = jnp.dot(qn[h], kv[NOPE * h : NOPE * (h + 1), :KVR], preferred_element_type=F32).astype(BF)
        lat[0, TREE * h : TREE * (h + 1)] = part[:TREE]
        lat[1, TREE * h : TREE * (h + 1)] = part[TREE:]
    lanes = lax.broadcasted_iota(jnp.int32, (TREE, 128), 1)
    logs = jnp.zeros((TREE, 128), F32)
    group = 8
    size = group * TREE
    over_last = (((1,), (1,)), ((), ()))
    for g in range(2):
        for i in range(HEADS // group):
            rows = slice(size * i, size * (i + 1))
            scores = lax.dot_general(lat[g, rows], keys[g, :, :KVR], over_last, preferred_element_type=F32)
            scores += lax.dot_general(qr[g, rows], keys[g, :, KVR:], over_last, preferred_element_type=F32)
            scores = scores * (NOPE + ROPE) ** -0.5
            scores = (scores.reshape(group, TREE, -1) + bias[g][None]).reshape(size, -1)
            top = jnp.max(scores, axis=-1, keepdims=True)
            weights = jnp.exp(scores - top)
            total = jnp.sum(weights, axis=-1, keepdims=True)
            acc = jnp.dot(weights.astype(BF), keys[g, :, :KVR], preferred_element_type=F32)
            lat[g, rows] = (acc / total).astype(BF)
            if g == 1:
                column = top + jnp.log(total)
                for k in range(group):
                    logs = jnp.where(lanes == group * i + k, column[TREE * k : TREE * (k + 1)], logs)
    count = out.shape[0]
    for j in range(HEADS // 4):
        quad = []
        for h in range(4 * j, 4 * j + 4):
            both = jnp.concatenate([lat[g, TREE * h : TREE * (h + 1)] for g in range(2)], axis=0)
            rows = kv[VDIM * h : VDIM * (h + 1), KVR:]
            quad.append(lax.dot_general(both, rows, over_last, preferred_element_type=F32))
        heads = jnp.concatenate(quad, axis=1).astype(BF)
        for d in range(count):
            out[d, 2 * TREE * j : 2 * TREE * (j + 1)] = heads
    high, mid, low = split3(logs)
    base = 2 * TREE * (HEADS // 4)
    for d in range(count):
        out[d, base : base + TREE, :128] = high
        out[d, base : base + TREE, 128:] = mid
        out[d, base + TREE : base + 2 * TREE, :128] = low
        out[d, base + TREE : base + 2 * TREE, 128:] = low


def read_logs(parts, base):
    high = parts[:, base : base + TREE, :128].astype(F32)
    mid = parts[:, base : base + TREE, 128:].astype(F32)
    return high + mid + parts[:, base + TREE : base + 2 * TREE, :128].astype(F32)


def join_pieces(parts, base, pick):
    logs = read_logs(parts, base)
    count = logs.shape[0]
    top = jnp.max(logs, axis=0)
    share = jnp.exp(logs - top[None])
    total = jnp.sum(share, axis=0)
    share = (share / total[None]).reshape(count * TREE, 128)
    high = share.astype(BF)
    low = (share - high.astype(F32)).astype(BF)
    joined = []
    for j in range(HEADS // 4):
        owner = lax.broadcasted_iota(jnp.int32, (128, 256), 1) // VDIM + 4 * j
        select = jnp.where(lax.broadcasted_iota(jnp.int32, (128, 256), 0) == owner, 1.0, 0.0).astype(BF)
        wide = jnp.dot(high, select, preferred_element_type=F32) + jnp.dot(low, select, preferred_element_type=F32)
        piece = pick(j).astype(F32) * wide.reshape(count, TREE, 256)
        joined.append(jnp.sum(piece, axis=0).astype(BF))
    return joined, top + jnp.log(total)


def project(rows, weight):
    span = HEADS * VDIM // 4
    lanes = lax.broadcasted_iota(jnp.int32, (rows.shape[0], 128), 1) // 32
    tail = weight[16:20].reshape(span, 128)
    main = jnp.zeros((rows.shape[0], 128), F32)
    rest = jnp.zeros((rows.shape[0], 128), F32)
    for g in range(4):
        left = rows[:, span * g : span * (g + 1)]
        block = weight[4 * g : 4 * (g + 1)].reshape(span, 128)
        main += jnp.dot(left, block, preferred_element_type=F32)
        rest += jnp.where(lanes == g, jnp.dot(left, tail, preferred_element_type=F32), 0.0)
    rest = rest + pltpu.roll(rest, 64, 1)
    return main, rest + pltpu.roll(rest, 32, 1)


def project_kernel(place, got, *refs):
    owns, twins, (send, weight, rows, sems) = refs[:4], refs[4:8], refs[8:]
    c, x = place[1], place[2]
    copies = []
    for k in range(4):
        copies.append(pltpu.make_async_copy(owns[k], weight.at[k, :, c], sems.at[k]))
        copies.append(pltpu.make_async_copy(twins[k], weight.at[k, :, 1 - c], sems.at[4 + k]))
    for copy in copies:
        copy.start()
    chunks = HEADS // 4
    for j in range(chunks):
        rows[:, 256 * j : 256 * (j + 1)] = got[:, 2 * TREE * j : 2 * TREE * j + TREE].reshape(4 * TREE, 256)
    base = 2 * TREE * chunks
    joined, logs = join_pieces(got, base, lambda j: got[:, 2 * TREE * j + TREE : 2 * TREE * (j + 1)])
    high, mid, low = split3(logs)
    first = 4 * TREE
    last = first + TREE * chunks
    for d in range(4):
        for j in range(chunks):
            send[d, first + TREE * j : first + TREE * (j + 1)] = joined[j]
        send[d, last : last + TREE, :128] = high
        send[d, last : last + TREE, 128:] = mid
        send[d, last + TREE :, :128] = low
        send[d, last + TREE :, 128:] = low
    for copy in copies:
        copy.wait()
    for k in range(4):
        main, rest = project(rows[...], weight[k])
        target = lax.rem(x + k, 4)
        send[target, :first, :128] = main.astype(BF)
        send[target, :first, 128:] = rest.astype(BF)


def finish_kernel(place, got, own, twin, residual, long_residual, hidden, long_hidden, weight, rows, sems):
    c = place[1]
    copies = [
        pltpu.make_async_copy(own, weight.at[:, c], sems.at[0]),
        pltpu.make_async_copy(twin, weight.at[:, 1 - c], sems.at[1]),
    ]
    for copy in copies:
        copy.start()
    for y in range(4):
        for x in range(4):
            piece = got[x, TREE * y : TREE * (y + 1)]
            for part in (slice(0, 128), slice(128, 160)):
                total = residual[4 * y + x, :, part].astype(F32) + piece[:, part].astype(F32)
                hidden[4 * y + x, :, part] = total.astype(BF)
    first = 4 * TREE
    chunks = HEADS // 4
    joined, _ = join_pieces(got, first + TREE * chunks, lambda j: got[:, first + TREE * j : first + TREE * (j + 1)])
    for j in range(chunks):
        rows[:, 256 * j : 256 * (j + 1)] = joined[j]
    for copy in copies:
        copy.wait()
    main, rest = project(rows[...], weight[...])
    long_hidden[0, :, :128] = (long_residual[0, :, :128].astype(F32) + main).astype(BF)
    long_hidden[0, :, 128:160] = (long_residual[0, :, 128:160].astype(F32) + rest[:, :32]).astype(BF)


SMEM = pl.BlockSpec(memory_space=pltpu.SMEM)
VMEM = pl.BlockSpec(memory_space=pltpu.VMEM)
ANY = pl.BlockSpec(memory_space=pl.ANY)
PARAMS = pltpu.CompilerParams(vmem_limit_bytes=48 << 20)


def on_device(
    queries, tree_latent, parents, cache, cache_lengths, accepted, residual,
    long_queries, long_tree_latent, long_parents, long_cache, long_plan, long_residual,
    key_up, value_up, out_weight,
):
    ny, nx, nz = lax.axis_size("y"), lax.axis_size("x"), lax.axis_size("z")
    nr = ny * nx
    x, z, c = lax.axis_index("x"), lax.axis_index("z"), lax.axis_index("c")
    r = lax.axis_index(ROWS)
    place = jnp.stack([z, c, x]).astype(jnp.int32)
    kv = jnp.concatenate([key_up, value_up], axis=1)
    pairs = [(i * nz + (j + i) % nz, i * nz + j) for i in range(nr) for j in range(nz)]
    kv = lax.ppermute(kv, ("y", "x", "z"), pairs)
    mine = spread(kv, ROWS, nr)
    twin = lax.ppermute(mine, "c", SWAP)
    held, step = out_weight[None], nz // 2
    while step:
        more = lax.ppermute(held, "z", [((j + step) % nz, j) for j in range(nz)])
        held = jnp.stack([held, more], axis=1).reshape((-1,) + out_weight.shape)
        step //= 2
    held = jnp.roll(held, z, axis=0)
    shard = out_weight.shape[0]
    tail = held[:, :, 128:].reshape(4, 4 * shard, 32).transpose(1, 0, 2).reshape(4, shard, 128)
    held = jnp.concatenate([held[:, :, :128], tail], axis=0)
    owns = [held] + [lax.ppermute(held, "x", [((j + k) % nx, j) for j in range(nx)]) for k in range(1, nx)]
    twins = [lax.ppermute(block, "c", SWAP) for block in owns]

    per_head = jnp.concatenate([queries[0], long_queries[0]], axis=0).reshape(2 * TREE, HEADS, NOPE + ROPE)
    per_head = per_head.transpose(1, 0, 2)
    rope = per_head[..., NOPE:].reshape(HEADS, 2, TREE, ROPE).transpose(1, 0, 2, 3)
    rope = rope.reshape(2, HEADS * TREE, ROPE)
    keys = jnp.stack([
        jnp.concatenate([cache[0, 0], tree_latent[0]], axis=0),
        jnp.concatenate([long_cache[0], long_tree_latent[0]], axis=0),
    ])
    slots = cache.shape[2]
    lengths = jnp.stack([cache_lengths[0, 0], long_plan[0, 0]])
    cache_ok = jnp.arange(slots, dtype=jnp.int32)[None, None, :] < lengths[:, None, None]
    reach = tree_reach(jnp.concatenate([parents[0], long_parents], axis=0))
    reach = reach & ((jnp.arange(2) == 0) | (r == 0))[:, None, None]
    allowed = jnp.concatenate([jnp.broadcast_to(cache_ok, (2, TREE, slots)), reach], axis=2)
    bias = jnp.where(allowed, 0.0, -jnp.inf).astype(F32)

    chunks = HEADS // 4
    heads = pl.pallas_call(
        attend_kernel,
        out_shape=jax.ShapeDtypeStruct((ny, 2 * TREE * (chunks + 1), 256), BF),
        in_specs=[SMEM, VMEM, VMEM, VMEM, VMEM, ANY, ANY],
        out_specs=VMEM,
        scratch_shapes=[
            pltpu.VMEM((HEADS * NOPE, 2 * KVR), BF),
            pltpu.VMEM((2, HEADS * TREE, KVR), BF),
            pltpu.SemaphoreType.DMA((2 * nz,)),
        ],
        compiler_params=PARAMS,
    )(place, per_head[..., :NOPE], rope, keys, bias, mine, twin)
    got = lax.all_to_all(heads, "y", 0, 0)
    send = pl.pallas_call(
        project_kernel,
        out_shape=jax.ShapeDtypeStruct((nx, (ny + chunks + 2) * TREE, 256), BF),
        in_specs=[SMEM, VMEM] + [ANY] * 8,
        out_specs=VMEM,
        scratch_shapes=[
            pltpu.VMEM((nx, 20, 2, shard, 128), BF),
            pltpu.VMEM((ny * TREE, HEADS * VDIM), BF),
            pltpu.SemaphoreType.DMA((8,)),
        ],
        compiler_params=PARAMS,
    )(place, got, *owns, *twins)
    back = lax.all_to_all(send, "x", 0, 0)
    hidden, long_hidden = pl.pallas_call(
        finish_kernel,
        out_shape=(
            jax.ShapeDtypeStruct(residual.shape, BF),
            jax.ShapeDtypeStruct(long_residual.shape, BF),
        ),
        in_specs=[SMEM, VMEM, ANY, ANY, VMEM, VMEM],
        out_specs=(VMEM, VMEM),
        scratch_shapes=[
            pltpu.VMEM((20, 2, shard, 128), BF),
            pltpu.VMEM((TREE, HEADS * VDIM), BF),
            pltpu.SemaphoreType.DMA((2,)),
        ],
        compiler_params=PARAMS,
    )(place, back, owns[0], twins[0], residual, long_residual)
    accepted_cache = jnp.take_along_axis(tree_latent[0], accepted[0, 0][:, None], axis=0)[None, None]
    return hidden, accepted_cache, long_hidden


def solution(mesh):
    split = Mesh(mesh.devices.reshape(4, 4, 16, 2), ("y", "x", "z", "c"))
    return jax.shard_map(
        on_device,
        mesh=split,
        in_specs=(
            P(ROWS, COLS, None),
            P(ROWS, COLS, None),
            P(ROWS, COLS, None),
            P(ROWS, COLS, None, None),
            P(ROWS, COLS),
            P(ROWS, COLS, None),
            P(None, COLS, ROWS),
            P(COLS, None, None),
            P(COLS, None, None),
            P(COLS, None),
            P(COLS, ROWS, None),
            P(COLS, ROWS),
            P(COLS, None, ROWS),
            P(COLS, None),
            P(COLS, None),
            P(COLS, ROWS),
        ),
        out_specs=(P(None, COLS, ROWS), P(ROWS, COLS, None, None), P(COLS, None, ROWS)),
        check_vma=False,
    )
```

```python
import jax
import jax.numpy as jnp
from jax import lax
from jax.experimental import pallas as pl
from jax.experimental.pallas import tpu as pltpu
from jax.sharding import Mesh, PartitionSpec as P

HEADS = 40
NOPE = 64
ROPE = 32
VDIM = 64
KVR = 256
TREE = 32
ROWS = ("y", "x")
COLS = ("z", "c")
SWAP = [(0, 1), (1, 0)]
BF = jnp.bfloat16
F32 = jnp.float32


def tree_reach(parent_ids):
    tree_count = parent_ids.shape[-1]
    positions = jnp.arange(tree_count, dtype=jnp.int32)
    reach = (parent_ids[..., :, None] == positions).astype(F32)
    reach = reach + (positions[:, None] == positions[None, :]).astype(F32)
    for _ in range(max(1, (tree_count - 1).bit_length())):
        product = jnp.einsum("...ij,...jk->...ik", reach, reach, preferred_element_type=F32)
        reach = jnp.minimum(reach + product, 1.0)
    return reach > 0.5


OVER_LAST = (((1,), (1,)), ((), ()))
SLICE = HEADS // 4
SPAN = SLICE * VDIM
LONG_AT, TREE_AT, QUERY_AT, BLOCK = 576, 1152, 1280, 1536
TOKENS = 16 * TREE + TREE
QUARTER = TOKENS // 4


def split3(value):
    high = value.astype(BF)
    rest = value - high.astype(F32)
    mid = rest.astype(BF)
    return high, mid, (rest - mid.astype(F32)).astype(BF)


def dot(left, right):
    return jnp.dot(left, right, preferred_element_type=F32)


def dot_t(left, right):
    return lax.dot_general(left, right, OVER_LAST, preferred_element_type=F32)


def place_shards(z, c, mine, twin, target, sems):
    copies = []
    for j in range(4):
        at = lax.rem(lax.rem(z, 4) + 4 - j, 4)
        copies.append(pltpu.make_async_copy(mine.at[j], target.at[at, c], sems.at[j]))
        copies.append(pltpu.make_async_copy(twin.at[j], target.at[at, 1 - c], sems.at[4 + j]))
    for copy in copies:
        copy.start()
    return copies


def attend_kernel(place, got, query_l, tree_l, mine, twin, out, kv, lat, sems):
    copies = place_shards(place[0], place[1], mine, twin, kv, sems)
    lanes = lax.broadcasted_iota(jnp.int32, (TREE, 128), 1)
    slots = lax.broadcasted_iota(jnp.int32, (1, 256), 1).astype(F32)
    scale = (NOPE + ROPE) ** -0.5
    size = SLICE * TREE

    def rope_rows(chunk):
        zero = jnp.zeros((TREE, 128), BF)
        return jnp.concatenate([jnp.where(lanes // 32 == h % 4, chunk(5 + h // 4), zero) for h in range(SLICE)], axis=0)

    def cached(query, rope, block, at, length):
        keys = jnp.concatenate([block[at : at + 288], block[at + 288 : at + 576]], axis=1)
        scores = dot(query, keys[:KVR]) + dot(rope, jnp.concatenate([keys[KVR:]] * 4, axis=0))
        return jnp.where(slots < length, scores * scale, -jnp.inf), keys[:KVR]

    def treed(query, rope, block, at):
        keys = jnp.concatenate([block[at : at + TREE], block[at + TREE : at + 2 * TREE]], axis=1)
        scores = dot_t(query, keys) + dot_t(rope, block[at + 2 * TREE : at + 3 * TREE])
        reach = block[at + 3 * TREE : at + 4 * TREE, :TREE].astype(F32)
        reach = jnp.concatenate([reach] * SLICE, axis=0)
        return jnp.where(reach > 0.5, scores * scale, -jnp.inf), keys

    for copy in copies:
        copy.wait()
    for p in range(SLICE // 2):
        at = TREE * p
        rows = [got[k, QUERY_AT + at : QUERY_AT + at + TREE] for k in range(4)] + [query_l[at : at + TREE]]
        even = [jnp.where(lanes < NOPE, row, jnp.zeros_like(row)) for row in rows]
        odd = [jnp.where(lanes < NOPE, jnp.zeros_like(row), row) for row in rows]
        weight = kv[...][:, :, :, :KVR].reshape(SPAN, KVR)[128 * p : 128 * (p + 1)]
        part = dot(jnp.concatenate(even + odd, axis=0), weight).astype(BF)
        for s in range(2):
            for k in range(5):
                lat[k, TREE * (2 * p + s) : TREE * (2 * p + s + 1)] = part[TREE * (5 * s + k) : TREE * (5 * s + k + 1)]

    for k in range(4):
        block = got.at[k]
        query = lat[k]
        rope = rope_rows(lambda i: block[QUERY_AT + TREE * i : QUERY_AT + TREE * (i + 1)])
        length = block[TREE_AT + 3 * TREE : TREE_AT + 3 * TREE + 1, 32:33].astype(F32)
        first, keys = cached(query, rope, block, 0, length)
        second, tree = treed(query, rope, block, TREE_AT)
        top = jnp.maximum(jnp.max(first, axis=-1, keepdims=True), jnp.max(second, axis=-1, keepdims=True))
        first, second = jnp.exp(first - top), jnp.exp(second - top)
        total = jnp.sum(first, axis=-1, keepdims=True) + jnp.sum(second, axis=-1, keepdims=True)
        acc = dot_t(first.astype(BF), keys) + dot(second.astype(BF), tree)
        lat[k] = (acc / total).astype(BF)

    query = lat[4]
    rope = rope_rows(lambda i: query_l[TREE * i : TREE * (i + 1)])
    second, tree = treed(query, rope, tree_l, 0)
    scored = []
    for k in range(4):
        block = got.at[k]
        length = block[TREE_AT + 3 * TREE : TREE_AT + 3 * TREE + 1, 33:34].astype(F32)
        scored.append(cached(query, rope, block, LONG_AT, length))
    top = jnp.max(second, axis=-1, keepdims=True)
    for scores, _ in scored:
        top = jnp.maximum(top, jnp.max(scores, axis=-1, keepdims=True))
    second = jnp.exp(second - top)
    total = jnp.sum(second, axis=-1, keepdims=True)
    acc = dot(second.astype(BF), tree)
    for scores, keys in scored:
        weights = jnp.exp(scores - top)
        total += jnp.sum(weights, axis=-1, keepdims=True)
        acc += dot_t(weights.astype(BF), keys)
    lat[4] = (acc / total).astype(BF)
    column = top + jnp.log(total)
    logs = jnp.zeros((TREE, 128), F32)
    for h in range(SLICE):
        logs = jnp.where(lanes == h, column[TREE * h : TREE * (h + 1)], logs)

    for p in range(SLICE // 2):
        pair = []
        for h in (2 * p, 2 * p + 1):
            rows = jnp.concatenate([lat[k, TREE * h : TREE * (h + 1)] for k in range(5)], axis=0)
            weight = kv[...][:, :, :, KVR:].reshape(SPAN, KVR)[VDIM * h : VDIM * (h + 1)]
            pair.append(dot_t(rows, weight))
        heads = jnp.concatenate(pair, axis=1).astype(BF)
        for d in range(4):
            out[d, 5 * TREE * p : 5 * TREE * (p + 1)] = heads
    base = 5 * TREE * (SLICE // 2)
    for i, part in enumerate(split3(logs)):
        for d in range(4):
            out[d, base + TREE * i : base + TREE * (i + 1)] = part


def project_kernel(place, got, mine, twin, send, weight, rows, sems):
    copies = place_shards(place[0], place[1], mine, twin, weight, sems)
    base = 5 * TREE * (SLICE // 2)
    logs = sum(got[:, base + TREE * i : base + TREE * (i + 1)].astype(F32) for i in range(3))
    share = jnp.exp(logs - jnp.max(logs, axis=0)[None])
    share = (share / jnp.sum(share, axis=0)[None]).reshape(4 * TREE, 128)
    high = share.astype(BF)
    low = (share - high.astype(F32)).astype(BF)
    for p in range(SLICE // 2):
        at = 5 * TREE * p
        cols = slice(128 * p, 128 * (p + 1))
        for y in range(4):
            rows[4 * TREE * y : 4 * TREE * (y + 1), cols] = got[y, at : at + 4 * TREE]
        owner = lax.broadcasted_iota(jnp.int32, (128, 128), 1) // VDIM + 2 * p
        select = jnp.where(lax.broadcasted_iota(jnp.int32, (128, 128), 0) == owner, 1.0, 0.0).astype(BF)
        wide = (dot(high, select) + dot(low, select)).reshape(4, TREE, 128)
        piece = got[:, at + 4 * TREE : at + 5 * TREE].astype(F32) * wide
        rows[16 * TREE : 17 * TREE, cols] = jnp.sum(piece, axis=0).astype(BF)
    for copy in copies:
        copy.wait()
    full = weight[...].reshape(SPAN, 640)
    for x in range(4):
        send[x, :TOKENS] = dot(rows[...], full[:, 128 * x : 128 * (x + 1)]).astype(BF)
    rest = dot(rows[...], full[:, 512:])
    lanes = lax.broadcasted_iota(jnp.int32, (QUARTER, 128), 1) // 32
    for x in range(4):
        packed = jnp.zeros((QUARTER, 128), F32)
        for g in range(4):
            part = rest[QUARTER * g : QUARTER * (g + 1)]
            shift = (32 * (g - x)) % 128
            part = pltpu.roll(part, shift, 1) if shift else part
            packed = jnp.where(lanes == g, part, packed)
        send[x, TOKENS : TOKENS + QUARTER] = packed.astype(BF)
        send[x, TOKENS + QUARTER :] = jnp.zeros((send.shape[1] - TOKENS - QUARTER, 128), BF)


def finish_kernel(got, residual, long_residual, hidden, long_hidden, tail):
    rest = jnp.sum(got[:, TOKENS : TOKENS + QUARTER].astype(F32), axis=0)
    for g in range(4):
        tail[QUARTER * g : QUARTER * (g + 1)] = pltpu.roll(rest, (-32 * g) % 128, 1) if g else rest
    for i in range(17):
        at = slice(TREE * i, TREE * (i + 1))
        main = jnp.sum(got[:, at].astype(F32), axis=0)
        source, target, k = (residual, hidden, i) if i < 16 else (long_residual, long_hidden, 0)
        target[k, :, :128] = (source[k, :, :128].astype(F32) + main).astype(BF)
        target[k, :, 128:160] = (source[k, :, 128:160].astype(F32) + tail[at, :32]).astype(BF)


SMEM = pl.BlockSpec(memory_space=pltpu.SMEM)
VMEM = pl.BlockSpec(memory_space=pltpu.VMEM)
ANY = pl.BlockSpec(memory_space=pl.ANY)
PARAMS = pltpu.CompilerParams(vmem_limit_bytes=48 << 20)


def slice_queries(queries):
    heads = queries.reshape(TREE, 4, SLICE, NOPE + ROPE)
    nope = heads[..., :NOPE].reshape(TREE, 4, SLICE // 2, 128).transpose(1, 2, 0, 3)
    rope = heads[..., NOPE:].reshape(TREE, 4, SLICE * ROPE)
    rope = jnp.pad(rope, ((0, 0), (0, 0), (0, 64))).reshape(TREE, 4, 3, 128).transpose(1, 2, 0, 3)
    return jnp.concatenate([nope, rope], axis=1).reshape(4, 8 * TREE, 128)


def tree_block(rows, reach, lengths):
    extra = jnp.concatenate([reach.astype(BF), jnp.broadcast_to(lengths.astype(BF)[None], (TREE, 2))], axis=1)
    extra = jnp.pad(extra, ((0, 0), (0, 128 - extra.shape[1])))
    rope = jnp.concatenate([rows[:, KVR:]] * 4, axis=1)
    return jnp.concatenate([rows[:, :128], rows[:, 128:KVR], rope, extra], axis=0)


def fetch_slice(value, nx, nz):
    parts = []
    for j in range(4):
        pairs = [
            (i * nz + 4 * k + m, k * nz + 4 * i + (m + j) % 4) for i in range(nx) for k in range(nx) for m in range(4)
        ]
        parts.append(lax.ppermute(value, ("x", "z"), pairs))
    return jnp.stack(parts)


def on_device(
    queries, tree_latent, parents, cache, cache_lengths, accepted, residual,
    long_queries, long_tree_latent, long_parents, long_cache, long_plan, long_residual,
    key_up, value_up, out_weight,
):
    nx, nz = lax.axis_size("x"), lax.axis_size("z")
    y, x, z, c = lax.axis_index("y"), lax.axis_index("x"), lax.axis_index("z"), lax.axis_index("c")
    place = jnp.stack([z, c]).astype(jnp.int32)
    kv = fetch_slice(jnp.concatenate([key_up, value_up], axis=1), nx, nz)
    kv_twin = lax.ppermute(kv, "c", SWAP)
    cols = lax.all_gather(out_weight, "x")
    cols = jnp.concatenate([cols[k, :, :128] for k in range(nx)] + [cols[k, :, 128:] for k in range(nx)], axis=1)
    out_rows = fetch_slice(cols, nx, nz)
    out_twin = lax.ppermute(out_rows, "c", SWAP)

    reach = tree_reach(jnp.concatenate([parents[0], long_parents], axis=0))
    lengths = jnp.concatenate([cache_lengths[0], long_plan[0]])
    short_t, long_t = cache[0, 0].T, long_cache[0].T
    keys = jnp.concatenate([short_t[:, :128], short_t[:, 128:], long_t[:, :128], long_t[:, 128:]], axis=0)
    keys = jnp.concatenate([keys, tree_block(tree_latent[0], reach[0], lengths)], axis=0)
    block = jnp.concatenate(
        [jnp.broadcast_to(keys[None], (nx,) + keys.shape), slice_queries(queries[0])], axis=1
    )
    got = lax.all_to_all(block, "x", 0, 0)
    query_l = lax.dynamic_index_in_dim(slice_queries(long_queries[0]), x, 0, keepdims=False)
    tree_l = tree_block(long_tree_latent[0], reach[1] & (y == 0), lengths)
    shard = key_up.shape[0]

    heads = pl.pallas_call(
        attend_kernel,
        out_shape=jax.ShapeDtypeStruct((4, 5 * TREE * (SLICE // 2) + 3 * TREE, 128), BF),
        in_specs=[SMEM, VMEM, VMEM, VMEM, ANY, ANY],
        out_specs=VMEM,
        scratch_shapes=[
            pltpu.VMEM((4, 2, shard, 2 * KVR), BF),
            pltpu.VMEM((5, SLICE * TREE, KVR), BF),
            pltpu.SemaphoreType.DMA((8,)),
        ],
        compiler_params=PARAMS,
    )(place, got, query_l, tree_l, kv, kv_twin)
    shared = lax.all_to_all(heads, "y", 0, 0)
    send = pl.pallas_call(
        project_kernel,
        out_shape=jax.ShapeDtypeStruct((4, 688, 128), BF),
        in_specs=[SMEM, VMEM, ANY, ANY],
        out_specs=VMEM,
        scratch_shapes=[
            pltpu.VMEM((4, 2, shard, 640), BF),
            pltpu.VMEM((TOKENS, SPAN), BF),
            pltpu.SemaphoreType.DMA((8,)),
        ],
        compiler_params=PARAMS,
    )(place, shared, out_rows, out_twin)
    back = lax.all_to_all(send, "x", 0, 0)
    hidden, long_hidden = pl.pallas_call(
        finish_kernel,
        out_shape=(
            jax.ShapeDtypeStruct(residual.shape, BF),
            jax.ShapeDtypeStruct(long_residual.shape, BF),
        ),
        in_specs=[VMEM, VMEM, VMEM],
        out_specs=(VMEM, VMEM),
        scratch_shapes=[pltpu.VMEM((TOKENS, 128), F32)],
        compiler_params=PARAMS,
    )(back, residual, long_residual)
    accepted_cache = jnp.take_along_axis(tree_latent[0], accepted[0, 0][:, None], axis=0)[None, None]
    return hidden, accepted_cache, long_hidden


def solution(mesh):
    split = Mesh(mesh.devices.reshape(4, 4, 16, 2), ("y", "x", "z", "c"))
    return jax.shard_map(
        on_device,
        mesh=split,
        in_specs=(
            P(ROWS, COLS, None),
            P(ROWS, COLS, None),
            P(ROWS, COLS, None),
            P(ROWS, COLS, None, None),
            P(ROWS, COLS),
            P(ROWS, COLS, None),
            P(None, COLS, ROWS),
            P(COLS, None, None),
            P(COLS, None, None),
            P(COLS, None),
            P(COLS, ROWS, None),
            P(COLS, ROWS),
            P(COLS, None, ROWS),
            P(COLS, None),
            P(COLS, None),
            P(COLS, ROWS),
        ),
        out_specs=(P(None, COLS, ROWS), P(ROWS, COLS, None, None), P(COLS, None, ROWS)),
        check_vma=False,
    )
```

```python
import jax
import jax.numpy as jnp
from jax import lax
from jax.experimental import pallas as pl
from jax.experimental.pallas import tpu as pltpu
from jax.sharding import Mesh, PartitionSpec as P

HEADS = 40
NOPE = 64
ROPE = 32
VDIM = 64
KVR = 256
TREE = 32
ROWS = ("y", "x")
COLS = ("a", "b", "c")
SWAP = [(0, 1), (1, 0)]
BF = jnp.bfloat16
F32 = jnp.float32


def tree_reach(parent_ids):
    tree_count = parent_ids.shape[-1]
    positions = jnp.arange(tree_count, dtype=jnp.int32)
    reach = (parent_ids[..., :, None] == positions).astype(F32)
    reach = reach + (positions[:, None] == positions[None, :]).astype(F32)
    for _ in range(max(1, (tree_count - 1).bit_length())):
        product = jnp.einsum("...ij,...jk->...ik", reach, reach, preferred_element_type=F32)
        reach = jnp.minimum(reach + product, 1.0)
    return reach > 0.5


OVER_LAST = (((1,), (1,)), ((), ()))
SLICE = HEADS // 4
SPAN = SLICE * VDIM
LONG_AT, TREE_AT, QUERY_AT, BLOCK = 576, 1152, 1280, 1536
TOKENS = 16 * TREE + TREE
QUARTER = TOKENS // 4


def split3(value):
    high = value.astype(BF)
    rest = value - high.astype(F32)
    mid = rest.astype(BF)
    return high, mid, (rest - mid.astype(F32)).astype(BF)


def dot(left, right):
    return jnp.dot(left, right, preferred_element_type=F32)


def dot_t(left, right):
    return lax.dot_general(left, right, OVER_LAST, preferred_element_type=F32)


def place_shards(c, mine, twin, target, sems):
    copies = [
        pltpu.make_async_copy(mine, target.at[..., c, :, :], sems.at[0]),
        pltpu.make_async_copy(twin, target.at[..., 1 - c, :, :], sems.at[1]),
    ]
    for copy in copies:
        copy.start()
    return copies


def attend_kernel(place, got, query_l, tree_l, mine, twin, out, kv, lat, sems):
    copies = place_shards(place[0], mine, twin, kv, sems)
    lanes = lax.broadcasted_iota(jnp.int32, (TREE, 128), 1)
    slots = lax.broadcasted_iota(jnp.int32, (1, 256), 1).astype(F32)
    scale = (NOPE + ROPE) ** -0.5
    size = SLICE * TREE

    def rope_rows(chunk):
        zero = jnp.zeros((TREE, 128), BF)
        return jnp.concatenate([jnp.where(lanes // 32 == h % 4, chunk(5 + h // 4), zero) for h in range(SLICE)], axis=0)

    def cached(query, rope, block, at, length):
        keys = jnp.concatenate([block[at : at + 288], block[at + 288 : at + 576]], axis=1)
        scores = dot(query, keys[:KVR]) + dot(rope, jnp.concatenate([keys[KVR:]] * 4, axis=0))
        return jnp.where(slots < length, scores * scale, -jnp.inf), keys[:KVR]

    def treed(query, rope, block, at):
        keys = jnp.concatenate([block[at : at + TREE], block[at + TREE : at + 2 * TREE]], axis=1)
        scores = dot_t(query, keys) + dot_t(rope, block[at + 2 * TREE : at + 3 * TREE])
        reach = block[at + 3 * TREE : at + 4 * TREE, :TREE].astype(F32)
        reach = jnp.concatenate([reach] * SLICE, axis=0)
        return jnp.where(reach > 0.5, scores * scale, -jnp.inf), keys

    for copy in copies:
        copy.wait()
    for p in range(SLICE // 2):
        at = TREE * p
        rows = [got[k, QUERY_AT + at : QUERY_AT + at + TREE] for k in range(4)] + [query_l[at : at + TREE]]
        even = [jnp.where(lanes < NOPE, row, jnp.zeros_like(row)) for row in rows]
        odd = [jnp.where(lanes < NOPE, jnp.zeros_like(row), row) for row in rows]
        weight = kv[...][:, :, :, :KVR].reshape(SPAN, KVR)[128 * p : 128 * (p + 1)]
        part = dot(jnp.concatenate(even + odd, axis=0), weight).astype(BF)
        for s in range(2):
            for k in range(5):
                lat[k, TREE * (2 * p + s) : TREE * (2 * p + s + 1)] = part[TREE * (5 * s + k) : TREE * (5 * s + k + 1)]

    for k in range(4):
        block = got.at[k]
        query = lat[k]
        rope = rope_rows(lambda i: block[QUERY_AT + TREE * i : QUERY_AT + TREE * (i + 1)])
        length = block[TREE_AT + 3 * TREE : TREE_AT + 3 * TREE + 1, 32:33].astype(F32)
        first, keys = cached(query, rope, block, 0, length)
        second, tree = treed(query, rope, block, TREE_AT)
        top = jnp.maximum(jnp.max(first, axis=-1, keepdims=True), jnp.max(second, axis=-1, keepdims=True))
        first, second = jnp.exp(first - top), jnp.exp(second - top)
        total = jnp.sum(first, axis=-1, keepdims=True) + jnp.sum(second, axis=-1, keepdims=True)
        acc = dot_t(first.astype(BF), keys) + dot(second.astype(BF), tree)
        lat[k] = (acc / total).astype(BF)

    query = lat[4]
    rope = rope_rows(lambda i: query_l[TREE * i : TREE * (i + 1)])
    second, tree = treed(query, rope, tree_l, 0)
    scored = []
    for k in range(4):
        block = got.at[k]
        length = block[TREE_AT + 3 * TREE : TREE_AT + 3 * TREE + 1, 33:34].astype(F32)
        scored.append(cached(query, rope, block, LONG_AT, length))
    top = jnp.max(second, axis=-1, keepdims=True)
    for scores, _ in scored:
        top = jnp.maximum(top, jnp.max(scores, axis=-1, keepdims=True))
    second = jnp.exp(second - top)
    total = jnp.sum(second, axis=-1, keepdims=True)
    acc = dot(second.astype(BF), tree)
    for scores, keys in scored:
        weights = jnp.exp(scores - top)
        total += jnp.sum(weights, axis=-1, keepdims=True)
        acc += dot_t(weights.astype(BF), keys)
    lat[4] = (acc / total).astype(BF)
    column = top + jnp.log(total)
    logs = jnp.zeros((TREE, 128), F32)
    for h in range(SLICE):
        logs = jnp.where(lanes == h, column[TREE * h : TREE * (h + 1)], logs)

    for p in range(SLICE // 2):
        pair = []
        for h in (2 * p, 2 * p + 1):
            rows = jnp.concatenate([lat[k, TREE * h : TREE * (h + 1)] for k in range(5)], axis=0)
            weight = kv[...][:, :, :, KVR:].reshape(SPAN, KVR)[VDIM * h : VDIM * (h + 1)]
            pair.append(dot_t(rows, weight))
        heads = jnp.concatenate(pair, axis=1).astype(BF)
        for d in range(4):
            out[d, 5 * TREE * p : 5 * TREE * (p + 1)] = heads
    base = 5 * TREE * (SLICE // 2)
    for i, part in enumerate(split3(logs)):
        for d in range(4):
            out[d, base + TREE * i : base + TREE * (i + 1)] = part


def project_kernel(place, got, mine, twin, send, weight, rows, sems):
    copies = place_shards(place[0], mine, twin, weight, sems)
    base = 5 * TREE * (SLICE // 2)
    logs = sum(got[:, base + TREE * i : base + TREE * (i + 1)].astype(F32) for i in range(3))
    share = jnp.exp(logs - jnp.max(logs, axis=0)[None])
    share = (share / jnp.sum(share, axis=0)[None]).reshape(4 * TREE, 128)
    high = share.astype(BF)
    low = (share - high.astype(F32)).astype(BF)
    for p in range(SLICE // 2):
        at = 5 * TREE * p
        cols = slice(128 * p, 128 * (p + 1))
        for y in range(4):
            rows[4 * TREE * y : 4 * TREE * (y + 1), cols] = got[y, at : at + 4 * TREE]
        owner = lax.broadcasted_iota(jnp.int32, (128, 128), 1) // VDIM + 2 * p
        select = jnp.where(lax.broadcasted_iota(jnp.int32, (128, 128), 0) == owner, 1.0, 0.0).astype(BF)
        wide = (dot(high, select) + dot(low, select)).reshape(4, TREE, 128)
        piece = got[:, at + 4 * TREE : at + 5 * TREE].astype(F32) * wide
        rows[16 * TREE : 17 * TREE, cols] = jnp.sum(piece, axis=0).astype(BF)
    for copy in copies:
        copy.wait()
    full = [weight[x].reshape(SPAN, 160) for x in range(4)]
    for x in range(4):
        send[x, :TOKENS] = dot(rows[...], full[x][:, :128]).astype(BF)
    rest = dot(rows[...], jnp.concatenate([part[:, 128:] for part in full], axis=1))
    lanes = lax.broadcasted_iota(jnp.int32, (QUARTER, 128), 1) // 32
    for x in range(4):
        packed = jnp.zeros((QUARTER, 128), F32)
        for g in range(4):
            part = rest[QUARTER * g : QUARTER * (g + 1)]
            shift = (32 * (g - x)) % 128
            part = pltpu.roll(part, shift, 1) if shift else part
            packed = jnp.where(lanes == g, part, packed)
        send[x, TOKENS : TOKENS + QUARTER] = packed.astype(BF)
        send[x, TOKENS + QUARTER :] = jnp.zeros((send.shape[1] - TOKENS - QUARTER, 128), BF)


def finish_kernel(got, residual, long_residual, hidden, long_hidden, tail):
    rest = jnp.sum(got[:, TOKENS : TOKENS + QUARTER].astype(F32), axis=0)
    for g in range(4):
        tail[QUARTER * g : QUARTER * (g + 1)] = pltpu.roll(rest, (-32 * g) % 128, 1) if g else rest
    for i in range(17):
        at = slice(TREE * i, TREE * (i + 1))
        main = jnp.sum(got[:, at].astype(F32), axis=0)
        source, target, k = (residual, hidden, i) if i < 16 else (long_residual, long_hidden, 0)
        target[k, :, :128] = (source[k, :, :128].astype(F32) + main).astype(BF)
        target[k, :, 128:160] = (source[k, :, 128:160].astype(F32) + tail[at, :32]).astype(BF)


SMEM = pl.BlockSpec(memory_space=pltpu.SMEM)
VMEM = pl.BlockSpec(memory_space=pltpu.VMEM)
ANY = pl.BlockSpec(memory_space=pl.ANY)
PARAMS = pltpu.CompilerParams(vmem_limit_bytes=48 << 20)


def slice_queries(queries):
    heads = queries.reshape(TREE, 4, SLICE, NOPE + ROPE)
    nope = heads[..., :NOPE].reshape(TREE, 4, SLICE // 2, 128).transpose(1, 2, 0, 3)
    rope = heads[..., NOPE:].reshape(TREE, 4, SLICE * ROPE)
    rope = jnp.pad(rope, ((0, 0), (0, 0), (0, 64))).reshape(TREE, 4, 3, 128).transpose(1, 2, 0, 3)
    return jnp.concatenate([nope, rope], axis=1).reshape(4, 8 * TREE, 128)


def tree_block(rows, reach, lengths):
    extra = jnp.concatenate([reach.astype(BF), jnp.broadcast_to(lengths.astype(BF)[None], (TREE, 2))], axis=1)
    extra = jnp.pad(extra, ((0, 0), (0, 128 - extra.shape[1])))
    rope = jnp.concatenate([rows[:, KVR:]] * 4, axis=1)
    return jnp.concatenate([rows[:, :128], rows[:, 128:KVR], rope, extra], axis=0)


def on_device(
    queries, tree_latent, parents, cache, cache_lengths, accepted, residual,
    long_queries, long_tree_latent, long_parents, long_cache, long_plan, long_residual,
    key_up, value_up, out_weight,
):
    nx = 4
    y, x, c = lax.axis_index("y"), lax.axis_index("x"), lax.axis_index("c")
    place = c.reshape(1).astype(jnp.int32)
    kv = jnp.concatenate([key_up, value_up], axis=1)
    pairs = [(r * 16 + z, ((z % 4) * 4 + z // 4) * 16 + (z + r) % 16) for r in range(16) for z in range(16)]
    kv = lax.ppermute(kv, ("y", "x", "a", "b"), pairs)
    swapped = lax.ppermute(out_weight, ("x", "a"), [(4 * i + k, 4 * k + i) for i in range(4) for k in range(4)])
    out_rows = lax.all_gather(swapped, "b")
    kv, out_rows = lax.optimization_barrier((kv, out_rows))
    kv = lax.all_gather(kv, "y")
    kv_twin = lax.ppermute(kv, "c", SWAP)
    out_rows = lax.all_gather(out_rows, "a")
    out_twin = lax.ppermute(out_rows, "c", SWAP)

    reach = tree_reach(jnp.concatenate([parents[0], long_parents], axis=0))
    lengths = jnp.concatenate([cache_lengths[0], long_plan[0]])
    short_t, long_t = cache[0, 0].T, long_cache[0].T
    keys = jnp.concatenate([short_t[:, :128], short_t[:, 128:], long_t[:, :128], long_t[:, 128:]], axis=0)
    keys = jnp.concatenate([keys, tree_block(tree_latent[0], reach[0], lengths)], axis=0)
    block = jnp.concatenate(
        [jnp.broadcast_to(keys[None], (nx,) + keys.shape), slice_queries(queries[0])], axis=1
    )
    block, _ = lax.optimization_barrier((block, swapped))
    got = lax.all_to_all(block, "x", 0, 0)
    query_l = lax.dynamic_index_in_dim(slice_queries(long_queries[0]), x, 0, keepdims=False)
    tree_l = tree_block(long_tree_latent[0], reach[1] & (y == 0), lengths)
    shard = key_up.shape[0]

    heads = pl.pallas_call(
        attend_kernel,
        out_shape=jax.ShapeDtypeStruct((4, 5 * TREE * (SLICE // 2) + 3 * TREE, 128), BF),
        in_specs=[SMEM, VMEM, VMEM, VMEM, ANY, ANY],
        out_specs=VMEM,
        scratch_shapes=[
            pltpu.VMEM((4, 2, shard, 2 * KVR), BF),
            pltpu.VMEM((5, SLICE * TREE, KVR), BF),
            pltpu.SemaphoreType.DMA((2,)),
        ],
        compiler_params=PARAMS,
    )(place, got, query_l, tree_l, kv, kv_twin)
    shared = lax.all_to_all(heads, "y", 0, 0)
    send = pl.pallas_call(
        project_kernel,
        out_shape=jax.ShapeDtypeStruct((4, 688, 128), BF),
        in_specs=[SMEM, VMEM, ANY, ANY],
        out_specs=VMEM,
        scratch_shapes=[
            pltpu.VMEM((4, 4, 2, shard, 160), BF),
            pltpu.VMEM((TOKENS, SPAN), BF),
            pltpu.SemaphoreType.DMA((2,)),
        ],
        compiler_params=PARAMS,
    )(place, shared, out_rows, out_twin)
    back = lax.all_to_all(send, "x", 0, 0)
    hidden, long_hidden = pl.pallas_call(
        finish_kernel,
        out_shape=(
            jax.ShapeDtypeStruct(residual.shape, BF),
            jax.ShapeDtypeStruct(long_residual.shape, BF),
        ),
        in_specs=[VMEM, VMEM, VMEM],
        out_specs=(VMEM, VMEM),
        scratch_shapes=[pltpu.VMEM((TOKENS, 128), F32)],
        compiler_params=PARAMS,
    )(back, residual, long_residual)
    accepted_cache = jnp.take_along_axis(tree_latent[0], accepted[0, 0][:, None], axis=0)[None, None]
    return hidden, accepted_cache, long_hidden


def solution(mesh):
    split = Mesh(mesh.devices.reshape(4, 4, 4, 4, 2), ("y", "x", "a", "b", "c"))
    return jax.shard_map(
        on_device,
        mesh=split,
        in_specs=(
            P(ROWS, COLS, None),
            P(ROWS, COLS, None),
            P(ROWS, COLS, None),
            P(ROWS, COLS, None, None),
            P(ROWS, COLS),
            P(ROWS, COLS, None),
            P(None, COLS, ROWS),
            P(COLS, None, None),
            P(COLS, None, None),
            P(COLS, None),
            P(COLS, ROWS, None),
            P(COLS, ROWS),
            P(COLS, None, ROWS),
            P(COLS, None),
            P(COLS, None),
            P(COLS, ROWS),
        ),
        out_specs=(P(None, COLS, ROWS), P(ROWS, COLS, None, None), P(COLS, None, ROWS)),
        check_vma=False,
    )
```

```python
import jax
import jax.numpy as jnp
from jax import lax
from jax.experimental import pallas as pl
from jax.experimental.pallas import tpu as pltpu
from jax.sharding import Mesh, PartitionSpec as P

HEADS = 40
NOPE = 64
ROPE = 32
VDIM = 64
KVR = 256
TREE = 32
ROWS = ("y", "x")
COLS = ("a", "b", "c")
SWAP = [(0, 1), (1, 0)]
BF = jnp.bfloat16
F32 = jnp.float32


def tree_reach(parent_ids):
    tree_count = parent_ids.shape[-1]
    positions = jnp.arange(tree_count, dtype=jnp.int32)
    reach = (parent_ids[..., :, None] == positions).astype(F32)
    reach = reach + (positions[:, None] == positions[None, :]).astype(F32)
    for _ in range(max(1, (tree_count - 1).bit_length())):
        product = jnp.einsum("...ij,...jk->...ik", reach, reach, preferred_element_type=F32)
        reach = jnp.minimum(reach + product, 1.0)
    return reach > 0.5


OVER_LAST = (((1,), (1,)), ((), ()))
SLICE = HEADS // 4
SPAN = SLICE * VDIM
LONG_AT, TREE_AT, QUERY_AT, BLOCK = 576, 1152, 1280, 1536
TOKENS = 16 * TREE + TREE
QUARTER = TOKENS // 4


def split3(value):
    high = value.astype(BF)
    rest = value - high.astype(F32)
    mid = rest.astype(BF)
    return high, mid, (rest - mid.astype(F32)).astype(BF)


def dot(left, right):
    return jnp.dot(left, right, preferred_element_type=F32)


def dot_t(left, right):
    return lax.dot_general(left, right, OVER_LAST, preferred_element_type=F32)


def place_shards(c, mine, twin, target, sems):
    copies = [
        pltpu.make_async_copy(mine, target.at[..., c, :, :], sems.at[0]),
        pltpu.make_async_copy(twin, target.at[..., 1 - c, :, :], sems.at[1]),
    ]
    for copy in copies:
        copy.start()
    return copies


def attend_kernel(place, got, query_l, tree_l, mine, twin, out, kv, lat, sems):
    copies = place_shards(place[0], mine, twin, kv, sems)
    lanes = lax.broadcasted_iota(jnp.int32, (TREE, 128), 1)
    slots = lax.broadcasted_iota(jnp.int32, (1, 256), 1).astype(F32)
    scale = (NOPE + ROPE) ** -0.5
    size = SLICE * TREE

    def rope_rows(chunk):
        zero = jnp.zeros((TREE, 128), BF)
        return jnp.concatenate([jnp.where(lanes // 32 == h % 4, chunk(5 + h // 4), zero) for h in range(SLICE)], axis=0)

    def cached(query, rope, block, at, length):
        keys = jnp.concatenate([block[at : at + 288], block[at + 288 : at + 576]], axis=1)
        scores = dot(query, keys[:KVR]) + dot(rope, jnp.concatenate([keys[KVR:]] * 4, axis=0))
        return jnp.where(slots < length, scores * scale, -jnp.inf), keys[:KVR]

    def treed(query, rope, block, at):
        keys = jnp.concatenate([block[at : at + TREE], block[at + TREE : at + 2 * TREE]], axis=1)
        scores = dot_t(query, keys) + dot_t(rope, block[at + 2 * TREE : at + 3 * TREE])
        reach = block[at + 3 * TREE : at + 4 * TREE, :TREE].astype(F32)
        reach = jnp.concatenate([reach] * SLICE, axis=0)
        return jnp.where(reach > 0.5, scores * scale, -jnp.inf), keys

    for copy in copies:
        copy.wait()
    for p in range(SLICE // 2):
        at = TREE * p
        rows = [got[k, QUERY_AT + at : QUERY_AT + at + TREE] for k in range(4)] + [query_l[at : at + TREE]]
        even = [jnp.where(lanes < NOPE, row, jnp.zeros_like(row)) for row in rows]
        odd = [jnp.where(lanes < NOPE, jnp.zeros_like(row), row) for row in rows]
        weight = kv[...][:, :, :, :KVR].reshape(SPAN, KVR)[128 * p : 128 * (p + 1)]
        part = dot(jnp.concatenate(even + odd, axis=0), weight).astype(BF)
        for s in range(2):
            for k in range(5):
                lat[k, TREE * (2 * p + s) : TREE * (2 * p + s + 1)] = part[TREE * (5 * s + k) : TREE * (5 * s + k + 1)]

    for k in range(4):
        block = got.at[k]
        query = lat[k]
        rope = rope_rows(lambda i: block[QUERY_AT + TREE * i : QUERY_AT + TREE * (i + 1)])
        length = block[TREE_AT + 3 * TREE : TREE_AT + 3 * TREE + 1, 32:33].astype(F32)
        first, keys = cached(query, rope, block, 0, length)
        second, tree = treed(query, rope, block, TREE_AT)
        top = jnp.maximum(jnp.max(first, axis=-1, keepdims=True), jnp.max(second, axis=-1, keepdims=True))
        first, second = jnp.exp(first - top), jnp.exp(second - top)
        total = jnp.sum(first, axis=-1, keepdims=True) + jnp.sum(second, axis=-1, keepdims=True)
        acc = dot_t(first.astype(BF), keys) + dot(second.astype(BF), tree)
        lat[k] = (acc / total).astype(BF)

    query = lat[4]
    rope = rope_rows(lambda i: query_l[TREE * i : TREE * (i + 1)])
    second, tree = treed(query, rope, tree_l, 0)
    scored = []
    for k in range(4):
        block = got.at[k]
        length = block[TREE_AT + 3 * TREE : TREE_AT + 3 * TREE + 1, 33:34].astype(F32)
        scored.append(cached(query, rope, block, LONG_AT, length))
    top = jnp.max(second, axis=-1, keepdims=True)
    for scores, _ in scored:
        top = jnp.maximum(top, jnp.max(scores, axis=-1, keepdims=True))
    second = jnp.exp(second - top)
    total = jnp.sum(second, axis=-1, keepdims=True)
    acc = dot(second.astype(BF), tree)
    for scores, keys in scored:
        weights = jnp.exp(scores - top)
        total += jnp.sum(weights, axis=-1, keepdims=True)
        acc += dot_t(weights.astype(BF), keys)
    lat[4] = (acc / total).astype(BF)
    column = top + jnp.log(total)
    logs = jnp.zeros((TREE, 128), F32)
    for h in range(SLICE):
        logs = jnp.where(lanes == h, column[TREE * h : TREE * (h + 1)], logs)

    for p in range(SLICE // 2):
        pair = []
        for h in (2 * p, 2 * p + 1):
            rows = jnp.concatenate([lat[k, TREE * h : TREE * (h + 1)] for k in range(5)], axis=0)
            weight = kv[...][:, :, :, KVR:].reshape(SPAN, KVR)[VDIM * h : VDIM * (h + 1)]
            pair.append(dot_t(rows, weight))
        heads = jnp.concatenate(pair, axis=1).astype(BF)
        for d in range(4):
            out[d, 5 * TREE * p : 5 * TREE * (p + 1)] = heads
    base = 5 * TREE * (SLICE // 2)
    for i, part in enumerate(split3(logs)):
        for d in range(4):
            out[d, base + TREE * i : base + TREE * (i + 1)] = part


def project_kernel(place, got, mine, twin, send, weight, rows, sems):
    c, a = place[0], place[2]
    copies = []
    for k in range(5):
        copies.append(pltpu.make_async_copy(mine.at[:, k], weight.at[k, :, c], sems.at[k]))
        copies.append(pltpu.make_async_copy(twin.at[:, k], weight.at[k, :, 1 - c], sems.at[5 + k]))
    for copy in copies:
        copy.start()
    base = 5 * TREE * (SLICE // 2)
    logs = sum(got[:, base + TREE * i : base + TREE * (i + 1)].astype(F32) for i in range(3))
    share = jnp.exp(logs - jnp.max(logs, axis=0)[None])
    share = (share / jnp.sum(share, axis=0)[None]).reshape(4 * TREE, 128)
    high = share.astype(BF)
    low = (share - high.astype(F32)).astype(BF)
    for p in range(SLICE // 2):
        at = 5 * TREE * p
        cols = slice(128 * p, 128 * (p + 1))
        for y in range(4):
            rows[4 * TREE * y : 4 * TREE * (y + 1), cols] = got[y, at : at + 4 * TREE]
        owner = lax.broadcasted_iota(jnp.int32, (128, 128), 1) // VDIM + 2 * p
        select = jnp.where(lax.broadcasted_iota(jnp.int32, (128, 128), 0) == owner, 1.0, 0.0).astype(BF)
        wide = (dot(high, select) + dot(low, select)).reshape(4, TREE, 128)
        piece = got[:, at + 4 * TREE : at + 5 * TREE].astype(F32) * wide
        rows[16 * TREE : 17 * TREE, cols] = jnp.sum(piece, axis=0).astype(BF)
    for copy in copies:
        copy.wait()
    rest = dot(rows[...], weight[4].reshape(SPAN, 128))
    lanes = lax.broadcasted_iota(jnp.int32, (QUARTER, 128), 1) // 32
    for k in range(4):
        x = lax.rem(a + 4 - k, 4)
        send[x, :TOKENS] = dot(rows[...], weight[k].reshape(SPAN, 128)).astype(BF)
        packed = jnp.zeros((QUARTER, 128), F32)
        for g in range(4):
            part = rest[QUARTER * g : QUARTER * (g + 1)]
            shift = (32 * (g - k)) % 128
            part = pltpu.roll(part, shift, 1) if shift else part
            packed = jnp.where(lanes == g, part, packed)
        send[x, TOKENS : TOKENS + QUARTER] = packed.astype(BF)
        send[x, TOKENS + QUARTER :] = jnp.zeros((send.shape[1] - TOKENS - QUARTER, 128), BF)


def finish_kernel(got, residual, long_residual, hidden, long_hidden, tail):
    rest = jnp.sum(got[:, TOKENS : TOKENS + QUARTER].astype(F32), axis=0)
    for g in range(4):
        tail[QUARTER * g : QUARTER * (g + 1)] = pltpu.roll(rest, (-32 * g) % 128, 1) if g else rest
    for i in range(17):
        at = slice(TREE * i, TREE * (i + 1))
        main = jnp.sum(got[:, at].astype(F32), axis=0)
        source, target, k = (residual, hidden, i) if i < 16 else (long_residual, long_hidden, 0)
        target[k, :, :128] = (source[k, :, :128].astype(F32) + main).astype(BF)
        target[k, :, 128:160] = (source[k, :, 128:160].astype(F32) + tail[at, :32]).astype(BF)


SMEM = pl.BlockSpec(memory_space=pltpu.SMEM)
VMEM = pl.BlockSpec(memory_space=pltpu.VMEM)
ANY = pl.BlockSpec(memory_space=pl.ANY)
PARAMS = pltpu.CompilerParams(vmem_limit_bytes=48 << 20)


def onehot(rows, cols, match):
    row = lax.broadcasted_iota(jnp.int32, (rows, cols), 0)
    col = lax.broadcasted_iota(jnp.int32, (rows, cols), 1)
    return jnp.where(match(row, col), 1.0, 0.0).astype(BF)


def pack_kernel(place, lengths, queries, queries_l, keys, keys_l, tree, tree_l, reach, block, own_q, own_tree, slices):
    for d in range(4):
        block[d, 0:288] = keys[:, :128]
        block[d, 288:576] = keys[:, 128:]
        block[d, 576:864] = keys_l[:, :128]
        block[d, 864:1152] = keys_l[:, 128:]
    lanes = lax.broadcasted_iota(jnp.int32, (TREE, 128), 1)
    tile4 = onehot(TREE, 128, lambda row, col: col % 32 == row)
    widen = onehot(TREE, 128, lambda row, col: col == row)
    for i, rows in enumerate((tree, tree_l)):
        extra = dot(reach[i], widen)
        extra = jnp.where(lanes == 32, lengths[0].astype(F32), extra)
        extra = jnp.where(lanes == 33, lengths[1].astype(F32), extra).astype(BF)
        parts = (rows[:, :128], rows[:, 128:KVR], dot(rows[:, KVR:], tile4).astype(BF), extra)
        for k, part in enumerate(parts):
            at = slice(TREE * k, TREE * (k + 1))
            if i == 0:
                for d in range(4):
                    block[d, TREE_AT + at.start : TREE_AT + at.stop] = part
            else:
                own_tree[at] = part

    def source(col):
        nope = 96 * (col // NOPE) + col % NOPE
        rope = 96 * ((col - 256) // ROPE) + NOPE + (col - 256) % ROPE
        return jnp.where(col < 256, nope, rope)

    sort = onehot(384, 384, lambda row, col: source(col) == row)
    rope = []
    for w in range(HEADS // 4):
        cols = slice(384 * w, 384 * (w + 1))
        moved = dot(jnp.concatenate([queries[:, cols], queries_l[:, cols]], axis=0), sort)
        rope.append(moved[:, 256:])
        for half in range(2):
            s, p = divmod(2 * w + half, SLICE // 2)
            part = moved[:, 128 * half : 128 * (half + 1)].astype(BF)
            block[s, QUERY_AT + TREE * p : QUERY_AT + TREE * (p + 1)] = part[:TREE]
            slices[s, TREE * p : TREE * (p + 1)] = part[TREE:]
    wide = lax.broadcasted_iota(jnp.int32, (2 * TREE, 128), 1)
    for s in range(4):
        first = SLICE * s // 4
        for k in range(3):
            if s % 2 == 0:
                part = rope[first + k]
            else:
                after = pltpu.roll(rope[first + k + 1], 64, 1) if k < 2 else jnp.zeros((2 * TREE, 128), F32)
                part = jnp.where(wide < 64, pltpu.roll(rope[first + k], 64, 1), after)
            part = part.astype(BF)
            at = TREE * (5 + k)
            block[s, QUERY_AT + at : QUERY_AT + at + TREE] = part[:TREE]
            slices[s, at : at + TREE] = part[TREE:]
    own_q[...] = slices[place[1]]


def on_device(
    queries, tree_latent, parents, cache, cache_lengths, accepted, residual,
    long_queries, long_tree_latent, long_parents, long_cache, long_plan, long_residual,
    key_up, value_up, out_weight,
):
    y, x, a, c = lax.axis_index("y"), lax.axis_index("x"), lax.axis_index("a"), lax.axis_index("c")
    place = jnp.stack([c, x, a]).astype(jnp.int32)
    shard = key_up.shape[0]
    kv = jnp.concatenate([key_up, value_up], axis=1)
    pairs = [(r * 16 + z, ((z % 4) * 4 + z // 4) * 16 + (z + r) % 16) for r in range(16) for z in range(16)]
    kv = lax.ppermute(kv, ("y", "x", "a", "b"), pairs)
    moved = [
        lax.ppermute(out_weight, ("x", "a"), [(4 * i + j, 4 * j + (i + k) % 4) for i in range(4) for j in range(4)])
        for k in range(4)
    ]
    reach = tree_reach(jnp.concatenate([parents[0], long_parents], axis=0))
    reach = (reach & ((jnp.arange(2) == 0) | (y == 0))[:, None, None]).astype(BF)
    lengths = jnp.concatenate([cache_lengths[0], long_plan[0]])
    rows = 8 * TREE
    block, query_l, tree_l = pl.pallas_call(
        pack_kernel,
        out_shape=(
            jax.ShapeDtypeStruct((4, BLOCK, 128), BF),
            jax.ShapeDtypeStruct((rows, 128), BF),
            jax.ShapeDtypeStruct((4 * TREE, 128), BF),
        ),
        in_specs=[SMEM, SMEM] + [VMEM] * 7,
        out_specs=(VMEM, VMEM, VMEM),
        scratch_shapes=[pltpu.VMEM((4, rows, 128), BF)],
        compiler_params=PARAMS,
    )(
        place, lengths, queries[0], long_queries[0], cache[0, 0].T, long_cache[0].T,
        tree_latent[0], long_tree_latent[0], reach,
    )
    block, kv, *moved = lax.optimization_barrier((block, kv, *moved))
    got = lax.all_to_all(block, "x", 0, 0)
    kv = lax.all_gather(kv, "y")
    kv_twin = lax.ppermute(kv, "c", SWAP)
    tails = jnp.concatenate([part[:, 128:] for part in moved], axis=1)
    out_rows = lax.all_gather(jnp.stack([part[:, :128] for part in moved] + [tails]), "b")
    out_twin = lax.ppermute(out_rows, "c", SWAP)

    heads = pl.pallas_call(
        attend_kernel,
        out_shape=jax.ShapeDtypeStruct((4, 5 * TREE * (SLICE // 2) + 3 * TREE, 128), BF),
        in_specs=[SMEM, VMEM, VMEM, VMEM, ANY, ANY],
        out_specs=VMEM,
        scratch_shapes=[
            pltpu.VMEM((4, 2, shard, 2 * KVR), BF),
            pltpu.VMEM((5, SLICE * TREE, KVR), BF),
            pltpu.SemaphoreType.DMA((2,)),
        ],
        compiler_params=PARAMS,
    )(place, got, query_l, tree_l, kv, kv_twin)
    shared = lax.all_to_all(heads, "y", 0, 0)
    send = pl.pallas_call(
        project_kernel,
        out_shape=jax.ShapeDtypeStruct((4, 688, 128), BF),
        in_specs=[SMEM, VMEM, ANY, ANY],
        out_specs=VMEM,
        scratch_shapes=[
            pltpu.VMEM((5, 4, 2, shard, 128), BF),
            pltpu.VMEM((TOKENS, SPAN), BF),
            pltpu.SemaphoreType.DMA((10,)),
        ],
        compiler_params=PARAMS,
    )(place, shared, out_rows, out_twin)
    back = lax.all_to_all(send, "x", 0, 0)
    hidden, long_hidden = pl.pallas_call(
        finish_kernel,
        out_shape=(
            jax.ShapeDtypeStruct(residual.shape, BF),
            jax.ShapeDtypeStruct(long_residual.shape, BF),
        ),
        in_specs=[VMEM, VMEM, VMEM],
        out_specs=(VMEM, VMEM),
        scratch_shapes=[pltpu.VMEM((TOKENS, 128), F32)],
        compiler_params=PARAMS,
    )(back, residual, long_residual)
    accepted_cache = jnp.take_along_axis(tree_latent[0], accepted[0, 0][:, None], axis=0)[None, None]
    return hidden, accepted_cache, long_hidden


def solution(mesh):
    split = Mesh(mesh.devices.reshape(4, 4, 4, 4, 2), ("y", "x", "a", "b", "c"))
    return jax.shard_map(
        on_device,
        mesh=split,
        in_specs=(
            P(ROWS, COLS, None),
            P(ROWS, COLS, None),
            P(ROWS, COLS, None),
            P(ROWS, COLS, None, None),
            P(ROWS, COLS),
            P(ROWS, COLS, None),
            P(None, COLS, ROWS),
            P(COLS, None, None),
            P(COLS, None, None),
            P(COLS, None),
            P(COLS, ROWS, None),
            P(COLS, ROWS),
            P(COLS, None, ROWS),
            P(COLS, None),
            P(COLS, None),
            P(COLS, ROWS),
        ),
        out_specs=(P(None, COLS, ROWS), P(ROWS, COLS, None, None), P(COLS, None, ROWS)),
        check_vma=False,
    )
```

```python
import jax
import jax.numpy as jnp
from jax import lax
from jax.experimental import pallas as pl
from jax.experimental.pallas import tpu as pltpu
from jax.sharding import Mesh, PartitionSpec as P

HEADS = 40
NOPE = 64
ROPE = 32
VDIM = 64
KVR = 256
TREE = 32
ROWS = ("y", "x")
COLS = ("a", "b", "c")
BF = jnp.bfloat16
F32 = jnp.float32


OVER_LAST = (((1,), (1,)), ((), ()))
SLICE = HEADS // 4
SPAN = SLICE * VDIM
LONG_AT, TREE_AT, QUERY_AT, BLOCK = 576, 1152, 1280, 1536
TOKENS = 16 * TREE + TREE
QUARTER = TOKENS // 4


def split3(value):
    high = value.astype(BF)
    rest = value - high.astype(F32)
    mid = rest.astype(BF)
    return high, mid, (rest - mid.astype(F32)).astype(BF)


def dot(left, right):
    return jnp.dot(left, right, preferred_element_type=F32)


def dot_t(left, right):
    return lax.dot_general(left, right, OVER_LAST, preferred_element_type=F32)


def attend_kernel(got, query_l, tree_l, kv, out, lat):
    lanes = lax.broadcasted_iota(jnp.int32, (TREE, 128), 1)
    slots = lax.broadcasted_iota(jnp.int32, (1, 256), 1).astype(F32)
    scale = (NOPE + ROPE) ** -0.5
    size = SLICE * TREE

    def rope_rows(chunk):
        zero = jnp.zeros((TREE, 128), BF)
        return jnp.concatenate([jnp.where(lanes // 32 == h % 4, chunk(5 + h // 4), zero) for h in range(SLICE)], axis=0)

    def cached(query, rope, block, at, length):
        keys = jnp.concatenate([block[at : at + 288], block[at + 288 : at + 576]], axis=1)
        scores = dot(query, keys[:KVR]) + dot(rope, jnp.concatenate([keys[KVR:]] * 4, axis=0))
        return jnp.where(slots < length, scores * scale, -jnp.inf), keys[:KVR]

    def treed(query, rope, block, at):
        keys = jnp.concatenate([block[at : at + TREE], block[at + TREE : at + 2 * TREE]], axis=1)
        scores = dot_t(query, keys) + dot_t(rope, block[at + 2 * TREE : at + 3 * TREE])
        reach = block[at + 3 * TREE : at + 4 * TREE, :TREE].astype(F32)
        reach = jnp.concatenate([reach] * SLICE, axis=0)
        return jnp.where(reach > 0.5, scores * scale, -jnp.inf), keys

    for p in range(SLICE // 2):
        at = TREE * p
        rows = [got[k, QUERY_AT + at : QUERY_AT + at + TREE] for k in range(4)] + [query_l[at : at + TREE]]
        even = [jnp.where(lanes < NOPE, row, jnp.zeros_like(row)) for row in rows]
        odd = [jnp.where(lanes < NOPE, jnp.zeros_like(row), row) for row in rows]
        weight = kv[...][:, :, :, :KVR].reshape(SPAN, KVR)[128 * p : 128 * (p + 1)]
        part = dot(jnp.concatenate(even + odd, axis=0), weight).astype(BF)
        for s in range(2):
            for k in range(5):
                lat[k, TREE * (2 * p + s) : TREE * (2 * p + s + 1)] = part[TREE * (5 * s + k) : TREE * (5 * s + k + 1)]

    for k in range(4):
        block = got.at[k]
        query = lat[k]
        rope = rope_rows(lambda i: block[QUERY_AT + TREE * i : QUERY_AT + TREE * (i + 1)])
        length = block[TREE_AT + 3 * TREE : TREE_AT + 3 * TREE + 1, 32:33].astype(F32)
        first, keys = cached(query, rope, block, 0, length)
        second, tree = treed(query, rope, block, TREE_AT)
        top = jnp.maximum(jnp.max(first, axis=-1, keepdims=True), jnp.max(second, axis=-1, keepdims=True))
        first, second = jnp.exp(first - top), jnp.exp(second - top)
        total = jnp.sum(first, axis=-1, keepdims=True) + jnp.sum(second, axis=-1, keepdims=True)
        acc = dot_t(first.astype(BF), keys) + dot(second.astype(BF), tree)
        lat[k] = (acc / total).astype(BF)

    query = lat[4]
    rope = rope_rows(lambda i: query_l[TREE * i : TREE * (i + 1)])
    second, tree = treed(query, rope, tree_l, 0)
    scored = []
    for k in range(4):
        block = got.at[k]
        length = block[TREE_AT + 3 * TREE : TREE_AT + 3 * TREE + 1, 33:34].astype(F32)
        scored.append(cached(query, rope, block, LONG_AT, length))
    top = jnp.max(second, axis=-1, keepdims=True)
    for scores, _ in scored:
        top = jnp.maximum(top, jnp.max(scores, axis=-1, keepdims=True))
    second = jnp.exp(second - top)
    total = jnp.sum(second, axis=-1, keepdims=True)
    acc = dot(second.astype(BF), tree)
    for scores, keys in scored:
        weights = jnp.exp(scores - top)
        total += jnp.sum(weights, axis=-1, keepdims=True)
        acc += dot_t(weights.astype(BF), keys)
    lat[4] = (acc / total).astype(BF)
    column = top + jnp.log(total)
    logs = jnp.zeros((TREE, 128), F32)
    for h in range(SLICE):
        logs = jnp.where(lanes == h, column[TREE * h : TREE * (h + 1)], logs)

    for p in range(SLICE // 2):
        pair = []
        for h in (2 * p, 2 * p + 1):
            rows = jnp.concatenate([lat[k, TREE * h : TREE * (h + 1)] for k in range(5)], axis=0)
            weight = kv[...][:, :, :, KVR:].reshape(SPAN, KVR)[VDIM * h : VDIM * (h + 1)]
            pair.append(dot_t(rows, weight))
        heads = jnp.concatenate(pair, axis=1).astype(BF)
        for d in range(4):
            out[d, 5 * TREE * p : 5 * TREE * (p + 1)] = heads
    base = 5 * TREE * (SLICE // 2)
    for i, part in enumerate(split3(logs)):
        for d in range(4):
            out[d, base + TREE * i : base + TREE * (i + 1)] = part


def project_kernel(place, got, weight, send, rows):
    a = place[1]
    base = 5 * TREE * (SLICE // 2)
    logs = sum(got[:, base + TREE * i : base + TREE * (i + 1)].astype(F32) for i in range(3))
    share = jnp.exp(logs - jnp.max(logs, axis=0)[None])
    share = (share / jnp.sum(share, axis=0)[None]).reshape(4 * TREE, 128)
    high = share.astype(BF)
    low = (share - high.astype(F32)).astype(BF)
    for p in range(SLICE // 2):
        at = 5 * TREE * p
        cols = slice(128 * p, 128 * (p + 1))
        for y in range(4):
            rows[4 * TREE * y : 4 * TREE * (y + 1), cols] = got[y, at : at + 4 * TREE]
        owner = lax.broadcasted_iota(jnp.int32, (128, 128), 1) // VDIM + 2 * p
        select = jnp.where(lax.broadcasted_iota(jnp.int32, (128, 128), 0) == owner, 1.0, 0.0).astype(BF)
        wide = (dot(high, select) + dot(low, select)).reshape(4, TREE, 128)
        piece = got[:, at + 4 * TREE : at + 5 * TREE].astype(F32) * wide
        rows[16 * TREE : 17 * TREE, cols] = jnp.sum(piece, axis=0).astype(BF)
    rest = dot(rows[...], weight[:, :, 4].reshape(SPAN, 128))
    lanes = lax.broadcasted_iota(jnp.int32, (QUARTER, 128), 1) // 32
    for k in range(4):
        x = lax.rem(a + k, 4)
        send[x, :TOKENS] = dot(rows[...], weight[:, :, k].reshape(SPAN, 128)).astype(BF)
        packed = jnp.zeros((QUARTER, 128), F32)
        for g in range(4):
            part = rest[QUARTER * g : QUARTER * (g + 1)]
            shift = (32 * (g - k)) % 128
            part = pltpu.roll(part, shift, 1) if shift else part
            packed = jnp.where(lanes == g, part, packed)
        send[x, TOKENS : TOKENS + QUARTER] = packed.astype(BF)
        send[x, TOKENS + QUARTER :] = jnp.zeros((send.shape[1] - TOKENS - QUARTER, 128), BF)


def finish_kernel(got, residual, long_residual, hidden, long_hidden, tail):
    rest = jnp.sum(got[:, TOKENS : TOKENS + QUARTER].astype(F32), axis=0)
    for g in range(4):
        tail[QUARTER * g : QUARTER * (g + 1)] = pltpu.roll(rest, (-32 * g) % 128, 1) if g else rest
    for i in range(17):
        at = slice(TREE * i, TREE * (i + 1))
        main = jnp.sum(got[:, at].astype(F32), axis=0)
        source, target, k = (residual, hidden, i) if i < 16 else (long_residual, long_hidden, 0)
        target[k, :, :128] = (source[k, :, :128].astype(F32) + main).astype(BF)
        target[k, :, 128:160] = (source[k, :, 128:160].astype(F32) + tail[at, :32]).astype(BF)


SMEM = pl.BlockSpec(memory_space=pltpu.SMEM)
VMEM = pl.BlockSpec(memory_space=pltpu.VMEM)
HBM = pl.BlockSpec(memory_space=pltpu.HBM)
PARAMS = pltpu.CompilerParams(vmem_limit_bytes=48 << 20)


def onehot(rows, cols, match):
    row = lax.broadcasted_iota(jnp.int32, (rows, cols), 0)
    col = lax.broadcasted_iota(jnp.int32, (rows, cols), 1)
    return jnp.where(match(row, col), 1.0, 0.0).astype(BF)


def pack_kernel(place, length, length_l, parents, parents_l, *refs):
    sources, (block, own_q, own_tree), held, (slices, sems) = refs[:6], refs[6:9], refs[9:15], refs[15:]
    copies = [pltpu.make_async_copy(sources[i], held[i], sems.at[i]) for i in range(6)]
    for copy in copies:
        copy.start()
    queries, queries_l, keys, keys_l, tree, tree_l = held
    lanes = lax.broadcasted_iota(jnp.int32, (TREE, 128), 1)
    tile4 = onehot(TREE, 128, lambda row, col: col % 32 == row)
    widen = onehot(TREE, 128, lambda row, col: col == row)
    above = lax.broadcasted_iota(jnp.int32, (TREE, TREE), 0)
    same = above == lax.broadcasted_iota(jnp.int32, (TREE, TREE), 1)
    extras = []
    for i, ids in enumerate((parents, parents_l)):
        reach = jnp.where(same | (above == ids[...]), 1.0, 0.0).astype(BF)
        for _ in range((TREE - 1).bit_length()):
            reach = jnp.minimum(dot(reach, reach), 1.0).astype(BF)
        extra = lax.dot_general(reach, widen, (((0,), (0,)), ((), ())), preferred_element_type=F32)
        if i == 1:
            extra = jnp.where(place[2] == 0, extra, 0.0)
        extra = jnp.where(lanes == 32, length[0, 0].astype(F32), extra)
        extras.append(jnp.where(lanes == 33, length_l[0, 0].astype(F32), extra).astype(BF))
    for copy in copies:
        copy.wait()
    for d in range(4):
        block[d, 0:288] = keys[:, :128]
        block[d, 288:576] = keys[:, 128:]
        block[d, 576:864] = keys_l[:, :128]
        block[d, 864:1152] = keys_l[:, 128:]
    for i, rows in enumerate((tree, tree_l)):
        parts = (rows[:, :128], rows[:, 128:KVR], dot(rows[:, KVR:], tile4).astype(BF), extras[i])
        for k, part in enumerate(parts):
            at = slice(TREE * k, TREE * (k + 1))
            if i == 0:
                for d in range(4):
                    block[d, TREE_AT + at.start : TREE_AT + at.stop] = part
            else:
                own_tree[at] = part

    def source(col):
        nope = 96 * (col // NOPE) + col % NOPE
        rope = 96 * ((col - 256) // ROPE) + NOPE + (col - 256) % ROPE
        return jnp.where(col < 256, nope, rope)

    sort = onehot(384, 384, lambda row, col: source(col) == row)
    rope = []
    for w in range(HEADS // 4):
        cols = slice(384 * w, 384 * (w + 1))
        moved = dot(jnp.concatenate([queries[:, cols], queries_l[:, cols]], axis=0), sort)
        rope.append(moved[:, 256:])
        for half in range(2):
            s, p = divmod(2 * w + half, SLICE // 2)
            part = moved[:, 128 * half : 128 * (half + 1)].astype(BF)
            block[s, QUERY_AT + TREE * p : QUERY_AT + TREE * (p + 1)] = part[:TREE]
            slices[s, TREE * p : TREE * (p + 1)] = part[TREE:]
    wide = lax.broadcasted_iota(jnp.int32, (2 * TREE, 128), 1)
    for s in range(4):
        first = SLICE * s // 4
        for k in range(3):
            if s % 2 == 0:
                part = rope[first + k]
            else:
                after = pltpu.roll(rope[first + k + 1], 64, 1) if k < 2 else jnp.zeros((2 * TREE, 128), F32)
                part = jnp.where(wide < 64, pltpu.roll(rope[first + k], 64, 1), after)
            part = part.astype(BF)
            at = TREE * (5 + k)
            block[s, QUERY_AT + at : QUERY_AT + at + TREE] = part[:TREE]
            slices[s, at : at + TREE] = part[TREE:]
    own_q[...] = slices[place[0]]


def on_device(
    queries, tree_latent, parents, cache, cache_lengths, accepted, residual,
    long_queries, long_tree_latent, long_parents, long_cache, long_plan, long_residual,
    key_up, value_up, out_weight,
):
    y, x, a = lax.axis_index("y"), lax.axis_index("x"), lax.axis_index("a")
    place = jnp.stack([x, a, y]).astype(jnp.int32)
    moved = jnp.pad(jnp.concatenate([key_up, value_up, out_weight], axis=1), ((0, 0), (0, 96)))
    moved = lax.ppermute(moved, ("x", "a"), [(4 * i + j, 4 * j + i) for i in range(4) for j in range(4)])
    rows = 8 * TREE
    block, query_l, tree_l = pl.pallas_call(
        pack_kernel,
        out_shape=(
            jax.ShapeDtypeStruct((4, BLOCK, 128), BF),
            jax.ShapeDtypeStruct((rows, 128), BF),
            jax.ShapeDtypeStruct((4 * TREE, 128), BF),
        ),
        in_specs=[SMEM] * 3 + [VMEM] * 2 + [HBM] * 6,
        out_specs=(VMEM, VMEM, VMEM),
        scratch_shapes=[pltpu.VMEM((TREE, HEADS * (NOPE + ROPE)), BF)] * 2
        + [pltpu.VMEM((KVR + ROPE, 256), BF)] * 2
        + [pltpu.VMEM((TREE, KVR + ROPE), BF)] * 2
        + [pltpu.VMEM((4, rows, 128), BF), pltpu.SemaphoreType.DMA((6,))],
        compiler_params=PARAMS,
    )(
        place, cache_lengths, long_plan, parents[0], long_parents, queries[0], long_queries[0],
        cache[0, 0].T, long_cache[0].T, tree_latent[0], long_tree_latent[0],
    )
    block, moved = lax.optimization_barrier((block, moved))
    got = lax.all_to_all(block, "x", 0, 0)
    held = moved[None, :, 2 * KVR : 2 * KVR + 160]
    far = lax.ppermute(held, "a", [((j + 2) % 4, j) for j in range(4)])
    moved, far = lax.optimization_barrier((moved, far))
    kv = lax.all_gather(moved[:, : 2 * KVR], ("b", "c")).reshape((4, 2) + key_up.shape[:1] + (2 * KVR,))
    held = jnp.concatenate([held, far])
    far = lax.ppermute(held, "a", [((j + 1) % 4, j) for j in range(4)])
    kv, far = lax.optimization_barrier((kv, far))
    blocks = [held[0], far[0], held[1], far[1]]
    tails = jnp.concatenate([part[:, 128:] for part in blocks], axis=1)
    out_rows = lax.all_gather(jnp.stack([part[:, :128] for part in blocks] + [tails]), ("b", "c"))
    out_rows = out_rows.reshape((4, 2) + out_rows.shape[1:])

    heads = pl.pallas_call(
        attend_kernel,
        out_shape=jax.ShapeDtypeStruct((4, 5 * TREE * (SLICE // 2) + 3 * TREE, 128), BF),
        in_specs=[VMEM] * 4,
        out_specs=VMEM,
        scratch_shapes=[pltpu.VMEM((5, SLICE * TREE, KVR), BF)],
        compiler_params=PARAMS,
    )(got, query_l, tree_l, kv)
    shared = lax.all_to_all(heads, "y", 0, 0)
    send = pl.pallas_call(
        project_kernel,
        out_shape=jax.ShapeDtypeStruct((4, 688, 128), BF),
        in_specs=[SMEM, VMEM, VMEM],
        out_specs=VMEM,
        scratch_shapes=[pltpu.VMEM((TOKENS, SPAN), BF)],
        compiler_params=PARAMS,
    )(place, shared, out_rows)
    back = lax.all_to_all(send, "x", 0, 0)
    hidden, long_hidden = pl.pallas_call(
        finish_kernel,
        out_shape=(
            jax.ShapeDtypeStruct(residual.shape, BF),
            jax.ShapeDtypeStruct(long_residual.shape, BF),
        ),
        in_specs=[VMEM, VMEM, VMEM],
        out_specs=(VMEM, VMEM),
        scratch_shapes=[pltpu.VMEM((TOKENS, 128), F32)],
        compiler_params=PARAMS,
    )(back, residual, long_residual)
    accepted_cache = jnp.take_along_axis(tree_latent[0], accepted[0, 0][:, None], axis=0)[None, None]
    return hidden, accepted_cache, long_hidden


def solution(mesh):
    split = Mesh(mesh.devices.reshape(4, 4, 4, 4, 2), ("y", "x", "a", "b", "c"))
    return jax.shard_map(
        on_device,
        mesh=split,
        in_specs=(
            P(ROWS, COLS, None),
            P(ROWS, COLS, None),
            P(ROWS, COLS, None),
            P(ROWS, COLS, None, None),
            P(ROWS, COLS),
            P(ROWS, COLS, None),
            P(None, COLS, ROWS),
            P(COLS, None, None),
            P(COLS, None, None),
            P(COLS, None),
            P(COLS, ROWS, None),
            P(COLS, ROWS),
            P(COLS, None, ROWS),
            P(COLS, None),
            P(COLS, None),
            P(COLS, ROWS),
        ),
        out_specs=(P(None, COLS, ROWS), P(ROWS, COLS, None, None), P(COLS, None, ROWS)),
        check_vma=False,
    )
```

```python
import jax
import jax.numpy as jnp
from jax import lax
from jax.experimental import pallas as pl
from jax.experimental.pallas import tpu as pltpu
from jax.sharding import Mesh, PartitionSpec as P

HEADS = 40
NOPE = 64
ROPE = 32
VDIM = 64
KVR = 256
TREE = 32
ROWS = ("y", "x")
COLS = ("a", "b", "c")
BF = jnp.bfloat16
F32 = jnp.float32


OVER_LAST = (((1,), (1,)), ((), ()))
SLICE = HEADS // 4
SPAN = SLICE * VDIM
LONG_AT, TREE_AT, QUERY_AT, OUT_AT, BLOCK = 576, 1152, 1280, 1536, 1696
TOKENS = 16 * TREE + TREE
QUARTER = TOKENS // 4


def split3(value):
    high = value.astype(BF)
    rest = value - high.astype(F32)
    mid = rest.astype(BF)
    return high, mid, (rest - mid.astype(F32)).astype(BF)


def dot(left, right):
    return jnp.dot(left, right, preferred_element_type=F32)


def dot_t(left, right):
    return lax.dot_general(left, right, OVER_LAST, preferred_element_type=F32)


def attend_kernel(got, query_l, tree_l, kv, out, lat):
    lanes = lax.broadcasted_iota(jnp.int32, (TREE, 128), 1)
    slots = lax.broadcasted_iota(jnp.int32, (1, 256), 1).astype(F32)
    scale = (NOPE + ROPE) ** -0.5
    size = SLICE * TREE

    def rope_rows(chunk):
        zero = jnp.zeros((TREE, 128), BF)
        return jnp.concatenate([jnp.where(lanes // 32 == h % 4, chunk(5 + h // 4), zero) for h in range(SLICE)], axis=0)

    def cached(query, rope, block, at, length):
        keys = jnp.concatenate([block[at : at + 288], block[at + 288 : at + 576]], axis=1)
        scores = dot(query, keys[:KVR]) + dot(rope, jnp.concatenate([keys[KVR:]] * 4, axis=0))
        return jnp.where(slots < length, scores * scale, -jnp.inf), keys[:KVR]

    def treed(query, rope, block, at):
        keys = jnp.concatenate([block[at : at + TREE], block[at + TREE : at + 2 * TREE]], axis=1)
        scores = dot_t(query, keys) + dot_t(rope, block[at + 2 * TREE : at + 3 * TREE])
        reach = block[at + 3 * TREE : at + 4 * TREE, :TREE].astype(F32)
        reach = jnp.concatenate([reach] * SLICE, axis=0)
        return jnp.where(reach > 0.5, scores * scale, -jnp.inf), keys

    for p in range(SLICE // 2):
        at = TREE * p
        rows = [got[k, QUERY_AT + at : QUERY_AT + at + TREE] for k in range(4)] + [query_l[at : at + TREE]]
        even = [jnp.where(lanes < NOPE, row, jnp.zeros_like(row)) for row in rows]
        odd = [jnp.where(lanes < NOPE, jnp.zeros_like(row), row) for row in rows]
        weight = kv[...][:, :, :, :KVR].reshape(SPAN, KVR)[128 * p : 128 * (p + 1)]
        part = dot(jnp.concatenate(even + odd, axis=0), weight).astype(BF)
        for s in range(2):
            for k in range(5):
                lat[k, TREE * (2 * p + s) : TREE * (2 * p + s + 1)] = part[TREE * (5 * s + k) : TREE * (5 * s + k + 1)]

    for k in range(4):
        block = got.at[k]
        query = lat[k]
        rope = rope_rows(lambda i: block[QUERY_AT + TREE * i : QUERY_AT + TREE * (i + 1)])
        length = block[TREE_AT + 3 * TREE : TREE_AT + 3 * TREE + 1, 32:33].astype(F32)
        first, keys = cached(query, rope, block, 0, length)
        second, tree = treed(query, rope, block, TREE_AT)
        top = jnp.maximum(jnp.max(first, axis=-1, keepdims=True), jnp.max(second, axis=-1, keepdims=True))
        first, second = jnp.exp(first - top), jnp.exp(second - top)
        total = jnp.sum(first, axis=-1, keepdims=True) + jnp.sum(second, axis=-1, keepdims=True)
        acc = dot_t(first.astype(BF), keys) + dot(second.astype(BF), tree)
        lat[k] = (acc / total).astype(BF)

    query = lat[4]
    rope = rope_rows(lambda i: query_l[TREE * i : TREE * (i + 1)])
    second, tree = treed(query, rope, tree_l, 0)
    scored = []
    for k in range(4):
        block = got.at[k]
        length = block[TREE_AT + 3 * TREE : TREE_AT + 3 * TREE + 1, 33:34].astype(F32)
        scored.append(cached(query, rope, block, LONG_AT, length))
    top = jnp.max(second, axis=-1, keepdims=True)
    for scores, _ in scored:
        top = jnp.maximum(top, jnp.max(scores, axis=-1, keepdims=True))
    second = jnp.exp(second - top)
    total = jnp.sum(second, axis=-1, keepdims=True)
    acc = dot(second.astype(BF), tree)
    for scores, keys in scored:
        weights = jnp.exp(scores - top)
        total += jnp.sum(weights, axis=-1, keepdims=True)
        acc += dot_t(weights.astype(BF), keys)
    lat[4] = (acc / total).astype(BF)
    column = top + jnp.log(total)
    logs = jnp.zeros((TREE, 128), F32)
    for h in range(SLICE):
        logs = jnp.where(lanes == h, column[TREE * h : TREE * (h + 1)], logs)

    for p in range(SLICE // 2):
        pair = []
        for h in (2 * p, 2 * p + 1):
            rows = jnp.concatenate([lat[k, TREE * h : TREE * (h + 1)] for k in range(5)], axis=0)
            weight = kv[...][:, :, :, KVR:].reshape(SPAN, KVR)[VDIM * h : VDIM * (h + 1)]
            pair.append(dot_t(rows, weight))
        heads = jnp.concatenate(pair, axis=1).astype(BF)
        for d in range(4):
            out[d, 5 * TREE * p : 5 * TREE * (p + 1)] = heads
    base = 5 * TREE * (SLICE // 2)
    for i, part in enumerate(split3(logs)):
        for d in range(4):
            out[d, base + TREE * i : base + TREE * (i + 1)] = part


def project_kernel(got, weight, send, rows):
    base = 5 * TREE * (SLICE // 2)
    logs = sum(got[:, base + TREE * i : base + TREE * (i + 1)].astype(F32) for i in range(3))
    share = jnp.exp(logs - jnp.max(logs, axis=0)[None])
    share = (share / jnp.sum(share, axis=0)[None]).reshape(4 * TREE, 128)
    high = share.astype(BF)
    low = (share - high.astype(F32)).astype(BF)
    for p in range(SLICE // 2):
        at = 5 * TREE * p
        cols = slice(128 * p, 128 * (p + 1))
        for y in range(4):
            rows[4 * TREE * y : 4 * TREE * (y + 1), cols] = got[y, at : at + 4 * TREE]
        owner = lax.broadcasted_iota(jnp.int32, (128, 128), 1) // VDIM + 2 * p
        select = jnp.where(lax.broadcasted_iota(jnp.int32, (128, 128), 0) == owner, 1.0, 0.0).astype(BF)
        wide = (dot(high, select) + dot(low, select)).reshape(4, TREE, 128)
        piece = got[:, at + 4 * TREE : at + 5 * TREE].astype(F32) * wide
        rows[16 * TREE : 17 * TREE, cols] = jnp.sum(piece, axis=0).astype(BF)
    rest = dot(rows[...], weight[:, :, 4].reshape(SPAN, 128))
    lanes = lax.broadcasted_iota(jnp.int32, (QUARTER, 128), 1) // 32
    for k in range(4):
        send[k, :TOKENS] = dot(rows[...], weight[:, :, k].reshape(SPAN, 128)).astype(BF)
        packed = jnp.zeros((QUARTER, 128), F32)
        for g in range(4):
            part = rest[QUARTER * g : QUARTER * (g + 1)]
            shift = (32 * (g - k)) % 128
            part = pltpu.roll(part, shift, 1) if shift else part
            packed = jnp.where(lanes == g, part, packed)
        send[k, TOKENS : TOKENS + QUARTER] = packed.astype(BF)
        send[k, TOKENS + QUARTER :] = jnp.zeros((send.shape[1] - TOKENS - QUARTER, 128), BF)


def finish_kernel(got, residual, long_residual, hidden, long_hidden, tail):
    rest = jnp.sum(got[:, TOKENS : TOKENS + QUARTER].astype(F32), axis=0)
    for g in range(4):
        tail[QUARTER * g : QUARTER * (g + 1)] = pltpu.roll(rest, (-32 * g) % 128, 1) if g else rest
    for i in range(17):
        at = slice(TREE * i, TREE * (i + 1))
        main = jnp.sum(got[:, at].astype(F32), axis=0)
        source, target, k = (residual, hidden, i) if i < 16 else (long_residual, long_hidden, 0)
        target[k, :, :128] = (source[k, :, :128].astype(F32) + main).astype(BF)
        target[k, :, 128:160] = (source[k, :, 128:160].astype(F32) + tail[at, :32]).astype(BF)


SMEM = pl.BlockSpec(memory_space=pltpu.SMEM)
VMEM = pl.BlockSpec(memory_space=pltpu.VMEM)
HBM = pl.BlockSpec(memory_space=pltpu.HBM)
COST = pl.CostEstimate(flops=6 * 10**9, transcendentals=10**6, bytes_accessed=18 * 10**6)
PARAMS = pltpu.CompilerParams(vmem_limit_bytes=48 << 20)


def onehot(rows, cols, match):
    row = lax.broadcasted_iota(jnp.int32, (rows, cols), 0)
    col = lax.broadcasted_iota(jnp.int32, (rows, cols), 1)
    return jnp.where(match(row, col), 1.0, 0.0).astype(BF)


def pack_kernel(place, length, length_l, parents, parents_l, *refs):
    sources, (block, own_q, own_tree), held, (slices, sems) = refs[:7], refs[7:10], refs[10:17], refs[17:]
    copies = [pltpu.make_async_copy(sources[i], held[i], sems.at[i]) for i in range(7)]
    for copy in copies:
        copy.start()
    queries, queries_l, keys, keys_l, tree, tree_l, weight = held
    lanes = lax.broadcasted_iota(jnp.int32, (TREE, 128), 1)
    tile4 = onehot(TREE, 128, lambda row, col: col % 32 == row)
    widen = onehot(TREE, 128, lambda row, col: col == row)
    above = lax.broadcasted_iota(jnp.int32, (TREE, TREE), 0)
    same = above == lax.broadcasted_iota(jnp.int32, (TREE, TREE), 1)
    extras = []
    for i, ids in enumerate((parents, parents_l)):
        reach = jnp.where(same | (above == ids[...]), 1.0, 0.0).astype(BF)
        for _ in range((TREE - 1).bit_length()):
            reach = jnp.minimum(dot(reach, reach), 1.0).astype(BF)
        extra = lax.dot_general(reach, widen, (((0,), (0,)), ((), ())), preferred_element_type=F32)
        if i == 1:
            extra = jnp.where(place[1] == 0, extra, 0.0)
        extra = jnp.where(lanes == 32, length[0, 0].astype(F32), extra)
        extras.append(jnp.where(lanes == 33, length_l[0, 0].astype(F32), extra).astype(BF))
    for copy in copies:
        copy.wait()
    tail = dot(weight[:, 128:], widen).astype(BF)
    for d in range(4):
        block[d, OUT_AT : OUT_AT + 80] = weight[:, :128]
        block[d, OUT_AT + 80 : BLOCK] = tail
        block[d, 0:288] = keys[:, :128]
        block[d, 288:576] = keys[:, 128:]
        block[d, 576:864] = keys_l[:, :128]
        block[d, 864:1152] = keys_l[:, 128:]
    for i, rows in enumerate((tree, tree_l)):
        parts = (rows[:, :128], rows[:, 128:KVR], dot(rows[:, KVR:], tile4).astype(BF), extras[i])
        for k, part in enumerate(parts):
            at = slice(TREE * k, TREE * (k + 1))
            if i == 0:
                for d in range(4):
                    block[d, TREE_AT + at.start : TREE_AT + at.stop] = part
            else:
                own_tree[at] = part

    def source(col):
        nope = 96 * (col // NOPE) + col % NOPE
        rope = 96 * ((col - 256) // ROPE) + NOPE + (col - 256) % ROPE
        return jnp.where(col < 256, nope, rope)

    sort = onehot(384, 384, lambda row, col: source(col) == row)
    rope = []
    for w in range(HEADS // 4):
        cols = slice(384 * w, 384 * (w + 1))
        moved = dot(jnp.concatenate([queries[:, cols], queries_l[:, cols]], axis=0), sort)
        rope.append(moved[:, 256:])
        for half in range(2):
            s, p = divmod(2 * w + half, SLICE // 2)
            part = moved[:, 128 * half : 128 * (half + 1)].astype(BF)
            block[s, QUERY_AT + TREE * p : QUERY_AT + TREE * (p + 1)] = part[:TREE]
            slices[s, TREE * p : TREE * (p + 1)] = part[TREE:]
    wide = lax.broadcasted_iota(jnp.int32, (2 * TREE, 128), 1)
    for s in range(4):
        first = SLICE * s // 4
        for k in range(3):
            if s % 2 == 0:
                part = rope[first + k]
            else:
                after = pltpu.roll(rope[first + k + 1], 64, 1) if k < 2 else jnp.zeros((2 * TREE, 128), F32)
                part = jnp.where(wide < 64, pltpu.roll(rope[first + k], 64, 1), after)
            part = part.astype(BF)
            at = TREE * (5 + k)
            block[s, QUERY_AT + at : QUERY_AT + at + TREE] = part[:TREE]
            slices[s, at : at + TREE] = part[TREE:]
    own_q[...] = slices[place[0]]


def on_device(
    queries, tree_latent, parents, cache, cache_lengths, accepted, residual,
    long_queries, long_tree_latent, long_parents, long_cache, long_plan, long_residual,
    key_up, value_up, out_weight,
):
    y, x = lax.axis_index("y"), lax.axis_index("x")
    place = jnp.stack([x, y]).astype(jnp.int32)
    pairs = [(r * 16 + z, ((z % 4) * 4 + z // 4) * 16 + (z + r) % 16) for r in range(16) for z in range(16)]
    kv, place = lax.optimization_barrier((jnp.concatenate([key_up, value_up], axis=1), place))
    kv = lax.ppermute(kv, ("y", "x", "a", "b"), pairs)
    rows = 8 * TREE
    block, query_l, tree_l = pl.pallas_call(
        pack_kernel,
        out_shape=(
            jax.ShapeDtypeStruct((4, BLOCK, 128), BF),
            jax.ShapeDtypeStruct((rows, 128), BF),
            jax.ShapeDtypeStruct((4 * TREE, 128), BF),
        ),
        in_specs=[SMEM] * 3 + [VMEM] * 2 + [HBM] * 7,
        out_specs=(VMEM, VMEM, VMEM),
        scratch_shapes=[pltpu.VMEM((TREE, HEADS * (NOPE + ROPE)), BF)] * 2
        + [pltpu.VMEM((KVR + ROPE, 256), BF)] * 2
        + [pltpu.VMEM((TREE, KVR + ROPE), BF)] * 2
        + [pltpu.VMEM(out_weight.shape, BF)]
        + [pltpu.VMEM((4, rows, 128), BF), pltpu.SemaphoreType.DMA((7,))],
        compiler_params=PARAMS,
        cost_estimate=COST,
    )(
        place, cache_lengths, long_plan, parents[0], long_parents,
        *[
            pltpu.with_memory_space_constraint(value, pltpu.HBM)
            for value in (
                queries[0], long_queries[0], cache[0, 0].T, long_cache[0].T,
                tree_latent[0], long_tree_latent[0], out_weight,
            )
        ],
    )
    block, kv = lax.optimization_barrier((block, kv))
    got = lax.all_to_all(block, "x", 0, 0)
    kv = lax.all_gather(kv, ("y", "c"))
    kv = kv.reshape((4, 2) + kv.shape[1:])
    shard = out_weight.shape[0]
    tails = [got[k, OUT_AT + shard : BLOCK, :32] for k in range(4)]
    out_rows = [got[k, OUT_AT : OUT_AT + shard] for k in range(4)] + [jnp.concatenate(tails, axis=1)]
    swap = [(4 * i + j, 4 * j + i) for i in range(4) for j in range(4)]
    got, out_rows = lax.optimization_barrier((got, jnp.stack(out_rows)))
    out_rows = lax.ppermute(out_rows, ("x", "a"), swap)

    heads = pl.pallas_call(
        attend_kernel,
        out_shape=jax.ShapeDtypeStruct((4, 5 * TREE * (SLICE // 2) + 3 * TREE, 128), BF),
        in_specs=[VMEM] * 4,
        out_specs=VMEM,
        scratch_shapes=[pltpu.VMEM((5, SLICE * TREE, KVR), BF)],
        compiler_params=PARAMS,
        cost_estimate=COST,
    )(got, query_l, tree_l, kv)
    heads, out_rows = lax.optimization_barrier((heads, out_rows))
    shared = lax.all_to_all(heads, "y", 0, 0)
    out_rows = lax.all_gather(out_rows, ("b", "c"))
    out_rows = out_rows.reshape((4, 2) + out_rows.shape[1:])
    send = pl.pallas_call(
        project_kernel,
        out_shape=jax.ShapeDtypeStruct((4, 688, 128), BF),
        in_specs=[VMEM, VMEM],
        out_specs=VMEM,
        scratch_shapes=[pltpu.VMEM((TOKENS, SPAN), BF)],
        compiler_params=PARAMS,
    )(shared, out_rows)
    back = lax.all_to_all(send, "x", 0, 0)
    hidden, long_hidden = pl.pallas_call(
        finish_kernel,
        out_shape=(
            jax.ShapeDtypeStruct(residual.shape, BF),
            jax.ShapeDtypeStruct(long_residual.shape, BF),
        ),
        in_specs=[VMEM, VMEM, VMEM],
        out_specs=(VMEM, VMEM),
        scratch_shapes=[pltpu.VMEM((TOKENS, 128), F32)],
        compiler_params=PARAMS,
    )(back, residual, long_residual)
    accepted_cache = jnp.take_along_axis(tree_latent[0], accepted[0, 0][:, None], axis=0)[None, None]
    return hidden, accepted_cache, long_hidden


def solution(mesh):
    split = Mesh(mesh.devices.reshape(4, 4, 4, 4, 2), ("y", "x", "a", "b", "c"))
    return jax.shard_map(
        on_device,
        mesh=split,
        in_specs=(
            P(ROWS, COLS, None),
            P(ROWS, COLS, None),
            P(ROWS, COLS, None),
            P(ROWS, COLS, None, None),
            P(ROWS, COLS),
            P(ROWS, COLS, None),
            P(None, COLS, ROWS),
            P(COLS, None, None),
            P(COLS, None, None),
            P(COLS, None),
            P(COLS, ROWS, None),
            P(COLS, ROWS),
            P(COLS, None, ROWS),
            P(COLS, None),
            P(COLS, None),
            P(COLS, ROWS),
        ),
        out_specs=(P(None, COLS, ROWS), P(ROWS, COLS, None, None), P(COLS, None, ROWS)),
        check_vma=False,
    )
```

```python
import jax
import jax.numpy as jnp
from jax import lax
from jax.experimental import pallas as pl
from jax.experimental.pallas import tpu as pltpu
from jax.sharding import Mesh, PartitionSpec as P

HEADS = 40
NOPE = 64
ROPE = 32
VDIM = 64
KVR = 256
TREE = 32
ROWS = ("y", "x")
COLS = ("a", "b", "c")
BF = jnp.bfloat16
F32 = jnp.float32


OVER_LAST = (((1,), (1,)), ((), ()))
SLICE = HEADS // 4
SPAN = SLICE * VDIM
LONG_AT, TREE_AT, QUERY_AT, BLOCK = 576, 1152, 1280, 1536
TOKENS = 16 * TREE + TREE
QUARTER = TOKENS // 4


def split3(value):
    high = value.astype(BF)
    rest = value - high.astype(F32)
    mid = rest.astype(BF)
    return high, mid, (rest - mid.astype(F32)).astype(BF)


def dot(left, right):
    return jnp.dot(left, right, preferred_element_type=F32)


def dot_t(left, right):
    return lax.dot_general(left, right, OVER_LAST, preferred_element_type=F32)


def attend_kernel(got, query_l, tree_l, kv, out, lat):
    lanes = lax.broadcasted_iota(jnp.int32, (TREE, 128), 1)
    slots = lax.broadcasted_iota(jnp.int32, (1, 256), 1).astype(F32)
    scale = (NOPE + ROPE) ** -0.5
    size = SLICE * TREE

    def rope_rows(chunk):
        zero = jnp.zeros((TREE, 128), BF)
        return jnp.concatenate([jnp.where(lanes // 32 == h % 4, chunk(5 + h // 4), zero) for h in range(SLICE)], axis=0)

    def cached(query, rope, block, at, length):
        keys = jnp.concatenate([block[at : at + 288], block[at + 288 : at + 576]], axis=1)
        scores = dot(query, keys[:KVR]) + dot(rope, jnp.concatenate([keys[KVR:]] * 4, axis=0))
        return jnp.where(slots < length, scores * scale, -jnp.inf), keys[:KVR]

    def treed(query, rope, block, at):
        keys = jnp.concatenate([block[at : at + TREE], block[at + TREE : at + 2 * TREE]], axis=1)
        scores = dot_t(query, keys) + dot_t(rope, block[at + 2 * TREE : at + 3 * TREE])
        reach = block[at + 3 * TREE : at + 4 * TREE, :TREE].astype(F32)
        reach = jnp.concatenate([reach] * SLICE, axis=0)
        return jnp.where(reach > 0.5, scores * scale, -jnp.inf), keys

    for p in range(SLICE // 2):
        at = TREE * p
        rows = [got[k, QUERY_AT + at : QUERY_AT + at + TREE] for k in range(4)] + [query_l[at : at + TREE]]
        even = [jnp.where(lanes < NOPE, row, jnp.zeros_like(row)) for row in rows]
        odd = [jnp.where(lanes < NOPE, jnp.zeros_like(row), row) for row in rows]
        weight = kv[...][:, :, :, :KVR].reshape(SPAN, KVR)[128 * p : 128 * (p + 1)]
        part = dot(jnp.concatenate(even + odd, axis=0), weight).astype(BF)
        for s in range(2):
            for k in range(5):
                lat[k, TREE * (2 * p + s) : TREE * (2 * p + s + 1)] = part[TREE * (5 * s + k) : TREE * (5 * s + k + 1)]

    for k in range(4):
        block = got.at[k]
        query = lat[k]
        rope = rope_rows(lambda i: block[QUERY_AT + TREE * i : QUERY_AT + TREE * (i + 1)])
        length = block[TREE_AT + 3 * TREE : TREE_AT + 3 * TREE + 1, 32:33].astype(F32)
        first, keys = cached(query, rope, block, 0, length)
        second, tree = treed(query, rope, block, TREE_AT)
        top = jnp.maximum(jnp.max(first, axis=-1, keepdims=True), jnp.max(second, axis=-1, keepdims=True))
        first, second = jnp.exp(first - top), jnp.exp(second - top)
        total = jnp.sum(first, axis=-1, keepdims=True) + jnp.sum(second, axis=-1, keepdims=True)
        acc = dot_t(first.astype(BF), keys) + dot(second.astype(BF), tree)
        lat[k] = (acc / total).astype(BF)

    query = lat[4]
    rope = rope_rows(lambda i: query_l[TREE * i : TREE * (i + 1)])
    second, tree = treed(query, rope, tree_l, 0)
    scored = []
    for k in range(4):
        block = got.at[k]
        length = block[TREE_AT + 3 * TREE : TREE_AT + 3 * TREE + 1, 33:34].astype(F32)
        scored.append(cached(query, rope, block, LONG_AT, length))
    top = jnp.max(second, axis=-1, keepdims=True)
    for scores, _ in scored:
        top = jnp.maximum(top, jnp.max(scores, axis=-1, keepdims=True))
    second = jnp.exp(second - top)
    total = jnp.sum(second, axis=-1, keepdims=True)
    acc = dot(second.astype(BF), tree)
    for scores, keys in scored:
        weights = jnp.exp(scores - top)
        total += jnp.sum(weights, axis=-1, keepdims=True)
        acc += dot_t(weights.astype(BF), keys)
    lat[4] = (acc / total).astype(BF)
    column = top + jnp.log(total)
    logs = jnp.zeros((TREE, 128), F32)
    for h in range(SLICE):
        logs = jnp.where(lanes == h, column[TREE * h : TREE * (h + 1)], logs)

    for p in range(SLICE // 2):
        pair = []
        for h in (2 * p, 2 * p + 1):
            rows = jnp.concatenate([lat[k, TREE * h : TREE * (h + 1)] for k in range(5)], axis=0)
            weight = kv[...][:, :, :, KVR:].reshape(SPAN, KVR)[VDIM * h : VDIM * (h + 1)]
            pair.append(dot_t(rows, weight))
        heads = jnp.concatenate(pair, axis=1).astype(BF)
        for d in range(4):
            out[d, 5 * TREE * p : 5 * TREE * (p + 1)] = heads
    base = 5 * TREE * (SLICE // 2)
    for i, part in enumerate(split3(logs)):
        for d in range(4):
            out[d, base + TREE * i : base + TREE * (i + 1)] = part


def project_kernel(got, weight, send, rows):
    base = 5 * TREE * (SLICE // 2)
    logs = sum(got[:, base + TREE * i : base + TREE * (i + 1)].astype(F32) for i in range(3))
    share = jnp.exp(logs - jnp.max(logs, axis=0)[None])
    share = (share / jnp.sum(share, axis=0)[None]).reshape(4 * TREE, 128)
    high = share.astype(BF)
    low = (share - high.astype(F32)).astype(BF)
    for p in range(SLICE // 2):
        at = 5 * TREE * p
        cols = slice(128 * p, 128 * (p + 1))
        for y in range(4):
            rows[4 * TREE * y : 4 * TREE * (y + 1), cols] = got[y, at : at + 4 * TREE]
        owner = lax.broadcasted_iota(jnp.int32, (128, 128), 1) // VDIM + 2 * p
        select = jnp.where(lax.broadcasted_iota(jnp.int32, (128, 128), 0) == owner, 1.0, 0.0).astype(BF)
        wide = (dot(high, select) + dot(low, select)).reshape(4, TREE, 128)
        piece = got[:, at + 4 * TREE : at + 5 * TREE].astype(F32) * wide
        rows[16 * TREE : 17 * TREE, cols] = jnp.sum(piece, axis=0).astype(BF)
    rest = dot(rows[...], weight[:, :, 4].reshape(SPAN, 128))
    lanes = lax.broadcasted_iota(jnp.int32, (QUARTER, 128), 1) // 32
    for k in range(4):
        send[k, :TOKENS] = dot(rows[...], weight[:, :, k].reshape(SPAN, 128)).astype(BF)
        packed = jnp.zeros((QUARTER, 128), F32)
        for g in range(4):
            part = rest[QUARTER * g : QUARTER * (g + 1)]
            shift = (32 * (g - k)) % 128
            part = pltpu.roll(part, shift, 1) if shift else part
            packed = jnp.where(lanes == g, part, packed)
        send[k, TOKENS : TOKENS + QUARTER] = packed.astype(BF)
        send[k, TOKENS + QUARTER :] = jnp.zeros((send.shape[1] - TOKENS - QUARTER, 128), BF)


def finish_kernel(got, residual, long_residual, hidden, long_hidden, tail):
    rest = jnp.sum(got[:, TOKENS : TOKENS + QUARTER].astype(F32), axis=0)
    for g in range(4):
        tail[QUARTER * g : QUARTER * (g + 1)] = pltpu.roll(rest, (-32 * g) % 128, 1) if g else rest
    for i in range(17):
        at = slice(TREE * i, TREE * (i + 1))
        main = jnp.sum(got[:, at].astype(F32), axis=0)
        source, target, k = (residual, hidden, i) if i < 16 else (long_residual, long_hidden, 0)
        target[k, :, :128] = (source[k, :, :128].astype(F32) + main).astype(BF)
        target[k, :, 128:160] = (source[k, :, 128:160].astype(F32) + tail[at, :32]).astype(BF)


SMEM = pl.BlockSpec(memory_space=pltpu.SMEM)
VMEM = pl.BlockSpec(memory_space=pltpu.VMEM)
HBM = pl.BlockSpec(memory_space=pltpu.HBM)
COST = pl.CostEstimate(flops=6 * 10**9, transcendentals=10**6, bytes_accessed=18 * 10**6)
PARAMS = pltpu.CompilerParams(vmem_limit_bytes=48 << 20)


def onehot(rows, cols, match):
    row = lax.broadcasted_iota(jnp.int32, (rows, cols), 0)
    col = lax.broadcasted_iota(jnp.int32, (rows, cols), 1)
    return jnp.where(match(row, col), 1.0, 0.0).astype(BF)


def pack_kernel(place, length, length_l, parents, parents_l, *refs):
    sources, (block, own_q, own_tree), held, (slices, sems) = refs[:6], refs[6:9], refs[9:15], refs[15:]
    copies = [pltpu.make_async_copy(sources[i], held[i], sems.at[i]) for i in range(6)]
    for copy in copies:
        copy.start()
    queries, queries_l, keys, keys_l, tree, tree_l = held
    lanes = lax.broadcasted_iota(jnp.int32, (TREE, 128), 1)
    tile4 = onehot(TREE, 128, lambda row, col: col % 32 == row)
    widen = onehot(TREE, 128, lambda row, col: col == row)
    above = lax.broadcasted_iota(jnp.int32, (TREE, TREE), 0)
    same = above == lax.broadcasted_iota(jnp.int32, (TREE, TREE), 1)
    extras = []
    for i, ids in enumerate((parents, parents_l)):
        reach = jnp.where(same | (above == ids[...]), 1.0, 0.0).astype(BF)
        for _ in range((TREE - 1).bit_length()):
            reach = jnp.minimum(dot(reach, reach), 1.0).astype(BF)
        extra = lax.dot_general(reach, widen, (((0,), (0,)), ((), ())), preferred_element_type=F32)
        if i == 1:
            extra = jnp.where(place[1] == 0, extra, 0.0)
        extra = jnp.where(lanes == 32, length[0, 0].astype(F32), extra)
        extras.append(jnp.where(lanes == 33, length_l[0, 0].astype(F32), extra).astype(BF))
    for copy in copies:
        copy.wait()
    for d in range(4):
        block[d, 0:288] = keys[:, :128]
        block[d, 288:576] = keys[:, 128:]
        block[d, 576:864] = keys_l[:, :128]
        block[d, 864:1152] = keys_l[:, 128:]
    for i, rows in enumerate((tree, tree_l)):
        parts = (rows[:, :128], rows[:, 128:KVR], dot(rows[:, KVR:], tile4).astype(BF), extras[i])
        for k, part in enumerate(parts):
            at = slice(TREE * k, TREE * (k + 1))
            if i == 0:
                for d in range(4):
                    block[d, TREE_AT + at.start : TREE_AT + at.stop] = part
            else:
                own_tree[at] = part

    def source(col):
        nope = 96 * (col // NOPE) + col % NOPE
        rope = 96 * ((col - 256) // ROPE) + NOPE + (col - 256) % ROPE
        return jnp.where(col < 256, nope, rope)

    sort = onehot(384, 384, lambda row, col: source(col) == row)
    rope = []
    for w in range(HEADS // 4):
        cols = slice(384 * w, 384 * (w + 1))
        moved = dot(jnp.concatenate([queries[:, cols], queries_l[:, cols]], axis=0), sort)
        rope.append(moved[:, 256:])
        for half in range(2):
            s, p = divmod(2 * w + half, SLICE // 2)
            part = moved[:, 128 * half : 128 * (half + 1)].astype(BF)
            block[s, QUERY_AT + TREE * p : QUERY_AT + TREE * (p + 1)] = part[:TREE]
            slices[s, TREE * p : TREE * (p + 1)] = part[TREE:]
    wide = lax.broadcasted_iota(jnp.int32, (2 * TREE, 128), 1)
    for s in range(4):
        first = SLICE * s // 4
        for k in range(3):
            if s % 2 == 0:
                part = rope[first + k]
            else:
                after = pltpu.roll(rope[first + k + 1], 64, 1) if k < 2 else jnp.zeros((2 * TREE, 128), F32)
                part = jnp.where(wide < 64, pltpu.roll(rope[first + k], 64, 1), after)
            part = part.astype(BF)
            at = TREE * (5 + k)
            block[s, QUERY_AT + at : QUERY_AT + at + TREE] = part[:TREE]
            slices[s, at : at + TREE] = part[TREE:]
    own_q[...] = slices[place[0]]


def on_device(
    queries, tree_latent, parents, cache, cache_lengths, accepted, residual,
    long_queries, long_tree_latent, long_parents, long_cache, long_plan, long_residual,
    key_up, value_up, out_weight,
):
    y, x = lax.axis_index("y"), lax.axis_index("x")
    place = jnp.stack([x, y]).astype(jnp.int32)
    pairs = [(r * 16 + z, ((z % 4) * 4 + z // 4) * 16 + (z + r) % 16) for r in range(16) for z in range(16)]
    kv, place = lax.optimization_barrier((jnp.concatenate([key_up, value_up], axis=1), place))
    kv = lax.ppermute(kv, ("y", "x", "a", "b"), pairs)
    rows = 8 * TREE
    block, query_l, tree_l = pl.pallas_call(
        pack_kernel,
        out_shape=(
            jax.ShapeDtypeStruct((4, BLOCK, 128), BF),
            jax.ShapeDtypeStruct((rows, 128), BF),
            jax.ShapeDtypeStruct((4 * TREE, 128), BF),
        ),
        in_specs=[SMEM] * 3 + [VMEM] * 2 + [HBM] * 6,
        out_specs=(VMEM, VMEM, VMEM),
        scratch_shapes=[pltpu.VMEM((TREE, HEADS * (NOPE + ROPE)), BF)] * 2
        + [pltpu.VMEM((KVR + ROPE, 256), BF)] * 2
        + [pltpu.VMEM((TREE, KVR + ROPE), BF)] * 2
        + [pltpu.VMEM((4, rows, 128), BF), pltpu.SemaphoreType.DMA((6,))],
        compiler_params=PARAMS,
        cost_estimate=COST,
    )(
        place, cache_lengths, long_plan, parents[0], long_parents,
        *[
            pltpu.with_memory_space_constraint(value, pltpu.HBM)
            for value in (
                queries[0], long_queries[0], cache[0, 0].T, long_cache[0].T,
                tree_latent[0], long_tree_latent[0],
            )
        ],
    )
    cols = lax.all_gather(out_weight, "x")
    out_rows = jnp.stack([cols[k, :, :128] for k in range(4)] + [jnp.concatenate([cols[k, :, 128:] for k in range(4)], axis=1)])
    block, kv, out_rows = lax.optimization_barrier((block, kv, out_rows))
    got = lax.all_to_all(block, "x", 0, 0)
    out_rows = lax.ppermute(out_rows, ("x", "a"), [(4 * i + j, 4 * j + i) for i in range(4) for j in range(4)])
    kv = lax.all_gather(kv, ("y", "c"))
    kv, out_rows = lax.optimization_barrier((kv, out_rows))
    kv = kv.reshape((4, 2) + kv.shape[1:])

    heads = pl.pallas_call(
        attend_kernel,
        out_shape=jax.ShapeDtypeStruct((4, 5 * TREE * (SLICE // 2) + 3 * TREE, 128), BF),
        in_specs=[VMEM] * 4,
        out_specs=VMEM,
        scratch_shapes=[pltpu.VMEM((5, SLICE * TREE, KVR), BF)],
        compiler_params=PARAMS,
        cost_estimate=COST,
    )(got, query_l, tree_l, kv)
    shared = lax.all_to_all(heads, "y", 0, 0)
    out_rows = lax.all_gather(out_rows, ("b", "c"))
    out_rows = out_rows.reshape((4, 2) + out_rows.shape[1:])
    send = pl.pallas_call(
        project_kernel,
        out_shape=jax.ShapeDtypeStruct((4, 688, 128), BF),
        in_specs=[VMEM, VMEM],
        out_specs=VMEM,
        scratch_shapes=[pltpu.VMEM((TOKENS, SPAN), BF)],
        compiler_params=PARAMS,
    )(shared, out_rows)
    back = lax.all_to_all(send, "x", 0, 0)
    hidden, long_hidden = pl.pallas_call(
        finish_kernel,
        out_shape=(
            jax.ShapeDtypeStruct(residual.shape, BF),
            jax.ShapeDtypeStruct(long_residual.shape, BF),
        ),
        in_specs=[VMEM, VMEM, VMEM],
        out_specs=(VMEM, VMEM),
        scratch_shapes=[pltpu.VMEM((TOKENS, 128), F32)],
        compiler_params=PARAMS,
    )(back, residual, long_residual)
    accepted_cache = jnp.take_along_axis(tree_latent[0], accepted[0, 0][:, None], axis=0)[None, None]
    return hidden, accepted_cache, long_hidden


def solution(mesh):
    split = Mesh(mesh.devices.reshape(4, 4, 4, 4, 2), ("y", "x", "a", "b", "c"))
    return jax.shard_map(
        on_device,
        mesh=split,
        in_specs=(
            P(ROWS, COLS, None),
            P(ROWS, COLS, None),
            P(ROWS, COLS, None),
            P(ROWS, COLS, None, None),
            P(ROWS, COLS),
            P(ROWS, COLS, None),
            P(None, COLS, ROWS),
            P(COLS, None, None),
            P(COLS, None, None),
            P(COLS, None),
            P(COLS, ROWS, None),
            P(COLS, ROWS),
            P(COLS, None, ROWS),
            P(COLS, None),
            P(COLS, None),
            P(COLS, ROWS),
        ),
        out_specs=(P(None, COLS, ROWS), P(ROWS, COLS, None, None), P(COLS, None, ROWS)),
        check_vma=False,
    )
```

```python
import jax
import jax.numpy as jnp
from jax import lax
from jax.experimental import pallas as pl
from jax.experimental.pallas import tpu as pltpu
from jax.sharding import Mesh, PartitionSpec as P

HEADS = 40
NOPE = 64
ROPE = 32
VDIM = 64
KVR = 256
TREE = 32
ROWS = ("y", "x")
COLS = ("a", "b", "c")
BF = jnp.bfloat16
F32 = jnp.float32


OVER_LAST = (((1,), (1,)), ((), ()))
SLICE = HEADS // 4
SPAN = SLICE * VDIM
LONG_AT, TREE_AT, QUERY_AT, BLOCK = 576, 1152, 1280, 1536
TOKENS = 16 * TREE + TREE
QUARTER = TOKENS // 4


def split3(value):
    high = value.astype(BF)
    rest = value - high.astype(F32)
    mid = rest.astype(BF)
    return high, mid, (rest - mid.astype(F32)).astype(BF)


def dot(left, right):
    return jnp.dot(left, right, preferred_element_type=F32)


def dot_t(left, right):
    return lax.dot_general(left, right, OVER_LAST, preferred_element_type=F32)


def attend_kernel(got, query_l, tree_l, kv, out, lat):
    lanes = lax.broadcasted_iota(jnp.int32, (TREE, 128), 1)
    slots = lax.broadcasted_iota(jnp.int32, (1, 256), 1).astype(F32)
    scale = (NOPE + ROPE) ** -0.5
    size = SLICE * TREE

    def rope_rows(chunk):
        zero = jnp.zeros((TREE, 128), BF)
        return jnp.concatenate([jnp.where(lanes // 32 == h % 4, chunk(5 + h // 4), zero) for h in range(SLICE)], axis=0)

    def cached(query, rope, block, at, length):
        keys = jnp.concatenate([block[at : at + 288], block[at + 288 : at + 576]], axis=1)
        scores = dot(query, keys[:KVR]) + dot(rope, jnp.concatenate([keys[KVR:]] * 4, axis=0))
        return jnp.where(slots < length, scores * scale, -jnp.inf), keys[:KVR]

    def treed(query, rope, block, at):
        keys = jnp.concatenate([block[at : at + TREE], block[at + TREE : at + 2 * TREE]], axis=1)
        scores = dot_t(query, keys) + dot_t(rope, block[at + 2 * TREE : at + 3 * TREE])
        reach = block[at + 3 * TREE : at + 4 * TREE, :TREE].astype(F32)
        reach = jnp.concatenate([reach] * SLICE, axis=0)
        return jnp.where(reach > 0.5, scores * scale, -jnp.inf), keys

    for p in range(SLICE // 2):
        at = TREE * p
        rows = [got[k, QUERY_AT + at : QUERY_AT + at + TREE] for k in range(4)] + [query_l[at : at + TREE]]
        even = [jnp.where(lanes < NOPE, row, jnp.zeros_like(row)) for row in rows]
        odd = [jnp.where(lanes < NOPE, jnp.zeros_like(row), row) for row in rows]
        weight = kv[...][:, :, :, :KVR].reshape(SPAN, KVR)[128 * p : 128 * (p + 1)]
        part = dot(jnp.concatenate(even + odd, axis=0), weight).astype(BF)
        for s in range(2):
            for k in range(5):
                lat[k, TREE * (2 * p + s) : TREE * (2 * p + s + 1)] = part[TREE * (5 * s + k) : TREE * (5 * s + k + 1)]

    for k in range(4):
        block = got.at[k]
        query = lat[k]
        rope = rope_rows(lambda i: block[QUERY_AT + TREE * i : QUERY_AT + TREE * (i + 1)])
        length = block[TREE_AT + 3 * TREE : TREE_AT + 3 * TREE + 1, 32:33].astype(F32)
        first, keys = cached(query, rope, block, 0, length)
        second, tree = treed(query, rope, block, TREE_AT)
        top = jnp.maximum(jnp.max(first, axis=-1, keepdims=True), jnp.max(second, axis=-1, keepdims=True))
        first, second = jnp.exp(first - top), jnp.exp(second - top)
        total = jnp.sum(first, axis=-1, keepdims=True) + jnp.sum(second, axis=-1, keepdims=True)
        acc = dot_t(first.astype(BF), keys) + dot(second.astype(BF), tree)
        lat[k] = (acc / total).astype(BF)

    query = lat[4]
    rope = rope_rows(lambda i: query_l[TREE * i : TREE * (i + 1)])
    second, tree = treed(query, rope, tree_l, 0)
    scored = []
    for k in range(4):
        block = got.at[k]
        length = block[TREE_AT + 3 * TREE : TREE_AT + 3 * TREE + 1, 33:34].astype(F32)
        scored.append(cached(query, rope, block, LONG_AT, length))
    top = jnp.max(second, axis=-1, keepdims=True)
    for scores, _ in scored:
        top = jnp.maximum(top, jnp.max(scores, axis=-1, keepdims=True))
    second = jnp.exp(second - top)
    total = jnp.sum(second, axis=-1, keepdims=True)
    acc = dot(second.astype(BF), tree)
    for scores, keys in scored:
        weights = jnp.exp(scores - top)
        total += jnp.sum(weights, axis=-1, keepdims=True)
        acc += dot_t(weights.astype(BF), keys)
    lat[4] = (acc / total).astype(BF)
    column = top + jnp.log(total)
    logs = jnp.zeros((TREE, 128), F32)
    for h in range(SLICE):
        logs = jnp.where(lanes == h, column[TREE * h : TREE * (h + 1)], logs)

    for p in range(SLICE // 2):
        pair = []
        for h in (2 * p, 2 * p + 1):
            rows = jnp.concatenate([lat[k, TREE * h : TREE * (h + 1)] for k in range(5)], axis=0)
            weight = kv[...][:, :, :, KVR:].reshape(SPAN, KVR)[VDIM * h : VDIM * (h + 1)]
            pair.append(dot_t(rows, weight))
        heads = jnp.concatenate(pair, axis=1).astype(BF)
        for d in range(4):
            out[d, 5 * TREE * p : 5 * TREE * (p + 1)] = heads
    base = 5 * TREE * (SLICE // 2)
    for i, part in enumerate(split3(logs)):
        for d in range(4):
            out[d, base + TREE * i : base + TREE * (i + 1)] = part


def project_kernel(got, weight, send, rows):
    base = 5 * TREE * (SLICE // 2)
    logs = sum(got[:, base + TREE * i : base + TREE * (i + 1)].astype(F32) for i in range(3))
    share = jnp.exp(logs - jnp.max(logs, axis=0)[None])
    share = (share / jnp.sum(share, axis=0)[None]).reshape(4 * TREE, 128)
    high = share.astype(BF)
    low = (share - high.astype(F32)).astype(BF)
    for p in range(SLICE // 2):
        at = 5 * TREE * p
        cols = slice(128 * p, 128 * (p + 1))
        for y in range(4):
            rows[4 * TREE * y : 4 * TREE * (y + 1), cols] = got[y, at : at + 4 * TREE]
        owner = lax.broadcasted_iota(jnp.int32, (128, 128), 1) // VDIM + 2 * p
        select = jnp.where(lax.broadcasted_iota(jnp.int32, (128, 128), 0) == owner, 1.0, 0.0).astype(BF)
        wide = (dot(high, select) + dot(low, select)).reshape(4, TREE, 128)
        piece = got[:, at + 4 * TREE : at + 5 * TREE].astype(F32) * wide
        rows[16 * TREE : 17 * TREE, cols] = jnp.sum(piece, axis=0).astype(BF)
    rest = dot(rows[...], weight[:, :, 4].reshape(SPAN, 128))
    lanes = lax.broadcasted_iota(jnp.int32, (QUARTER, 128), 1) // 32
    for k in range(4):
        send[k, :TOKENS] = dot(rows[...], weight[:, :, k].reshape(SPAN, 128)).astype(BF)
        packed = jnp.zeros((QUARTER, 128), F32)
        for g in range(4):
            part = rest[QUARTER * g : QUARTER * (g + 1)]
            shift = (32 * (g - k)) % 128
            part = pltpu.roll(part, shift, 1) if shift else part
            packed = jnp.where(lanes == g, part, packed)
        send[k, TOKENS : TOKENS + QUARTER] = packed.astype(BF)
        send[k, TOKENS + QUARTER :] = jnp.zeros((send.shape[1] - TOKENS - QUARTER, 128), BF)


def finish_kernel(got, residual, long_residual, hidden, long_hidden, tail):
    rest = jnp.sum(got[:, TOKENS : TOKENS + QUARTER].astype(F32), axis=0)
    for g in range(4):
        tail[QUARTER * g : QUARTER * (g + 1)] = pltpu.roll(rest, (-32 * g) % 128, 1) if g else rest
    for i in range(17):
        at = slice(TREE * i, TREE * (i + 1))
        main = jnp.sum(got[:, at].astype(F32), axis=0)
        source, target, k = (residual, hidden, i) if i < 16 else (long_residual, long_hidden, 0)
        target[k, :, :128] = (source[k, :, :128].astype(F32) + main).astype(BF)
        target[k, :, 128:160] = (source[k, :, 128:160].astype(F32) + tail[at, :32]).astype(BF)


SMEM = pl.BlockSpec(memory_space=pltpu.SMEM)
VMEM = pl.BlockSpec(memory_space=pltpu.VMEM)
HBM = pl.BlockSpec(memory_space=pltpu.HBM)
COST = pl.CostEstimate(flops=6 * 10**9, transcendentals=10**6, bytes_accessed=18 * 10**6)
PARAMS = pltpu.CompilerParams(vmem_limit_bytes=48 << 20)


def onehot(rows, cols, match):
    row = lax.broadcasted_iota(jnp.int32, (rows, cols), 0)
    col = lax.broadcasted_iota(jnp.int32, (rows, cols), 1)
    return jnp.where(match(row, col), 1.0, 0.0).astype(BF)


def pack_kernel(place, length, length_l, *refs):
    sources, (block, own_q, own_tree), held, (slices, sems) = refs[:8], refs[8:11], refs[11:19], refs[19:]
    copies = [pltpu.make_async_copy(sources[i], held[i], sems.at[i]) for i in range(8)]
    for copy in copies:
        copy.start()
    parents, parents_l, queries, queries_l, keys, keys_l, tree, tree_l = held
    lanes = lax.broadcasted_iota(jnp.int32, (TREE, 128), 1)
    tile4 = onehot(TREE, 128, lambda row, col: col % 32 == row)
    widen = onehot(TREE, 128, lambda row, col: col == row)
    above = lax.broadcasted_iota(jnp.int32, (TREE, TREE), 0)
    same = above == lax.broadcasted_iota(jnp.int32, (TREE, TREE), 1)
    extras = []
    for copy in copies[:2]:
        copy.wait()
    for i, ids in enumerate((parents, parents_l)):
        reach = jnp.where(same | (above == ids[...]), 1.0, 0.0).astype(BF)
        for _ in range((TREE - 1).bit_length()):
            reach = jnp.minimum(dot(reach, reach), 1.0).astype(BF)
        extra = lax.dot_general(reach, widen, (((0,), (0,)), ((), ())), preferred_element_type=F32)
        if i == 1:
            extra = jnp.where(place[1] == 0, extra, 0.0)
        extra = jnp.where(lanes == 32, length[0, 0].astype(F32), extra)
        extras.append(jnp.where(lanes == 33, length_l[0, 0].astype(F32), extra).astype(BF))
    for copy in copies[2:]:
        copy.wait()
    for d in range(4):
        block[d, 0:288] = keys[:, :128]
        block[d, 288:576] = keys[:, 128:]
        block[d, 576:864] = keys_l[:, :128]
        block[d, 864:1152] = keys_l[:, 128:]
    for i, rows in enumerate((tree, tree_l)):
        parts = (rows[:, :128], rows[:, 128:KVR], dot(rows[:, KVR:], tile4).astype(BF), extras[i])
        for k, part in enumerate(parts):
            at = slice(TREE * k, TREE * (k + 1))
            if i == 0:
                for d in range(4):
                    block[d, TREE_AT + at.start : TREE_AT + at.stop] = part
            else:
                own_tree[at] = part

    def source(col):
        nope = 96 * (col // NOPE) + col % NOPE
        rope = 96 * ((col - 256) // ROPE) + NOPE + (col - 256) % ROPE
        return jnp.where(col < 256, nope, rope)

    sort = onehot(384, 384, lambda row, col: source(col) == row)
    rope = []
    for w in range(HEADS // 4):
        cols = slice(384 * w, 384 * (w + 1))
        moved = dot(jnp.concatenate([queries[:, cols], queries_l[:, cols]], axis=0), sort)
        rope.append(moved[:, 256:])
        for half in range(2):
            s, p = divmod(2 * w + half, SLICE // 2)
            part = moved[:, 128 * half : 128 * (half + 1)].astype(BF)
            block[s, QUERY_AT + TREE * p : QUERY_AT + TREE * (p + 1)] = part[:TREE]
            slices[s, TREE * p : TREE * (p + 1)] = part[TREE:]
    wide = lax.broadcasted_iota(jnp.int32, (2 * TREE, 128), 1)
    for s in range(4):
        first = SLICE * s // 4
        for k in range(3):
            if s % 2 == 0:
                part = rope[first + k]
            else:
                after = pltpu.roll(rope[first + k + 1], 64, 1) if k < 2 else jnp.zeros((2 * TREE, 128), F32)
                part = jnp.where(wide < 64, pltpu.roll(rope[first + k], 64, 1), after)
            part = part.astype(BF)
            at = TREE * (5 + k)
            block[s, QUERY_AT + at : QUERY_AT + at + TREE] = part[:TREE]
            slices[s, at : at + TREE] = part[TREE:]
    own_q[...] = slices[place[0]]


def on_device(
    queries, tree_latent, parents, cache, cache_lengths, accepted, residual,
    long_queries, long_tree_latent, long_parents, long_cache, long_plan, long_residual,
    key_up, value_up, out_weight,
):
    y, x = lax.axis_index("y"), lax.axis_index("x")
    place = jnp.stack([x, y]).astype(jnp.int32)
    pairs = [(r * 16 + z, ((z % 4) * 4 + z // 4) * 16 + (z + r) % 16) for r in range(16) for z in range(16)]
    kv, place = lax.optimization_barrier((jnp.concatenate([key_up, value_up], axis=1), place))
    kv = lax.ppermute(kv, ("y", "x", "a", "b"), pairs)
    rows = 8 * TREE
    block, query_l, tree_l = pl.pallas_call(
        pack_kernel,
        out_shape=(
            jax.ShapeDtypeStruct((4, BLOCK, 128), BF),
            jax.ShapeDtypeStruct((rows, 128), BF),
            jax.ShapeDtypeStruct((4 * TREE, 128), BF),
        ),
        in_specs=[SMEM] * 3 + [HBM] * 8,
        out_specs=(VMEM, VMEM, VMEM),
        scratch_shapes=[pltpu.VMEM((1, TREE), jnp.int32)] * 2
        + [pltpu.VMEM((TREE, HEADS * (NOPE + ROPE)), BF)] * 2
        + [pltpu.VMEM((KVR + ROPE, 256), BF)] * 2
        + [pltpu.VMEM((TREE, KVR + ROPE), BF)] * 2
        + [pltpu.VMEM((4, rows, 128), BF), pltpu.SemaphoreType.DMA((8,))],
        compiler_params=PARAMS,
        cost_estimate=COST,
    )(
        place, cache_lengths, long_plan,
        *[
            pltpu.with_memory_space_constraint(value, pltpu.HBM)
            for value in (
                parents[0], long_parents, queries[0], long_queries[0], cache[0, 0].T, long_cache[0].T,
                tree_latent[0], long_tree_latent[0],
            )
        ],
    )
    block, out_weight = lax.optimization_barrier((block, out_weight))
    cols = lax.all_gather(out_weight, "x")
    out_rows = jnp.stack([cols[k, :, :128] for k in range(4)] + [jnp.concatenate([cols[k, :, 128:] for k in range(4)], axis=1)])
    kv, out_rows = lax.optimization_barrier((kv, out_rows))
    got = lax.all_to_all(block, "x", 0, 0)
    out_rows = lax.ppermute(out_rows, ("x", "a"), [(4 * i + j, 4 * j + i) for i in range(4) for j in range(4)])
    kv = lax.all_gather(kv, ("y", "c"))
    kv, out_rows = lax.optimization_barrier((kv, out_rows))
    kv = kv.reshape((4, 2) + kv.shape[1:])

    heads = pl.pallas_call(
        attend_kernel,
        out_shape=jax.ShapeDtypeStruct((4, 5 * TREE * (SLICE // 2) + 3 * TREE, 128), BF),
        in_specs=[VMEM] * 4,
        out_specs=VMEM,
        scratch_shapes=[pltpu.VMEM((5, SLICE * TREE, KVR), BF)],
        compiler_params=PARAMS,
        cost_estimate=COST,
    )(got, query_l, tree_l, kv)
    shared = lax.all_to_all(heads, "y", 0, 0)
    out_rows = lax.all_gather(out_rows, ("b", "c"))
    out_rows = out_rows.reshape((4, 2) + out_rows.shape[1:])
    send = pl.pallas_call(
        project_kernel,
        out_shape=jax.ShapeDtypeStruct((4, 688, 128), BF),
        in_specs=[VMEM, VMEM],
        out_specs=VMEM,
        scratch_shapes=[pltpu.VMEM((TOKENS, SPAN), BF)],
        compiler_params=PARAMS,
    )(shared, out_rows)
    back = lax.all_to_all(send, "x", 0, 0)
    hidden, long_hidden = pl.pallas_call(
        finish_kernel,
        out_shape=(
            jax.ShapeDtypeStruct(residual.shape, BF),
            jax.ShapeDtypeStruct(long_residual.shape, BF),
        ),
        in_specs=[VMEM, VMEM, VMEM],
        out_specs=(VMEM, VMEM),
        scratch_shapes=[pltpu.VMEM((TOKENS, 128), F32)],
        compiler_params=PARAMS,
    )(back, residual, long_residual)
    accepted_cache = jnp.take_along_axis(tree_latent[0], accepted[0, 0][:, None], axis=0)[None, None]
    return hidden, accepted_cache, long_hidden


def solution(mesh):
    split = Mesh(mesh.devices.reshape(4, 4, 4, 4, 2), ("y", "x", "a", "b", "c"))
    return jax.shard_map(
        on_device,
        mesh=split,
        in_specs=(
            P(ROWS, COLS, None),
            P(ROWS, COLS, None),
            P(ROWS, COLS, None),
            P(ROWS, COLS, None, None),
            P(ROWS, COLS),
            P(ROWS, COLS, None),
            P(None, COLS, ROWS),
            P(COLS, None, None),
            P(COLS, None, None),
            P(COLS, None),
            P(COLS, ROWS, None),
            P(COLS, ROWS),
            P(COLS, None, ROWS),
            P(COLS, None),
            P(COLS, None),
            P(COLS, ROWS),
        ),
        out_specs=(P(None, COLS, ROWS), P(ROWS, COLS, None, None), P(COLS, None, ROWS)),
        check_vma=False,
    )
```

```python
import jax
import jax.numpy as jnp
from jax import lax
from jax.experimental import pallas as pl
from jax.experimental.pallas import tpu as pltpu
from jax.sharding import Mesh, PartitionSpec as P

HEADS = 40
NOPE = 64
ROPE = 32
VDIM = 64
KVR = 256
TREE = 32
ROWS = ("y", "x")
COLS = ("a", "b", "c")
BF = jnp.bfloat16
F32 = jnp.float32


OVER_LAST = (((1,), (1,)), ((), ()))
SLICE = HEADS // 4
SPAN = SLICE * VDIM
LONG_AT, TREE_AT, QUERY_AT, BLOCK = 576, 1152, 1280, 1536
TOKENS = 16 * TREE + TREE
QUARTER = TOKENS // 4


def split3(value):
    high = value.astype(BF)
    rest = value - high.astype(F32)
    mid = rest.astype(BF)
    return high, mid, (rest - mid.astype(F32)).astype(BF)


def dot(left, right):
    return jnp.dot(left, right, preferred_element_type=F32)


def dot_t(left, right):
    return lax.dot_general(left, right, OVER_LAST, preferred_element_type=F32)


def attend_kernel(got, query_l, tree_l, kv, out, lat):
    lanes = lax.broadcasted_iota(jnp.int32, (TREE, 128), 1)
    slots = lax.broadcasted_iota(jnp.int32, (1, 256), 1).astype(F32)
    scale = (NOPE + ROPE) ** -0.5
    size = SLICE * TREE

    def rope_rows(chunk):
        zero = jnp.zeros((TREE, 128), BF)
        return jnp.concatenate([jnp.where(lanes // 32 == h % 4, chunk(5 + h // 4), zero) for h in range(SLICE)], axis=0)

    def cached(query, rope, block, at, length):
        keys = jnp.concatenate([block[at : at + 288], block[at + 288 : at + 576]], axis=1)
        scores = dot(query, keys[:KVR]) + dot(rope, jnp.concatenate([keys[KVR:]] * 4, axis=0))
        return jnp.where(slots < length, scores * scale, -jnp.inf), keys[:KVR]

    def treed(query, rope, block, at):
        keys = jnp.concatenate([block[at : at + TREE], block[at + TREE : at + 2 * TREE]], axis=1)
        scores = dot_t(query, keys) + dot_t(rope, block[at + 2 * TREE : at + 3 * TREE])
        reach = block[at + 3 * TREE : at + 4 * TREE, :TREE].astype(F32)
        reach = jnp.concatenate([reach] * SLICE, axis=0)
        return jnp.where(reach > 0.5, scores * scale, -jnp.inf), keys

    for p in range(SLICE // 2):
        at = TREE * p
        rows = [got[k, QUERY_AT + at : QUERY_AT + at + TREE] for k in range(4)] + [query_l[at : at + TREE]]
        even = [jnp.where(lanes < NOPE, row, jnp.zeros_like(row)) for row in rows]
        odd = [jnp.where(lanes < NOPE, jnp.zeros_like(row), row) for row in rows]
        weight = kv[...][:, :, :, :KVR].reshape(SPAN, KVR)[128 * p : 128 * (p + 1)]
        part = dot(jnp.concatenate(even + odd, axis=0), weight).astype(BF)
        for s in range(2):
            for k in range(5):
                lat[k, TREE * (2 * p + s) : TREE * (2 * p + s + 1)] = part[TREE * (5 * s + k) : TREE * (5 * s + k + 1)]

    for k in range(4):
        block = got.at[k]
        query = lat[k]
        rope = rope_rows(lambda i: block[QUERY_AT + TREE * i : QUERY_AT + TREE * (i + 1)])
        length = block[TREE_AT + 3 * TREE : TREE_AT + 3 * TREE + 1, 32:33].astype(F32)
        first, keys = cached(query, rope, block, 0, length)
        second, tree = treed(query, rope, block, TREE_AT)
        top = jnp.maximum(jnp.max(first, axis=-1, keepdims=True), jnp.max(second, axis=-1, keepdims=True))
        first, second = jnp.exp(first - top), jnp.exp(second - top)
        total = jnp.sum(first, axis=-1, keepdims=True) + jnp.sum(second, axis=-1, keepdims=True)
        acc = dot_t(first.astype(BF), keys) + dot(second.astype(BF), tree)
        lat[k] = (acc / total).astype(BF)

    query = lat[4]
    rope = rope_rows(lambda i: query_l[TREE * i : TREE * (i + 1)])
    second, tree = treed(query, rope, tree_l, 0)
    scored = []
    for k in range(4):
        block = got.at[k]
        length = block[TREE_AT + 3 * TREE : TREE_AT + 3 * TREE + 1, 33:34].astype(F32)
        scored.append(cached(query, rope, block, LONG_AT, length))
    top = jnp.max(second, axis=-1, keepdims=True)
    for scores, _ in scored:
        top = jnp.maximum(top, jnp.max(scores, axis=-1, keepdims=True))
    second = jnp.exp(second - top)
    total = jnp.sum(second, axis=-1, keepdims=True)
    acc = dot(second.astype(BF), tree)
    for scores, keys in scored:
        weights = jnp.exp(scores - top)
        total += jnp.sum(weights, axis=-1, keepdims=True)
        acc += dot_t(weights.astype(BF), keys)
    lat[4] = (acc / total).astype(BF)
    column = top + jnp.log(total)
    logs = jnp.zeros((TREE, 128), F32)
    for h in range(SLICE):
        logs = jnp.where(lanes == h, column[TREE * h : TREE * (h + 1)], logs)

    for p in range(SLICE // 2):
        pair = []
        for h in (2 * p, 2 * p + 1):
            rows = jnp.concatenate([lat[k, TREE * h : TREE * (h + 1)] for k in range(5)], axis=0)
            weight = kv[...][:, :, :, KVR:].reshape(SPAN, KVR)[VDIM * h : VDIM * (h + 1)]
            pair.append(dot_t(rows, weight))
        heads = jnp.concatenate(pair, axis=1).astype(BF)
        for d in range(4):
            out[d, 5 * TREE * p : 5 * TREE * (p + 1)] = heads
    base = 5 * TREE * (SLICE // 2)
    for i, part in enumerate(split3(logs)):
        for d in range(4):
            out[d, base + TREE * i : base + TREE * (i + 1)] = part


def project_kernel(got, weight, send, rows):
    base = 5 * TREE * (SLICE // 2)
    logs = sum(got[:, base + TREE * i : base + TREE * (i + 1)].astype(F32) for i in range(3))
    share = jnp.exp(logs - jnp.max(logs, axis=0)[None])
    share = (share / jnp.sum(share, axis=0)[None]).reshape(4 * TREE, 128)
    high = share.astype(BF)
    low = (share - high.astype(F32)).astype(BF)
    for p in range(SLICE // 2):
        at = 5 * TREE * p
        cols = slice(128 * p, 128 * (p + 1))
        for y in range(4):
            rows[4 * TREE * y : 4 * TREE * (y + 1), cols] = got[y, at : at + 4 * TREE]
        owner = lax.broadcasted_iota(jnp.int32, (128, 128), 1) // VDIM + 2 * p
        select = jnp.where(lax.broadcasted_iota(jnp.int32, (128, 128), 0) == owner, 1.0, 0.0).astype(BF)
        wide = (dot(high, select) + dot(low, select)).reshape(4, TREE, 128)
        piece = got[:, at + 4 * TREE : at + 5 * TREE].astype(F32) * wide
        rows[16 * TREE : 17 * TREE, cols] = jnp.sum(piece, axis=0).astype(BF)
    rest = dot(rows[...], weight[:, :, 4].reshape(SPAN, 128))
    lanes = lax.broadcasted_iota(jnp.int32, (QUARTER, 128), 1) // 32
    for k in range(4):
        send[k, :TOKENS] = dot(rows[...], weight[:, :, k].reshape(SPAN, 128)).astype(BF)
        packed = jnp.zeros((QUARTER, 128), F32)
        for g in range(4):
            part = rest[QUARTER * g : QUARTER * (g + 1)]
            shift = (32 * (g - k)) % 128
            part = pltpu.roll(part, shift, 1) if shift else part
            packed = jnp.where(lanes == g, part, packed)
        send[k, TOKENS : TOKENS + QUARTER] = packed.astype(BF)
        send[k, TOKENS + QUARTER :] = jnp.zeros((send.shape[1] - TOKENS - QUARTER, 128), BF)


def finish_kernel(got, residual, long_residual, hidden, long_hidden, tail):
    rest = jnp.sum(got[:, TOKENS : TOKENS + QUARTER].astype(F32), axis=0)
    for g in range(4):
        tail[QUARTER * g : QUARTER * (g + 1)] = pltpu.roll(rest, (-32 * g) % 128, 1) if g else rest
    for i in range(17):
        at = slice(TREE * i, TREE * (i + 1))
        main = jnp.sum(got[:, at].astype(F32), axis=0)
        source, target, k = (residual, hidden, i) if i < 16 else (long_residual, long_hidden, 0)
        target[k, :, :128] = (source[k, :, :128].astype(F32) + main).astype(BF)
        target[k, :, 128:160] = (source[k, :, 128:160].astype(F32) + tail[at, :32]).astype(BF)


SMEM = pl.BlockSpec(memory_space=pltpu.SMEM)
VMEM = pl.BlockSpec(memory_space=pltpu.VMEM)
HBM = pl.BlockSpec(memory_space=pltpu.HBM)
COST = pl.CostEstimate(flops=6 * 10**9, transcendentals=10**6, bytes_accessed=18 * 10**6)
PARAMS = pltpu.CompilerParams(vmem_limit_bytes=48 << 20)


def onehot(rows, cols, match):
    row = lax.broadcasted_iota(jnp.int32, (rows, cols), 0)
    col = lax.broadcasted_iota(jnp.int32, (rows, cols), 1)
    return jnp.where(match(row, col), 1.0, 0.0).astype(BF)


def pack_kernel(place, length, length_l, *refs):
    sources, (block, own_q, own_tree), held, (slices, sems) = refs[:8], refs[8:11], refs[11:19], refs[19:]
    copies = [pltpu.make_async_copy(sources[i], held[i], sems.at[i]) for i in range(8)]
    for copy in copies:
        copy.start()
    parents, parents_l, queries, queries_l, keys, keys_l, tree, tree_l = held
    lanes = lax.broadcasted_iota(jnp.int32, (TREE, 128), 1)
    tile4 = onehot(TREE, 128, lambda row, col: col % 32 == row)
    widen = onehot(TREE, 128, lambda row, col: col == row)
    above = lax.broadcasted_iota(jnp.int32, (TREE, TREE), 0)
    same = above == lax.broadcasted_iota(jnp.int32, (TREE, TREE), 1)
    extras = []
    for copy in copies:
        copy.wait()
    for i, ids in enumerate((parents, parents_l)):
        reach = jnp.where(same | (above == ids[...]), 1.0, 0.0).astype(BF)
        for _ in range((TREE - 1).bit_length()):
            reach = jnp.minimum(dot(reach, reach), 1.0).astype(BF)
        extra = lax.dot_general(reach, widen, (((0,), (0,)), ((), ())), preferred_element_type=F32)
        if i == 1:
            extra = jnp.where(place[1] == 0, extra, 0.0)
        extra = jnp.where(lanes == 32, length[0, 0].astype(F32), extra)
        extras.append(jnp.where(lanes == 33, length_l[0, 0].astype(F32), extra).astype(BF))
    for d in range(4):
        block[d, 0:288] = keys[:, :128]
        block[d, 288:576] = keys[:, 128:]
        block[d, 576:864] = keys_l[:, :128]
        block[d, 864:1152] = keys_l[:, 128:]
    for i, rows in enumerate((tree, tree_l)):
        parts = (rows[:, :128], rows[:, 128:KVR], dot(rows[:, KVR:], tile4).astype(BF), extras[i])
        for k, part in enumerate(parts):
            at = slice(TREE * k, TREE * (k + 1))
            if i == 0:
                for d in range(4):
                    block[d, TREE_AT + at.start : TREE_AT + at.stop] = part
            else:
                own_tree[at] = part

    def source(col):
        nope = 96 * (col // NOPE) + col % NOPE
        rope = 96 * ((col - 256) // ROPE) + NOPE + (col - 256) % ROPE
        return jnp.where(col < 256, nope, rope)

    sort = onehot(384, 384, lambda row, col: source(col) == row)
    rope = []
    for w in range(HEADS // 4):
        cols = slice(384 * w, 384 * (w + 1))
        moved = dot(jnp.concatenate([queries[:, cols], queries_l[:, cols]], axis=0), sort)
        rope.append(moved[:, 256:])
        for half in range(2):
            s, p = divmod(2 * w + half, SLICE // 2)
            part = moved[:, 128 * half : 128 * (half + 1)].astype(BF)
            block[s, QUERY_AT + TREE * p : QUERY_AT + TREE * (p + 1)] = part[:TREE]
            slices[s, TREE * p : TREE * (p + 1)] = part[TREE:]
    wide = lax.broadcasted_iota(jnp.int32, (2 * TREE, 128), 1)
    for s in range(4):
        first = SLICE * s // 4
        for k in range(3):
            if s % 2 == 0:
                part = rope[first + k]
            else:
                after = pltpu.roll(rope[first + k + 1], 64, 1) if k < 2 else jnp.zeros((2 * TREE, 128), F32)
                part = jnp.where(wide < 64, pltpu.roll(rope[first + k], 64, 1), after)
            part = part.astype(BF)
            at = TREE * (5 + k)
            block[s, QUERY_AT + at : QUERY_AT + at + TREE] = part[:TREE]
            slices[s, at : at + TREE] = part[TREE:]
    own_q[...] = slices[place[0]]


def on_device(
    queries, tree_latent, parents, cache, cache_lengths, accepted, residual,
    long_queries, long_tree_latent, long_parents, long_cache, long_plan, long_residual,
    key_up, value_up, out_weight,
):
    y, x = lax.axis_index("y"), lax.axis_index("x")
    place = jnp.stack([x, y]).astype(jnp.int32)
    pairs = [(r * 16 + z, ((z % 4) * 4 + z // 4) * 16 + (z + r) % 16) for r in range(16) for z in range(16)]
    kv, place = lax.optimization_barrier((jnp.concatenate([key_up, value_up], axis=1), place))
    kv = lax.ppermute(kv, ("y", "x", "a", "b"), pairs)
    rows = 8 * TREE
    block, query_l, tree_l = pl.pallas_call(
        pack_kernel,
        out_shape=(
            jax.ShapeDtypeStruct((4, BLOCK, 128), BF),
            jax.ShapeDtypeStruct((rows, 128), BF),
            jax.ShapeDtypeStruct((4 * TREE, 128), BF),
        ),
        in_specs=[SMEM] * 3 + [HBM] * 8,
        out_specs=(VMEM, VMEM, VMEM),
        scratch_shapes=[pltpu.VMEM((1, TREE), jnp.int32)] * 2
        + [pltpu.VMEM((TREE, HEADS * (NOPE + ROPE)), BF)] * 2
        + [pltpu.VMEM((KVR + ROPE, 256), BF)] * 2
        + [pltpu.VMEM((TREE, KVR + ROPE), BF)] * 2
        + [pltpu.VMEM((4, rows, 128), BF), pltpu.SemaphoreType.DMA((8,))],
        compiler_params=PARAMS,
        cost_estimate=COST,
    )(
        place, cache_lengths, long_plan,
        *[
            pltpu.with_memory_space_constraint(value, pltpu.HBM)
            for value in (
                parents[0], long_parents, queries[0], long_queries[0], cache[0, 0].T, long_cache[0].T,
                tree_latent[0], long_tree_latent[0],
            )
        ],
    )
    cols = lax.all_gather(out_weight, "x")
    out_rows = jnp.stack([cols[k, :, :128] for k in range(4)] + [jnp.concatenate([cols[k, :, 128:] for k in range(4)], axis=1)])
    block, kv, out_rows = lax.optimization_barrier((block, kv, out_rows))
    got = lax.all_to_all(block, "x", 0, 0)
    out_rows = lax.ppermute(out_rows, ("x", "a"), [(4 * i + j, 4 * j + i) for i in range(4) for j in range(4)])
    kv = lax.all_gather(kv, ("y", "c"))
    kv, out_rows = lax.optimization_barrier((kv, out_rows))
    kv = kv.reshape((4, 2) + kv.shape[1:])

    heads = pl.pallas_call(
        attend_kernel,
        out_shape=jax.ShapeDtypeStruct((4, 5 * TREE * (SLICE // 2) + 3 * TREE, 128), BF),
        in_specs=[VMEM] * 4,
        out_specs=VMEM,
        scratch_shapes=[pltpu.VMEM((5, SLICE * TREE, KVR), BF)],
        compiler_params=PARAMS,
        cost_estimate=COST,
    )(got, query_l, tree_l, kv)
    shared = lax.all_to_all(heads, "y", 0, 0)
    out_rows = lax.all_gather(out_rows, ("b", "c"))
    out_rows = out_rows.reshape((4, 2) + out_rows.shape[1:])
    send = pl.pallas_call(
        project_kernel,
        out_shape=jax.ShapeDtypeStruct((4, 688, 128), BF),
        in_specs=[VMEM, VMEM],
        out_specs=VMEM,
        scratch_shapes=[pltpu.VMEM((TOKENS, SPAN), BF)],
        compiler_params=PARAMS,
    )(shared, out_rows)
    back = lax.all_to_all(send, "x", 0, 0)
    hidden, long_hidden = pl.pallas_call(
        finish_kernel,
        out_shape=(
            jax.ShapeDtypeStruct(residual.shape, BF),
            jax.ShapeDtypeStruct(long_residual.shape, BF),
        ),
        in_specs=[VMEM, VMEM, VMEM],
        out_specs=(VMEM, VMEM),
        scratch_shapes=[pltpu.VMEM((TOKENS, 128), F32)],
        compiler_params=PARAMS,
    )(back, residual, long_residual)
    accepted_cache = jnp.take_along_axis(tree_latent[0], accepted[0, 0][:, None], axis=0)[None, None]
    return hidden, accepted_cache, long_hidden


def solution(mesh):
    split = Mesh(mesh.devices.reshape(4, 4, 4, 4, 2), ("y", "x", "a", "b", "c"))
    return jax.shard_map(
        on_device,
        mesh=split,
        in_specs=(
            P(ROWS, COLS, None),
            P(ROWS, COLS, None),
            P(ROWS, COLS, None),
            P(ROWS, COLS, None, None),
            P(ROWS, COLS),
            P(ROWS, COLS, None),
            P(None, COLS, ROWS),
            P(COLS, None, None),
            P(COLS, None, None),
            P(COLS, None),
            P(COLS, ROWS, None),
            P(COLS, ROWS),
            P(COLS, None, ROWS),
            P(COLS, None),
            P(COLS, None),
            P(COLS, ROWS),
        ),
        out_specs=(P(None, COLS, ROWS), P(ROWS, COLS, None, None), P(COLS, None, ROWS)),
        check_vma=False,
    )
```

```python
import jax
import jax.numpy as jnp
from jax import lax
from jax.experimental import pallas as pl
from jax.experimental.pallas import tpu as pltpu
from jax.sharding import Mesh, PartitionSpec as P

HEADS = 40
NOPE = 64
ROPE = 32
VDIM = 64
KVR = 256
TREE = 32
ROWS = ("y", "x")
COLS = ("a", "b", "c")
BF = jnp.bfloat16
F32 = jnp.float32


OVER_LAST = (((1,), (1,)), ((), ()))
SLICE = HEADS // 4
SPAN = SLICE * VDIM
LONG_AT, TREE_AT, QUERY_AT, BLOCK = 576, 1152, 1280, 1536
TOKENS = 16 * TREE + TREE
QUARTER = TOKENS // 4


def split3(value):
    high = value.astype(BF)
    rest = value - high.astype(F32)
    mid = rest.astype(BF)
    return high, mid, (rest - mid.astype(F32)).astype(BF)


def dot(left, right):
    return jnp.dot(left, right, preferred_element_type=F32)


def dot_t(left, right):
    return lax.dot_general(left, right, OVER_LAST, preferred_element_type=F32)


def attend_kernel(got, query_l, tree_l, kv, out, lat):
    lanes = lax.broadcasted_iota(jnp.int32, (TREE, 128), 1)
    slots = lax.broadcasted_iota(jnp.int32, (1, 256), 1).astype(F32)
    scale = (NOPE + ROPE) ** -0.5
    size = SLICE * TREE

    def rope_rows(chunk):
        zero = jnp.zeros((TREE, 128), BF)
        return jnp.concatenate([jnp.where(lanes // 32 == h % 4, chunk(5 + h // 4), zero) for h in range(SLICE)], axis=0)

    def cached(query, rope, block, at, length):
        keys = jnp.concatenate([block[at : at + 288], block[at + 288 : at + 576]], axis=1)
        scores = dot(query, keys[:KVR]) + dot(rope, jnp.concatenate([keys[KVR:]] * 4, axis=0))
        return jnp.where(slots < length, scores * scale, -jnp.inf), keys[:KVR]

    def treed(query, rope, block, at):
        keys = jnp.concatenate([block[at : at + TREE], block[at + TREE : at + 2 * TREE]], axis=1)
        scores = dot_t(query, keys) + dot_t(rope, block[at + 2 * TREE : at + 3 * TREE])
        reach = block[at + 3 * TREE : at + 4 * TREE, :TREE].astype(F32)
        reach = jnp.concatenate([reach] * SLICE, axis=0)
        return jnp.where(reach > 0.5, scores * scale, -jnp.inf), keys

    for p in range(SLICE // 2):
        at = TREE * p
        rows = [got[k, QUERY_AT + at : QUERY_AT + at + TREE] for k in range(4)] + [query_l[at : at + TREE]]
        even = [jnp.where(lanes < NOPE, row, jnp.zeros_like(row)) for row in rows]
        odd = [jnp.where(lanes < NOPE, jnp.zeros_like(row), row) for row in rows]
        weight = kv[...][:, :, :, :KVR].reshape(SPAN, KVR)[128 * p : 128 * (p + 1)]
        part = dot(jnp.concatenate(even + odd, axis=0), weight).astype(BF)
        for s in range(2):
            for k in range(5):
                lat[k, TREE * (2 * p + s) : TREE * (2 * p + s + 1)] = part[TREE * (5 * s + k) : TREE * (5 * s + k + 1)]

    for k in range(4):
        block = got.at[k]
        query = lat[k]
        rope = rope_rows(lambda i: block[QUERY_AT + TREE * i : QUERY_AT + TREE * (i + 1)])
        length = block[TREE_AT + 3 * TREE : TREE_AT + 3 * TREE + 1, 32:33].astype(F32)
        first, keys = cached(query, rope, block, 0, length)
        second, tree = treed(query, rope, block, TREE_AT)
        top = jnp.maximum(jnp.max(first, axis=-1, keepdims=True), jnp.max(second, axis=-1, keepdims=True))
        first, second = jnp.exp(first - top), jnp.exp(second - top)
        total = jnp.sum(first, axis=-1, keepdims=True) + jnp.sum(second, axis=-1, keepdims=True)
        acc = dot_t(first.astype(BF), keys) + dot(second.astype(BF), tree)
        lat[k] = (acc / total).astype(BF)

    query = lat[4]
    rope = rope_rows(lambda i: query_l[TREE * i : TREE * (i + 1)])
    second, tree = treed(query, rope, tree_l, 0)
    scored = []
    for k in range(4):
        block = got.at[k]
        length = block[TREE_AT + 3 * TREE : TREE_AT + 3 * TREE + 1, 33:34].astype(F32)
        scored.append(cached(query, rope, block, LONG_AT, length))
    top = jnp.max(second, axis=-1, keepdims=True)
    for scores, _ in scored:
        top = jnp.maximum(top, jnp.max(scores, axis=-1, keepdims=True))
    second = jnp.exp(second - top)
    total = jnp.sum(second, axis=-1, keepdims=True)
    acc = dot(second.astype(BF), tree)
    for scores, keys in scored:
        weights = jnp.exp(scores - top)
        total += jnp.sum(weights, axis=-1, keepdims=True)
        acc += dot_t(weights.astype(BF), keys)
    lat[4] = (acc / total).astype(BF)
    column = top + jnp.log(total)
    logs = jnp.zeros((TREE, 128), F32)
    for h in range(SLICE):
        logs = jnp.where(lanes == h, column[TREE * h : TREE * (h + 1)], logs)

    for p in range(SLICE // 2):
        pair = []
        for h in (2 * p, 2 * p + 1):
            rows = jnp.concatenate([lat[k, TREE * h : TREE * (h + 1)] for k in range(5)], axis=0)
            weight = kv[...][:, :, :, KVR:].reshape(SPAN, KVR)[VDIM * h : VDIM * (h + 1)]
            pair.append(dot_t(rows, weight))
        heads = jnp.concatenate(pair, axis=1).astype(BF)
        for d in range(4):
            out[d, 5 * TREE * p : 5 * TREE * (p + 1)] = heads
    base = 5 * TREE * (SLICE // 2)
    for i, part in enumerate(split3(logs)):
        for d in range(4):
            out[d, base + TREE * i : base + TREE * (i + 1)] = part


def project_kernel(got, weight, send, rows):
    base = 5 * TREE * (SLICE // 2)
    logs = sum(got[:, base + TREE * i : base + TREE * (i + 1)].astype(F32) for i in range(3))
    share = jnp.exp(logs - jnp.max(logs, axis=0)[None])
    share = (share / jnp.sum(share, axis=0)[None]).reshape(4 * TREE, 128)
    high = share.astype(BF)
    low = (share - high.astype(F32)).astype(BF)
    for p in range(SLICE // 2):
        at = 5 * TREE * p
        cols = slice(128 * p, 128 * (p + 1))
        for y in range(4):
            rows[4 * TREE * y : 4 * TREE * (y + 1), cols] = got[y, at : at + 4 * TREE]
        owner = lax.broadcasted_iota(jnp.int32, (128, 128), 1) // VDIM + 2 * p
        select = jnp.where(lax.broadcasted_iota(jnp.int32, (128, 128), 0) == owner, 1.0, 0.0).astype(BF)
        wide = (dot(high, select) + dot(low, select)).reshape(4, TREE, 128)
        piece = got[:, at + 4 * TREE : at + 5 * TREE].astype(F32) * wide
        rows[16 * TREE : 17 * TREE, cols] = jnp.sum(piece, axis=0).astype(BF)
    blocks = [weight[:, :, k].reshape(SPAN, 128) for k in range(5)]
    for k in (0, 2):
        both = dot(rows[...], jnp.concatenate(blocks[k : k + 2], axis=1)).astype(BF)
        send[k, :TOKENS] = both[:, :128]
        send[k + 1, :TOKENS] = both[:, 128:]
    rest = dot(rows[...], blocks[4])
    lanes = lax.broadcasted_iota(jnp.int32, (QUARTER, 128), 1) // 32
    for k in range(4):
        packed = jnp.zeros((QUARTER, 128), F32)
        for g in range(4):
            part = rest[QUARTER * g : QUARTER * (g + 1)]
            shift = (32 * (g - k)) % 128
            part = pltpu.roll(part, shift, 1) if shift else part
            packed = jnp.where(lanes == g, part, packed)
        send[k, TOKENS : TOKENS + QUARTER] = packed.astype(BF)
        send[k, TOKENS + QUARTER :] = jnp.zeros((send.shape[1] - TOKENS - QUARTER, 128), BF)


def finish_kernel(got, residual, long_residual, hidden, long_hidden, tail):
    rest = jnp.sum(got[:, TOKENS : TOKENS + QUARTER].astype(F32), axis=0)
    for g in range(4):
        tail[QUARTER * g : QUARTER * (g + 1)] = pltpu.roll(rest, (-32 * g) % 128, 1) if g else rest
    for i in range(17):
        at = slice(TREE * i, TREE * (i + 1))
        main = jnp.sum(got[:, at].astype(F32), axis=0)
        source, target, k = (residual, hidden, i) if i < 16 else (long_residual, long_hidden, 0)
        target[k, :, :128] = (source[k, :, :128].astype(F32) + main).astype(BF)
        target[k, :, 128:160] = (source[k, :, 128:160].astype(F32) + tail[at, :32]).astype(BF)


SMEM = pl.BlockSpec(memory_space=pltpu.SMEM)
VMEM = pl.BlockSpec(memory_space=pltpu.VMEM)
HBM = pl.BlockSpec(memory_space=pltpu.HBM)
COST = pl.CostEstimate(flops=6 * 10**9, transcendentals=10**6, bytes_accessed=18 * 10**6)
PARAMS = pltpu.CompilerParams(vmem_limit_bytes=48 << 20)


def onehot(rows, cols, match):
    row = lax.broadcasted_iota(jnp.int32, (rows, cols), 0)
    col = lax.broadcasted_iota(jnp.int32, (rows, cols), 1)
    return jnp.where(match(row, col), 1.0, 0.0).astype(BF)


def pack_kernel(place, length, length_l, *refs):
    sources, (block, own_q, own_tree), held, (slices, sems) = refs[:8], refs[8:11], refs[11:19], refs[19:]
    copies = [pltpu.make_async_copy(sources[i], held[i], sems.at[i]) for i in range(8)]
    for copy in copies:
        copy.start()
    parents, parents_l, queries, queries_l, keys, keys_l, tree, tree_l = held
    lanes = lax.broadcasted_iota(jnp.int32, (TREE, 128), 1)
    tile4 = onehot(TREE, 128, lambda row, col: col % 32 == row)
    widen = onehot(TREE, 128, lambda row, col: col == row)
    above = lax.broadcasted_iota(jnp.int32, (TREE, TREE), 0)
    same = above == lax.broadcasted_iota(jnp.int32, (TREE, TREE), 1)
    extras = []
    for copy in copies[:2]:
        copy.wait()
    for i, ids in enumerate((parents, parents_l)):
        reach = jnp.where(same | (above == ids[...]), 1.0, 0.0).astype(BF)
        for _ in range((TREE - 1).bit_length()):
            reach = jnp.minimum(dot(reach, reach), 1.0).astype(BF)
        extra = lax.dot_general(reach, widen, (((0,), (0,)), ((), ())), preferred_element_type=F32)
        if i == 1:
            extra = jnp.where(place[1] == 0, extra, 0.0)
        extra = jnp.where(lanes == 32, length[0, 0].astype(F32), extra)
        extras.append(jnp.where(lanes == 33, length_l[0, 0].astype(F32), extra).astype(BF))
    for copy in copies[2:]:
        copy.wait()
    for d in range(4):
        block[d, 0:288] = keys[:, :128]
        block[d, 288:576] = keys[:, 128:]
        block[d, 576:864] = keys_l[:, :128]
        block[d, 864:1152] = keys_l[:, 128:]
    for i, rows in enumerate((tree, tree_l)):
        parts = (rows[:, :128], rows[:, 128:KVR], dot(rows[:, KVR:], tile4).astype(BF), extras[i])
        for k, part in enumerate(parts):
            at = slice(TREE * k, TREE * (k + 1))
            if i == 0:
                for d in range(4):
                    block[d, TREE_AT + at.start : TREE_AT + at.stop] = part
            else:
                own_tree[at] = part

    def source(col):
        nope = 96 * (col // NOPE) + col % NOPE
        rope = 96 * ((col - 256) // ROPE) + NOPE + (col - 256) % ROPE
        return jnp.where(col < 256, nope, rope)

    sort = onehot(384, 384, lambda row, col: source(col) == row)
    windows = [slice(384 * w, 384 * (w + 1)) for w in range(HEADS // 4)]
    sorted_all = dot(jnp.concatenate([q[:, cols] for cols in windows for q in (queries, queries_l)], axis=0), sort)
    rope = []
    for w in range(HEADS // 4):
        moved = sorted_all[2 * TREE * w : 2 * TREE * (w + 1)]
        rope.append(moved[:, 256:])
        for half in range(2):
            s, p = divmod(2 * w + half, SLICE // 2)
            part = moved[:, 128 * half : 128 * (half + 1)].astype(BF)
            block[s, QUERY_AT + TREE * p : QUERY_AT + TREE * (p + 1)] = part[:TREE]
            slices[s, TREE * p : TREE * (p + 1)] = part[TREE:]
    wide = lax.broadcasted_iota(jnp.int32, (2 * TREE, 128), 1)
    for s in range(4):
        first = SLICE * s // 4
        for k in range(3):
            if s % 2 == 0:
                part = rope[first + k]
            else:
                after = pltpu.roll(rope[first + k + 1], 64, 1) if k < 2 else jnp.zeros((2 * TREE, 128), F32)
                part = jnp.where(wide < 64, pltpu.roll(rope[first + k], 64, 1), after)
            part = part.astype(BF)
            at = TREE * (5 + k)
            block[s, QUERY_AT + at : QUERY_AT + at + TREE] = part[:TREE]
            slices[s, at : at + TREE] = part[TREE:]
    own_q[...] = slices[place[0]]


def on_device(
    queries, tree_latent, parents, cache, cache_lengths, accepted, residual,
    long_queries, long_tree_latent, long_parents, long_cache, long_plan, long_residual,
    key_up, value_up, out_weight,
):
    y, x = lax.axis_index("y"), lax.axis_index("x")
    place = jnp.stack([x, y]).astype(jnp.int32)
    pairs = [(r * 16 + z, ((z % 4) * 4 + z // 4) * 16 + (z + r) % 16) for r in range(16) for z in range(16)]
    kv, place = lax.optimization_barrier((jnp.concatenate([key_up, value_up], axis=1), place))
    kv = lax.ppermute(kv, ("y", "x", "a", "b"), pairs)
    rows = 8 * TREE
    block, query_l, tree_l = pl.pallas_call(
        pack_kernel,
        out_shape=(
            jax.ShapeDtypeStruct((4, BLOCK, 128), BF),
            jax.ShapeDtypeStruct((rows, 128), BF),
            jax.ShapeDtypeStruct((4 * TREE, 128), BF),
        ),
        in_specs=[SMEM] * 3 + [HBM] * 8,
        out_specs=(VMEM, VMEM, VMEM),
        scratch_shapes=[pltpu.VMEM((1, TREE), jnp.int32)] * 2
        + [pltpu.VMEM((TREE, HEADS * (NOPE + ROPE)), BF)] * 2
        + [pltpu.VMEM((KVR + ROPE, 256), BF)] * 2
        + [pltpu.VMEM((TREE, KVR + ROPE), BF)] * 2
        + [pltpu.VMEM((4, rows, 128), BF), pltpu.SemaphoreType.DMA((8,))],
        compiler_params=PARAMS,
        cost_estimate=COST,
    )(
        place, cache_lengths, long_plan,
        *[
            pltpu.with_memory_space_constraint(value, pltpu.HBM)
            for value in (
                parents[0], long_parents, queries[0], long_queries[0], cache[0, 0].T, long_cache[0].T,
                tree_latent[0], long_tree_latent[0],
            )
        ],
    )
    cols = lax.all_gather(out_weight, "x")
    out_rows = jnp.stack([cols[k, :, :128] for k in range(4)] + [jnp.concatenate([cols[k, :, 128:] for k in range(4)], axis=1)])
    block, kv, out_rows = lax.optimization_barrier((block, kv, out_rows))
    got = lax.all_to_all(block, "x", 0, 0)
    out_rows = lax.ppermute(out_rows, ("x", "a"), [(4 * i + j, 4 * j + i) for i in range(4) for j in range(4)])
    kv = lax.all_gather(kv, ("y", "c"))
    kv, out_rows = lax.optimization_barrier((kv, out_rows))
    kv = kv.reshape((4, 2) + kv.shape[1:])

    heads = pl.pallas_call(
        attend_kernel,
        out_shape=jax.ShapeDtypeStruct((4, 5 * TREE * (SLICE // 2) + 3 * TREE, 128), BF),
        in_specs=[VMEM] * 4,
        out_specs=VMEM,
        scratch_shapes=[pltpu.VMEM((5, SLICE * TREE, KVR), BF)],
        compiler_params=PARAMS,
        cost_estimate=COST,
    )(got, query_l, tree_l, kv)
    shared = lax.all_to_all(heads, "y", 0, 0)
    out_rows = lax.all_gather(out_rows, ("b", "c"))
    out_rows = out_rows.reshape((4, 2) + out_rows.shape[1:])
    send = pl.pallas_call(
        project_kernel,
        out_shape=jax.ShapeDtypeStruct((4, 688, 128), BF),
        in_specs=[VMEM, VMEM],
        out_specs=VMEM,
        scratch_shapes=[pltpu.VMEM((TOKENS, SPAN), BF)],
        compiler_params=PARAMS,
    )(shared, out_rows)
    back = lax.all_to_all(send, "x", 0, 0)
    hidden, long_hidden = pl.pallas_call(
        finish_kernel,
        out_shape=(
            jax.ShapeDtypeStruct(residual.shape, BF),
            jax.ShapeDtypeStruct(long_residual.shape, BF),
        ),
        in_specs=[VMEM, VMEM, VMEM],
        out_specs=(VMEM, VMEM),
        scratch_shapes=[pltpu.VMEM((TOKENS, 128), F32)],
        compiler_params=PARAMS,
    )(back, residual, long_residual)
    accepted_cache = jnp.take_along_axis(tree_latent[0], accepted[0, 0][:, None], axis=0)[None, None]
    return hidden, accepted_cache, long_hidden


def solution(mesh):
    split = Mesh(mesh.devices.reshape(4, 4, 4, 4, 2), ("y", "x", "a", "b", "c"))
    return jax.shard_map(
        on_device,
        mesh=split,
        in_specs=(
            P(ROWS, COLS, None),
            P(ROWS, COLS, None),
            P(ROWS, COLS, None),
            P(ROWS, COLS, None, None),
            P(ROWS, COLS),
            P(ROWS, COLS, None),
            P(None, COLS, ROWS),
            P(COLS, None, None),
            P(COLS, None, None),
            P(COLS, None),
            P(COLS, ROWS, None),
            P(COLS, ROWS),
            P(COLS, None, ROWS),
            P(COLS, None),
            P(COLS, None),
            P(COLS, ROWS),
        ),
        out_specs=(P(None, COLS, ROWS), P(ROWS, COLS, None, None), P(COLS, None, ROWS)),
        check_vma=False,
    )
```

```python
import jax
import jax.numpy as jnp
from jax import lax
from jax.experimental import pallas as pl
from jax.experimental.pallas import tpu as pltpu
from jax.sharding import Mesh, PartitionSpec as P

HEADS = 40
NOPE = 64
ROPE = 32
VDIM = 64
KVR = 256
TREE = 32
ROWS = ("y", "x")
COLS = ("a", "b", "c")
BF = jnp.bfloat16
F32 = jnp.float32


OVER_LAST = (((1,), (1,)), ((), ()))
SLICE = HEADS // 4
SPAN = SLICE * VDIM
LONG_AT, TREE_AT, QUERY_AT, BLOCK = 576, 1152, 1280, 1536
TOKENS = 16 * TREE + TREE
QUARTER = TOKENS // 4


def split3(value):
    high = value.astype(BF)
    rest = value - high.astype(F32)
    mid = rest.astype(BF)
    return high, mid, (rest - mid.astype(F32)).astype(BF)


def dot(left, right):
    return jnp.dot(left, right, preferred_element_type=F32)


def dot_t(left, right):
    return lax.dot_general(left, right, OVER_LAST, preferred_element_type=F32)


def attend_kernel(got, query_l, tree_l, kv, out, lat):
    lanes = lax.broadcasted_iota(jnp.int32, (TREE, 128), 1)
    slots = lax.broadcasted_iota(jnp.int32, (1, 256), 1).astype(F32)
    scale = (NOPE + ROPE) ** -0.5
    size = SLICE * TREE

    def rope_rows(chunk):
        zero = jnp.zeros((TREE, 128), BF)
        return jnp.concatenate([jnp.where(lanes // 32 == h % 4, chunk(5 + h // 4), zero) for h in range(SLICE)], axis=0)

    def cached(query, rope, block, at, length):
        keys = jnp.concatenate([block[at : at + 288], block[at + 288 : at + 576]], axis=1)
        scores = dot(query, keys[:KVR]) + dot(rope, jnp.concatenate([keys[KVR:]] * 4, axis=0))
        return jnp.where(slots < length, scores * scale, -jnp.inf), keys[:KVR]

    def treed(query, rope, block, at):
        keys = jnp.concatenate([block[at : at + TREE], block[at + TREE : at + 2 * TREE]], axis=1)
        scores = dot_t(query, keys) + dot_t(rope, block[at + 2 * TREE : at + 3 * TREE])
        reach = block[at + 3 * TREE : at + 4 * TREE, :TREE].astype(F32)
        reach = jnp.concatenate([reach] * SLICE, axis=0)
        return jnp.where(reach > 0.5, scores * scale, -jnp.inf), keys

    for p in range(SLICE // 2):
        at = TREE * p
        rows = [got[k, QUERY_AT + at : QUERY_AT + at + TREE] for k in range(4)] + [query_l[at : at + TREE]]
        even = [jnp.where(lanes < NOPE, row, jnp.zeros_like(row)) for row in rows]
        odd = [jnp.where(lanes < NOPE, jnp.zeros_like(row), row) for row in rows]
        weight = kv[...][:, :, :, :KVR].reshape(SPAN, KVR)[128 * p : 128 * (p + 1)]
        part = dot(jnp.concatenate(even + odd, axis=0), weight).astype(BF)
        for s in range(2):
            for k in range(5):
                lat[k, TREE * (2 * p + s) : TREE * (2 * p + s + 1)] = part[TREE * (5 * s + k) : TREE * (5 * s + k + 1)]

    for k in range(4):
        block = got.at[k]
        query = lat[k]
        rope = rope_rows(lambda i: block[QUERY_AT + TREE * i : QUERY_AT + TREE * (i + 1)])
        length = block[TREE_AT + 3 * TREE : TREE_AT + 3 * TREE + 1, 32:33].astype(F32)
        first, keys = cached(query, rope, block, 0, length)
        second, tree = treed(query, rope, block, TREE_AT)
        top = jnp.maximum(jnp.max(first, axis=-1, keepdims=True), jnp.max(second, axis=-1, keepdims=True))
        first, second = jnp.exp(first - top), jnp.exp(second - top)
        total = jnp.sum(first, axis=-1, keepdims=True) + jnp.sum(second, axis=-1, keepdims=True)
        acc = dot_t(first.astype(BF), keys) + dot(second.astype(BF), tree)
        lat[k] = (acc / total).astype(BF)

    query = lat[4]
    rope = rope_rows(lambda i: query_l[TREE * i : TREE * (i + 1)])
    second, tree = treed(query, rope, tree_l, 0)
    scored = []
    for k in range(4):
        block = got.at[k]
        length = block[TREE_AT + 3 * TREE : TREE_AT + 3 * TREE + 1, 33:34].astype(F32)
        scored.append(cached(query, rope, block, LONG_AT, length))
    top = jnp.max(second, axis=-1, keepdims=True)
    for scores, _ in scored:
        top = jnp.maximum(top, jnp.max(scores, axis=-1, keepdims=True))
    second = jnp.exp(second - top)
    total = jnp.sum(second, axis=-1, keepdims=True)
    acc = dot(second.astype(BF), tree)
    for scores, keys in scored:
        weights = jnp.exp(scores - top)
        total += jnp.sum(weights, axis=-1, keepdims=True)
        acc += dot_t(weights.astype(BF), keys)
    lat[4] = (acc / total).astype(BF)
    column = top + jnp.log(total)
    logs = jnp.zeros((TREE, 128), F32)
    for h in range(SLICE):
        logs = jnp.where(lanes == h, column[TREE * h : TREE * (h + 1)], logs)

    for p in range(SLICE // 2):
        pair = []
        for h in (2 * p, 2 * p + 1):
            rows = jnp.concatenate([lat[k, TREE * h : TREE * (h + 1)] for k in range(5)], axis=0)
            weight = kv[...][:, :, :, KVR:].reshape(SPAN, KVR)[VDIM * h : VDIM * (h + 1)]
            pair.append(dot_t(rows, weight))
        heads = jnp.concatenate(pair, axis=1).astype(BF)
        for d in range(4):
            out[d, 5 * TREE * p : 5 * TREE * (p + 1)] = heads
    base = 5 * TREE * (SLICE // 2)
    for i, part in enumerate(split3(logs)):
        for d in range(4):
            out[d, base + TREE * i : base + TREE * (i + 1)] = part


def project_kernel(got, weight, send, rows):
    base = 5 * TREE * (SLICE // 2)
    logs = sum(got[:, base + TREE * i : base + TREE * (i + 1)].astype(F32) for i in range(3))
    share = jnp.exp(logs - jnp.max(logs, axis=0)[None])
    share = (share / jnp.sum(share, axis=0)[None]).reshape(4 * TREE, 128)
    high = share.astype(BF)
    low = (share - high.astype(F32)).astype(BF)
    for p in range(SLICE // 2):
        at = 5 * TREE * p
        cols = slice(128 * p, 128 * (p + 1))
        for y in range(4):
            rows[4 * TREE * y : 4 * TREE * (y + 1), cols] = got[y, at : at + 4 * TREE]
        owner = lax.broadcasted_iota(jnp.int32, (128, 128), 1) // VDIM + 2 * p
        select = jnp.where(lax.broadcasted_iota(jnp.int32, (128, 128), 0) == owner, 1.0, 0.0).astype(BF)
        wide = (dot(high, select) + dot(low, select)).reshape(4, TREE, 128)
        piece = got[:, at + 4 * TREE : at + 5 * TREE].astype(F32) * wide
        rows[16 * TREE : 17 * TREE, cols] = jnp.sum(piece, axis=0).astype(BF)
    blocks = [weight[:, :, k].reshape(SPAN, 128) for k in range(5)]
    for k in (0, 2):
        both = dot(rows[...], jnp.concatenate(blocks[k : k + 2], axis=1)).astype(BF)
        send[k, :TOKENS] = both[:, :128]
        send[k + 1, :TOKENS] = both[:, 128:]
    rest = dot(rows[...], blocks[4])
    lanes = lax.broadcasted_iota(jnp.int32, (QUARTER, 128), 1) // 32
    for k in range(4):
        packed = jnp.zeros((QUARTER, 128), F32)
        for g in range(4):
            part = rest[QUARTER * g : QUARTER * (g + 1)]
            shift = (32 * (g - k)) % 128
            part = pltpu.roll(part, shift, 1) if shift else part
            packed = jnp.where(lanes == g, part, packed)
        send[k, TOKENS : TOKENS + QUARTER] = packed.astype(BF)
        send[k, TOKENS + QUARTER :] = jnp.zeros((send.shape[1] - TOKENS - QUARTER, 128), BF)


def finish_kernel(got, residual, long_residual, hidden, long_hidden, tail):
    rest = jnp.sum(got[:, TOKENS : TOKENS + QUARTER].astype(F32), axis=0)
    for g in range(4):
        tail[QUARTER * g : QUARTER * (g + 1)] = pltpu.roll(rest, (-32 * g) % 128, 1) if g else rest
    for i in range(17):
        at = slice(TREE * i, TREE * (i + 1))
        main = jnp.sum(got[:, at].astype(F32), axis=0)
        source, target, k = (residual, hidden, i) if i < 16 else (long_residual, long_hidden, 0)
        target[k, :, :128] = (source[k, :, :128].astype(F32) + main).astype(BF)
        target[k, :, 128:160] = (source[k, :, 128:160].astype(F32) + tail[at, :32]).astype(BF)


SMEM = pl.BlockSpec(memory_space=pltpu.SMEM)
VMEM = pl.BlockSpec(memory_space=pltpu.VMEM)
HBM = pl.BlockSpec(memory_space=pltpu.HBM)
COST = pl.CostEstimate(flops=6 * 10**9, transcendentals=10**6, bytes_accessed=18 * 10**6)
PARAMS = pltpu.CompilerParams(vmem_limit_bytes=48 << 20)


def onehot(rows, cols, match):
    row = lax.broadcasted_iota(jnp.int32, (rows, cols), 0)
    col = lax.broadcasted_iota(jnp.int32, (rows, cols), 1)
    return jnp.where(match(row, col), 1.0, 0.0).astype(BF)


def pack_kernel(place, length, length_l, *refs):
    sources, (block, own_q, own_tree), held, (slices, sems) = refs[:8], refs[8:11], refs[11:19], refs[19:]
    copies = [pltpu.make_async_copy(sources[i], held[i], sems.at[i]) for i in range(8)]
    for copy in copies:
        copy.start()
    parents, parents_l, queries, queries_l, keys, keys_l, tree, tree_l = held
    lanes = lax.broadcasted_iota(jnp.int32, (TREE, 128), 1)
    tile4 = onehot(TREE, 128, lambda row, col: col % 32 == row)
    widen = onehot(TREE, 128, lambda row, col: col == row)
    above = lax.broadcasted_iota(jnp.int32, (TREE, TREE), 0)
    same = above == lax.broadcasted_iota(jnp.int32, (TREE, TREE), 1)
    extras = []
    for copy in copies[:2]:
        copy.wait()
    for i, ids in enumerate((parents, parents_l)):
        reach = jnp.where(same | (above == ids[...]), 1.0, 0.0).astype(BF)
        for _ in range((TREE - 1).bit_length()):
            reach = jnp.minimum(dot(reach, reach), 1.0).astype(BF)
        extra = lax.dot_general(reach, widen, (((0,), (0,)), ((), ())), preferred_element_type=F32)
        if i == 1:
            extra = jnp.where(place[1] == 0, extra, 0.0)
        extra = jnp.where(lanes == 32, length[0, 0].astype(F32), extra)
        extras.append(jnp.where(lanes == 33, length_l[0, 0].astype(F32), extra).astype(BF))
    for copy in copies[2:]:
        copy.wait()
    for d in range(4):
        block[d, 0:288] = keys[:, :128]
        block[d, 288:576] = keys[:, 128:]
        block[d, 576:864] = keys_l[:, :128]
        block[d, 864:1152] = keys_l[:, 128:]
    for i, rows in enumerate((tree, tree_l)):
        parts = (rows[:, :128], rows[:, 128:KVR], dot(rows[:, KVR:], tile4).astype(BF), extras[i])
        for k, part in enumerate(parts):
            at = slice(TREE * k, TREE * (k + 1))
            if i == 0:
                for d in range(4):
                    block[d, TREE_AT + at.start : TREE_AT + at.stop] = part
            else:
                own_tree[at] = part

    def source(col):
        nope = 96 * (col // NOPE) + col % NOPE
        rope = 96 * ((col - 256) // ROPE) + NOPE + (col - 256) % ROPE
        return jnp.where(col < 256, nope, rope)

    sort = onehot(384, 384, lambda row, col: source(col) == row)
    windows = [slice(384 * w, 384 * (w + 1)) for w in range(HEADS // 4)]
    sorted_all = dot(jnp.concatenate([q[:, cols] for cols in windows for q in (queries, queries_l)], axis=0), sort)
    rope = []
    for w in range(HEADS // 4):
        moved = sorted_all[2 * TREE * w : 2 * TREE * (w + 1)]
        rope.append(moved[:, 256:])
        for half in range(2):
            s, p = divmod(2 * w + half, SLICE // 2)
            part = moved[:, 128 * half : 128 * (half + 1)].astype(BF)
            block[s, QUERY_AT + TREE * p : QUERY_AT + TREE * (p + 1)] = part[:TREE]
            slices[s, TREE * p : TREE * (p + 1)] = part[TREE:]
    wide = lax.broadcasted_iota(jnp.int32, (2 * TREE, 128), 1)
    for s in range(4):
        first = SLICE * s // 4
        for k in range(3):
            if s % 2 == 0:
                part = rope[first + k]
            else:
                after = pltpu.roll(rope[first + k + 1], 64, 1) if k < 2 else jnp.zeros((2 * TREE, 128), F32)
                part = jnp.where(wide < 64, pltpu.roll(rope[first + k], 64, 1), after)
            part = part.astype(BF)
            at = TREE * (5 + k)
            block[s, QUERY_AT + at : QUERY_AT + at + TREE] = part[:TREE]
            slices[s, at : at + TREE] = part[TREE:]
    own_q[...] = slices[place[0]]


def on_device(
    queries, tree_latent, parents, cache, cache_lengths, accepted, residual,
    long_queries, long_tree_latent, long_parents, long_cache, long_plan, long_residual,
    key_up, value_up, out_weight,
):
    y, x = lax.axis_index("y"), lax.axis_index("x")
    place = jnp.stack([x, y]).astype(jnp.int32)
    pairs = [(r * 16 + z, ((z % 4) * 4 + z // 4) * 16 + (z + r) % 16) for r in range(16) for z in range(16)]
    rows = 8 * TREE
    block, query_l, tree_l = pl.pallas_call(
        pack_kernel,
        out_shape=(
            jax.ShapeDtypeStruct((4, BLOCK, 128), BF),
            jax.ShapeDtypeStruct((rows, 128), BF),
            jax.ShapeDtypeStruct((4 * TREE, 128), BF),
        ),
        in_specs=[SMEM] * 3 + [HBM] * 8,
        out_specs=(VMEM, VMEM, VMEM),
        scratch_shapes=[pltpu.VMEM((1, TREE), jnp.int32)] * 2
        + [pltpu.VMEM((TREE, HEADS * (NOPE + ROPE)), BF)] * 2
        + [pltpu.VMEM((KVR + ROPE, 256), BF)] * 2
        + [pltpu.VMEM((TREE, KVR + ROPE), BF)] * 2
        + [pltpu.VMEM((4, rows, 128), BF), pltpu.SemaphoreType.DMA((8,))],
        compiler_params=PARAMS,
        cost_estimate=COST,
    )(
        place, cache_lengths, long_plan,
        *[
            pltpu.with_memory_space_constraint(value, pltpu.HBM)
            for value in (
                parents[0], long_parents, queries[0], long_queries[0], cache[0, 0].T, long_cache[0].T,
                tree_latent[0], long_tree_latent[0],
            )
        ],
    )
    kv, block = lax.optimization_barrier((jnp.concatenate([key_up, value_up], axis=1), block))
    kv = lax.ppermute(kv, ("y", "x", "a", "b"), pairs)
    cols = lax.all_gather(out_weight, "x")
    out_rows = jnp.stack([cols[k, :, :128] for k in range(4)] + [jnp.concatenate([cols[k, :, 128:] for k in range(4)], axis=1)])
    block, kv, out_rows = lax.optimization_barrier((block, kv, out_rows))
    got = lax.all_to_all(block, "x", 0, 0)
    out_rows = lax.ppermute(out_rows, ("x", "a"), [(4 * i + j, 4 * j + i) for i in range(4) for j in range(4)])
    kv = lax.all_gather(kv, ("y", "c"))
    kv, out_rows = lax.optimization_barrier((kv, out_rows))
    kv = kv.reshape((4, 2) + kv.shape[1:])

    heads = pl.pallas_call(
        attend_kernel,
        out_shape=jax.ShapeDtypeStruct((4, 5 * TREE * (SLICE // 2) + 3 * TREE, 128), BF),
        in_specs=[VMEM] * 4,
        out_specs=VMEM,
        scratch_shapes=[pltpu.VMEM((5, SLICE * TREE, KVR), BF)],
        compiler_params=PARAMS,
        cost_estimate=COST,
    )(got, query_l, tree_l, kv)
    shared = lax.all_to_all(heads, "y", 0, 0)
    out_rows = lax.all_gather(out_rows, ("b", "c"))
    out_rows = out_rows.reshape((4, 2) + out_rows.shape[1:])
    send = pl.pallas_call(
        project_kernel,
        out_shape=jax.ShapeDtypeStruct((4, 688, 128), BF),
        in_specs=[VMEM, VMEM],
        out_specs=VMEM,
        scratch_shapes=[pltpu.VMEM((TOKENS, SPAN), BF)],
        compiler_params=PARAMS,
    )(shared, out_rows)
    back = lax.all_to_all(send, "x", 0, 0)
    hidden, long_hidden = pl.pallas_call(
        finish_kernel,
        out_shape=(
            jax.ShapeDtypeStruct(residual.shape, BF),
            jax.ShapeDtypeStruct(long_residual.shape, BF),
        ),
        in_specs=[VMEM, VMEM, VMEM],
        out_specs=(VMEM, VMEM),
        scratch_shapes=[pltpu.VMEM((TOKENS, 128), F32)],
        compiler_params=PARAMS,
    )(back, residual, long_residual)
    accepted_cache = jnp.take_along_axis(tree_latent[0], accepted[0, 0][:, None], axis=0)[None, None]
    return hidden, accepted_cache, long_hidden


def solution(mesh):
    split = Mesh(mesh.devices.reshape(4, 4, 4, 4, 2), ("y", "x", "a", "b", "c"))
    return jax.shard_map(
        on_device,
        mesh=split,
        in_specs=(
            P(ROWS, COLS, None),
            P(ROWS, COLS, None),
            P(ROWS, COLS, None),
            P(ROWS, COLS, None, None),
            P(ROWS, COLS),
            P(ROWS, COLS, None),
            P(None, COLS, ROWS),
            P(COLS, None, None),
            P(COLS, None, None),
            P(COLS, None),
            P(COLS, ROWS, None),
            P(COLS, ROWS),
            P(COLS, None, ROWS),
            P(COLS, None),
            P(COLS, None),
            P(COLS, ROWS),
        ),
        out_specs=(P(None, COLS, ROWS), P(ROWS, COLS, None, None), P(COLS, None, ROWS)),
        check_vma=False,
    )
```

```python
import jax
import jax.numpy as jnp
from jax import lax
from jax.experimental import pallas as pl
from jax.experimental.pallas import tpu as pltpu
from jax.sharding import Mesh, PartitionSpec as P

HEADS = 40
NOPE = 64
ROPE = 32
VDIM = 64
KVR = 256
TREE = 32
ROWS = ("y", "x")
COLS = ("a", "b", "c")
BF = jnp.bfloat16
F32 = jnp.float32


OVER_LAST = (((1,), (1,)), ((), ()))
SLICE = HEADS // 4
SPAN = SLICE * VDIM
LONG_AT, TREE_AT, QUERY_AT, BLOCK = 576, 1152, 1280, 1536
TOKENS = 16 * TREE + TREE
QUARTER = TOKENS // 4


def split3(value):
    high = value.astype(BF)
    rest = value - high.astype(F32)
    mid = rest.astype(BF)
    return high, mid, (rest - mid.astype(F32)).astype(BF)


def dot(left, right):
    return jnp.dot(left, right, preferred_element_type=F32)


def dot_t(left, right):
    return lax.dot_general(left, right, OVER_LAST, preferred_element_type=F32)


def attend_kernel(got, query_l, tree_l, kv, out, lat):
    lanes = lax.broadcasted_iota(jnp.int32, (TREE, 128), 1)
    slots = lax.broadcasted_iota(jnp.int32, (1, 256), 1).astype(F32)
    scale = (NOPE + ROPE) ** -0.5
    size = SLICE * TREE

    def rope_rows(chunk):
        zero = jnp.zeros((TREE, 128), BF)
        return jnp.concatenate([jnp.where(lanes // 32 == h % 4, chunk(5 + h // 4), zero) for h in range(SLICE)], axis=0)

    def cached(query, rope, block, at, length):
        keys = jnp.concatenate([block[at : at + 288], block[at + 288 : at + 576]], axis=1)
        scores = dot(query, keys[:KVR]) + dot(rope, jnp.concatenate([keys[KVR:]] * 4, axis=0))
        return jnp.where(slots < length, scores * scale, -jnp.inf), keys[:KVR]

    def treed(query, rope, block, at):
        keys = jnp.concatenate([block[at : at + TREE], block[at + TREE : at + 2 * TREE]], axis=1)
        scores = dot_t(query, keys) + dot_t(rope, block[at + 2 * TREE : at + 3 * TREE])
        reach = block[at + 3 * TREE : at + 4 * TREE, :TREE].astype(F32)
        reach = jnp.concatenate([reach] * SLICE, axis=0)
        return jnp.where(reach > 0.5, scores * scale, -jnp.inf), keys

    for p in range(SLICE // 2):
        at = TREE * p
        rows = [got[k, QUERY_AT + at : QUERY_AT + at + TREE] for k in range(4)] + [query_l[at : at + TREE]]
        even = [jnp.where(lanes < NOPE, row, jnp.zeros_like(row)) for row in rows]
        odd = [jnp.where(lanes < NOPE, jnp.zeros_like(row), row) for row in rows]
        weight = kv[...][:, :, :, :KVR].reshape(SPAN, KVR)[128 * p : 128 * (p + 1)]
        part = dot(jnp.concatenate(even + odd, axis=0), weight).astype(BF)
        for s in range(2):
            for k in range(5):
                lat[k, TREE * (2 * p + s) : TREE * (2 * p + s + 1)] = part[TREE * (5 * s + k) : TREE * (5 * s + k + 1)]

    for k in range(4):
        block = got.at[k]
        query = lat[k]
        rope = rope_rows(lambda i: block[QUERY_AT + TREE * i : QUERY_AT + TREE * (i + 1)])
        length = block[TREE_AT + 3 * TREE : TREE_AT + 3 * TREE + 1, 32:33].astype(F32)
        first, keys = cached(query, rope, block, 0, length)
        second, tree = treed(query, rope, block, TREE_AT)
        top = jnp.maximum(jnp.max(first, axis=-1, keepdims=True), jnp.max(second, axis=-1, keepdims=True))
        first, second = jnp.exp(first - top), jnp.exp(second - top)
        total = jnp.sum(first, axis=-1, keepdims=True) + jnp.sum(second, axis=-1, keepdims=True)
        acc = dot_t(first.astype(BF), keys) + dot(second.astype(BF), tree)
        lat[k] = (acc / total).astype(BF)

    query = lat[4]
    rope = rope_rows(lambda i: query_l[TREE * i : TREE * (i + 1)])
    second, tree = treed(query, rope, tree_l, 0)
    scored = []
    for k in range(4):
        block = got.at[k]
        length = block[TREE_AT + 3 * TREE : TREE_AT + 3 * TREE + 1, 33:34].astype(F32)
        scored.append(cached(query, rope, block, LONG_AT, length))
    top = jnp.max(second, axis=-1, keepdims=True)
    for scores, _ in scored:
        top = jnp.maximum(top, jnp.max(scores, axis=-1, keepdims=True))
    second = jnp.exp(second - top)
    total = jnp.sum(second, axis=-1, keepdims=True)
    acc = dot(second.astype(BF), tree)
    for scores, keys in scored:
        weights = jnp.exp(scores - top)
        total += jnp.sum(weights, axis=-1, keepdims=True)
        acc += dot_t(weights.astype(BF), keys)
    lat[4] = (acc / total).astype(BF)
    column = top + jnp.log(total)
    logs = jnp.zeros((TREE, 128), F32)
    for h in range(SLICE):
        logs = jnp.where(lanes == h, column[TREE * h : TREE * (h + 1)], logs)

    for p in range(SLICE // 2):
        pair = []
        for h in (2 * p, 2 * p + 1):
            rows = jnp.concatenate([lat[k, TREE * h : TREE * (h + 1)] for k in range(5)], axis=0)
            weight = kv[...][:, :, :, KVR:].reshape(SPAN, KVR)[VDIM * h : VDIM * (h + 1)]
            pair.append(dot_t(rows, weight))
        heads = jnp.concatenate(pair, axis=1).astype(BF)
        for d in range(4):
            out[d, 5 * TREE * p : 5 * TREE * (p + 1)] = heads
    base = 5 * TREE * (SLICE // 2)
    for i, part in enumerate(split3(logs)):
        for d in range(4):
            out[d, base + TREE * i : base + TREE * (i + 1)] = part


def project_kernel(got, weight, send, rows):
    base = 5 * TREE * (SLICE // 2)
    logs = sum(got[:, base + TREE * i : base + TREE * (i + 1)].astype(F32) for i in range(3))
    share = jnp.exp(logs - jnp.max(logs, axis=0)[None])
    share = (share / jnp.sum(share, axis=0)[None]).reshape(4 * TREE, 128)
    high = share.astype(BF)
    low = (share - high.astype(F32)).astype(BF)
    for p in range(SLICE // 2):
        at = 5 * TREE * p
        cols = slice(128 * p, 128 * (p + 1))
        for y in range(4):
            rows[4 * TREE * y : 4 * TREE * (y + 1), cols] = got[y, at : at + 4 * TREE]
        owner = lax.broadcasted_iota(jnp.int32, (128, 128), 1) // VDIM + 2 * p
        select = jnp.where(lax.broadcasted_iota(jnp.int32, (128, 128), 0) == owner, 1.0, 0.0).astype(BF)
        wide = (dot(high, select) + dot(low, select)).reshape(4, TREE, 128)
        piece = got[:, at + 4 * TREE : at + 5 * TREE].astype(F32) * wide
        rows[16 * TREE : 17 * TREE, cols] = jnp.sum(piece, axis=0).astype(BF)
    blocks = [weight[:, :, k].reshape(SPAN, 128) for k in range(5)]
    for k in (0, 2):
        both = dot(rows[...], jnp.concatenate(blocks[k : k + 2], axis=1)).astype(BF)
        send[k, :TOKENS] = both[:, :128]
        send[k + 1, :TOKENS] = both[:, 128:]
    rest = dot(rows[...], blocks[4])
    lanes = lax.broadcasted_iota(jnp.int32, (QUARTER, 128), 1) // 32
    for k in range(4):
        packed = jnp.zeros((QUARTER, 128), F32)
        for g in range(4):
            part = rest[QUARTER * g : QUARTER * (g + 1)]
            shift = (32 * (g - k)) % 128
            part = pltpu.roll(part, shift, 1) if shift else part
            packed = jnp.where(lanes == g, part, packed)
        send[k, TOKENS : TOKENS + QUARTER] = packed.astype(BF)
        send[k, TOKENS + QUARTER :] = jnp.zeros((send.shape[1] - TOKENS - QUARTER, 128), BF)


def finish_kernel(got, residual, long_residual, hidden, long_hidden, tail):
    rest = jnp.sum(got[:, TOKENS : TOKENS + QUARTER].astype(F32), axis=0)
    for g in range(4):
        tail[QUARTER * g : QUARTER * (g + 1)] = pltpu.roll(rest, (-32 * g) % 128, 1) if g else rest
    for i in range(17):
        at = slice(TREE * i, TREE * (i + 1))
        main = jnp.sum(got[:, at].astype(F32), axis=0)
        source, target, k = (residual, hidden, i) if i < 16 else (long_residual, long_hidden, 0)
        target[k, :, :128] = (source[k, :, :128].astype(F32) + main).astype(BF)
        target[k, :, 128:160] = (source[k, :, 128:160].astype(F32) + tail[at, :32]).astype(BF)


SMEM = pl.BlockSpec(memory_space=pltpu.SMEM)
VMEM = pl.BlockSpec(memory_space=pltpu.VMEM)
HBM = pl.BlockSpec(memory_space=pltpu.HBM)
COST = pl.CostEstimate(flops=6 * 10**9, transcendentals=10**6, bytes_accessed=18 * 10**6)
PARAMS = pltpu.CompilerParams(vmem_limit_bytes=48 << 20)


def onehot(rows, cols, match):
    row = lax.broadcasted_iota(jnp.int32, (rows, cols), 0)
    col = lax.broadcasted_iota(jnp.int32, (rows, cols), 1)
    return jnp.where(match(row, col), 1.0, 0.0).astype(BF)


def pack_kernel(place, length, length_l, *refs):
    sources, (block, own_q, own_tree, kept), held, (slices, sems) = refs[:9], refs[9:13], refs[13:22], refs[22:]
    copies = [pltpu.make_async_copy(sources[i], held[i], sems.at[i]) for i in range(9)]
    for copy in copies:
        copy.start()
    parents, parents_l, chosen, queries, queries_l, keys, keys_l, tree, tree_l = held
    lanes = lax.broadcasted_iota(jnp.int32, (TREE, 128), 1)
    tile4 = onehot(TREE, 128, lambda row, col: col % 32 == row)
    widen = onehot(TREE, 128, lambda row, col: col == row)
    above = lax.broadcasted_iota(jnp.int32, (TREE, TREE), 0)
    same = above == lax.broadcasted_iota(jnp.int32, (TREE, TREE), 1)
    extras = []
    for copy in copies[:2]:
        copy.wait()
    for i, ids in enumerate((parents, parents_l)):
        reach = jnp.where(same | (above == ids[...]), 1.0, 0.0).astype(BF)
        for _ in range((TREE - 1).bit_length()):
            reach = jnp.minimum(dot(reach, reach), 1.0).astype(BF)
        extra = lax.dot_general(reach, widen, (((0,), (0,)), ((), ())), preferred_element_type=F32)
        if i == 1:
            extra = jnp.where(place[1] == 0, extra, 0.0)
        extra = jnp.where(lanes == 32, length[0, 0].astype(F32), extra)
        extras.append(jnp.where(lanes == 33, length_l[0, 0].astype(F32), extra).astype(BF))
    for copy in copies[2:]:
        copy.wait()
    count = chosen.shape[1]
    pick = jnp.where(lax.broadcasted_iota(jnp.int32, (TREE, count), 0) == chosen[...], 1.0, 0.0).astype(BF)
    kept[...] = lax.dot_general(pick, tree[...], (((0,), (0,)), ((), ())), preferred_element_type=F32).astype(BF)
    for d in range(4):
        block[d, 0:288] = keys[:, :128]
        block[d, 288:576] = keys[:, 128:]
        block[d, 576:864] = keys_l[:, :128]
        block[d, 864:1152] = keys_l[:, 128:]
    for i, rows in enumerate((tree, tree_l)):
        parts = (rows[:, :128], rows[:, 128:KVR], dot(rows[:, KVR:], tile4).astype(BF), extras[i])
        for k, part in enumerate(parts):
            at = slice(TREE * k, TREE * (k + 1))
            if i == 0:
                for d in range(4):
                    block[d, TREE_AT + at.start : TREE_AT + at.stop] = part
            else:
                own_tree[at] = part

    def source(col):
        nope = 96 * (col // NOPE) + col % NOPE
        rope = 96 * ((col - 256) // ROPE) + NOPE + (col - 256) % ROPE
        return jnp.where(col < 256, nope, rope)

    sort = onehot(384, 384, lambda row, col: source(col) == row)
    windows = [slice(384 * w, 384 * (w + 1)) for w in range(HEADS // 4)]
    sorted_all = dot(jnp.concatenate([q[:, cols] for cols in windows for q in (queries, queries_l)], axis=0), sort)
    rope = []
    for w in range(HEADS // 4):
        moved = sorted_all[2 * TREE * w : 2 * TREE * (w + 1)]
        rope.append(moved[:, 256:])
        for half in range(2):
            s, p = divmod(2 * w + half, SLICE // 2)
            part = moved[:, 128 * half : 128 * (half + 1)].astype(BF)
            block[s, QUERY_AT + TREE * p : QUERY_AT + TREE * (p + 1)] = part[:TREE]
            slices[s, TREE * p : TREE * (p + 1)] = part[TREE:]
    wide = lax.broadcasted_iota(jnp.int32, (2 * TREE, 128), 1)
    for s in range(4):
        first = SLICE * s // 4
        for k in range(3):
            if s % 2 == 0:
                part = rope[first + k]
            else:
                after = pltpu.roll(rope[first + k + 1], 64, 1) if k < 2 else jnp.zeros((2 * TREE, 128), F32)
                part = jnp.where(wide < 64, pltpu.roll(rope[first + k], 64, 1), after)
            part = part.astype(BF)
            at = TREE * (5 + k)
            block[s, QUERY_AT + at : QUERY_AT + at + TREE] = part[:TREE]
            slices[s, at : at + TREE] = part[TREE:]
    own_q[...] = slices[place[0]]


def on_device(
    queries, tree_latent, parents, cache, cache_lengths, accepted, residual,
    long_queries, long_tree_latent, long_parents, long_cache, long_plan, long_residual,
    key_up, value_up, out_weight,
):
    y, x = lax.axis_index("y"), lax.axis_index("x")
    place = jnp.stack([x, y]).astype(jnp.int32)
    pairs = [(r * 16 + z, ((z % 4) * 4 + z // 4) * 16 + (z + r) % 16) for r in range(16) for z in range(16)]
    kv, place = lax.optimization_barrier((jnp.concatenate([key_up, value_up], axis=1), place))
    kv = lax.ppermute(kv, ("y", "x", "a", "b"), pairs)
    rows = 8 * TREE
    block, query_l, tree_l, accepted_cache = pl.pallas_call(
        pack_kernel,
        out_shape=(
            jax.ShapeDtypeStruct((4, BLOCK, 128), BF),
            jax.ShapeDtypeStruct((rows, 128), BF),
            jax.ShapeDtypeStruct((4 * TREE, 128), BF),
            jax.ShapeDtypeStruct((accepted.shape[2], KVR + ROPE), BF),
        ),
        in_specs=[SMEM] * 3 + [HBM] * 9,
        out_specs=(VMEM, VMEM, VMEM, VMEM),
        scratch_shapes=[pltpu.VMEM((1, TREE), jnp.int32)] * 2
        + [pltpu.VMEM((1, accepted.shape[2]), jnp.int32)]
        + [pltpu.VMEM((TREE, HEADS * (NOPE + ROPE)), BF)] * 2
        + [pltpu.VMEM((KVR + ROPE, 256), BF)] * 2
        + [pltpu.VMEM((TREE, KVR + ROPE), BF)] * 2
        + [pltpu.VMEM((4, rows, 128), BF), pltpu.SemaphoreType.DMA((9,))],
        compiler_params=PARAMS,
        cost_estimate=COST,
    )(
        place, cache_lengths, long_plan,
        *[
            pltpu.with_memory_space_constraint(value, pltpu.HBM)
            for value in (
                parents[0], long_parents, accepted[0], queries[0], long_queries[0], cache[0, 0].T, long_cache[0].T,
                tree_latent[0], long_tree_latent[0],
            )
        ],
    )
    cols = lax.all_gather(out_weight, "x")
    out_rows = jnp.stack([cols[k, :, :128] for k in range(4)] + [jnp.concatenate([cols[k, :, 128:] for k in range(4)], axis=1)])
    block, kv, out_rows = lax.optimization_barrier((block, kv, out_rows))
    got = lax.all_to_all(block, "x", 0, 0)
    out_rows = lax.ppermute(out_rows, ("x", "a"), [(4 * i + j, 4 * j + i) for i in range(4) for j in range(4)])
    kv = lax.all_gather(kv, ("y", "c"))
    kv, out_rows = lax.optimization_barrier((kv, out_rows))
    kv = kv.reshape((4, 2) + kv.shape[1:])

    heads = pl.pallas_call(
        attend_kernel,
        out_shape=jax.ShapeDtypeStruct((4, 5 * TREE * (SLICE // 2) + 3 * TREE, 128), BF),
        in_specs=[VMEM] * 4,
        out_specs=VMEM,
        scratch_shapes=[pltpu.VMEM((5, SLICE * TREE, KVR), BF)],
        compiler_params=PARAMS,
        cost_estimate=COST,
    )(got, query_l, tree_l, kv)
    shared = lax.all_to_all(heads, "y", 0, 0)
    out_rows = lax.all_gather(out_rows, ("b", "c"))
    out_rows = out_rows.reshape((4, 2) + out_rows.shape[1:])
    send = pl.pallas_call(
        project_kernel,
        out_shape=jax.ShapeDtypeStruct((4, 688, 128), BF),
        in_specs=[VMEM, VMEM],
        out_specs=VMEM,
        scratch_shapes=[pltpu.VMEM((TOKENS, SPAN), BF)],
        compiler_params=PARAMS,
    )(shared, out_rows)
    back = lax.all_to_all(send, "x", 0, 0)
    hidden, long_hidden = pl.pallas_call(
        finish_kernel,
        out_shape=(
            jax.ShapeDtypeStruct(residual.shape, BF),
            jax.ShapeDtypeStruct(long_residual.shape, BF),
        ),
        in_specs=[VMEM, VMEM, VMEM],
        out_specs=(VMEM, VMEM),
        scratch_shapes=[pltpu.VMEM((TOKENS, 128), F32)],
        compiler_params=PARAMS,
    )(back, residual, long_residual)
    return hidden, accepted_cache[None, None], long_hidden


def solution(mesh):
    split = Mesh(mesh.devices.reshape(4, 4, 4, 4, 2), ("y", "x", "a", "b", "c"))
    return jax.shard_map(
        on_device,
        mesh=split,
        in_specs=(
            P(ROWS, COLS, None),
            P(ROWS, COLS, None),
            P(ROWS, COLS, None),
            P(ROWS, COLS, None, None),
            P(ROWS, COLS),
            P(ROWS, COLS, None),
            P(None, COLS, ROWS),
            P(COLS, None, None),
            P(COLS, None, None),
            P(COLS, None),
            P(COLS, ROWS, None),
            P(COLS, ROWS),
            P(COLS, None, ROWS),
            P(COLS, None),
            P(COLS, None),
            P(COLS, ROWS),
        ),
        out_specs=(P(None, COLS, ROWS), P(ROWS, COLS, None, None), P(COLS, None, ROWS)),
        check_vma=False,
    )
```

```python
import jax
import jax.numpy as jnp
from jax import lax
from jax.experimental import pallas as pl
from jax.experimental.pallas import tpu as pltpu
from jax.sharding import Mesh, PartitionSpec as P

HEADS = 40
NOPE = 64
ROPE = 32
VDIM = 64
KVR = 256
TREE = 32
ROWS = ("y", "x")
COLS = ("a", "b", "c")
BF = jnp.bfloat16
F32 = jnp.float32


OVER_LAST = (((1,), (1,)), ((), ()))
SLICE = HEADS // 4
SPAN = SLICE * VDIM
LONG_AT, TREE_AT, QUERY_AT, BLOCK = 576, 1152, 1280, 1536
TOKENS = 16 * TREE + TREE
QUARTER = TOKENS // 4


def split3(value):
    high = value.astype(BF)
    rest = value - high.astype(F32)
    mid = rest.astype(BF)
    return high, mid, (rest - mid.astype(F32)).astype(BF)


def dot(left, right):
    return jnp.dot(left, right, preferred_element_type=F32)


def dot_t(left, right):
    return lax.dot_general(left, right, OVER_LAST, preferred_element_type=F32)


def attend_kernel(got, query_l, tree_l, kv, out, lat):
    lanes = lax.broadcasted_iota(jnp.int32, (TREE, 128), 1)
    slots = lax.broadcasted_iota(jnp.int32, (1, 256), 1).astype(F32)
    scale = (NOPE + ROPE) ** -0.5
    size = SLICE * TREE

    def rope_rows(chunk):
        zero = jnp.zeros((TREE, 128), BF)
        return jnp.concatenate([jnp.where(lanes // 32 == h % 4, chunk(5 + h // 4), zero) for h in range(SLICE)], axis=0)

    def cached(query, rope, block, at, length):
        keys = jnp.concatenate([block[at : at + 288], block[at + 288 : at + 576]], axis=1)
        scores = dot(query, keys[:KVR]) + dot(rope, jnp.concatenate([keys[KVR:]] * 4, axis=0))
        return jnp.where(slots < length, scores * scale, -jnp.inf), keys[:KVR]

    def treed(query, rope, block, at):
        keys = jnp.concatenate([block[at : at + TREE], block[at + TREE : at + 2 * TREE]], axis=1)
        scores = dot_t(query, keys) + dot_t(rope, block[at + 2 * TREE : at + 3 * TREE])
        reach = block[at + 3 * TREE : at + 4 * TREE, :TREE].astype(F32)
        reach = jnp.concatenate([reach] * SLICE, axis=0)
        return jnp.where(reach > 0.5, scores * scale, -jnp.inf), keys

    for p in range(SLICE // 2):
        at = TREE * p
        rows = [got[k, QUERY_AT + at : QUERY_AT + at + TREE] for k in range(4)] + [query_l[at : at + TREE]]
        even = [jnp.where(lanes < NOPE, row, jnp.zeros_like(row)) for row in rows]
        odd = [jnp.where(lanes < NOPE, jnp.zeros_like(row), row) for row in rows]
        weight = kv[...][:, :, :, :KVR].reshape(SPAN, KVR)[128 * p : 128 * (p + 1)]
        part = dot(jnp.concatenate(even + odd, axis=0), weight).astype(BF)
        for s in range(2):
            for k in range(5):
                lat[k, TREE * (2 * p + s) : TREE * (2 * p + s + 1)] = part[TREE * (5 * s + k) : TREE * (5 * s + k + 1)]

    for k in range(4):
        block = got.at[k]
        query = lat[k]
        rope = rope_rows(lambda i: block[QUERY_AT + TREE * i : QUERY_AT + TREE * (i + 1)])
        length = block[TREE_AT + 3 * TREE : TREE_AT + 3 * TREE + 1, 32:33].astype(F32)
        first, keys = cached(query, rope, block, 0, length)
        second, tree = treed(query, rope, block, TREE_AT)
        top = jnp.maximum(jnp.max(first, axis=-1, keepdims=True), jnp.max(second, axis=-1, keepdims=True))
        first, second = jnp.exp(first - top), jnp.exp(second - top)
        total = jnp.sum(first, axis=-1, keepdims=True) + jnp.sum(second, axis=-1, keepdims=True)
        acc = dot_t(first.astype(BF), keys) + dot(second.astype(BF), tree)
        lat[k] = (acc / total).astype(BF)

    query = lat[4]
    rope = rope_rows(lambda i: query_l[TREE * i : TREE * (i + 1)])
    second, tree = treed(query, rope, tree_l, 0)
    scored = []
    for k in range(4):
        block = got.at[k]
        length = block[TREE_AT + 3 * TREE : TREE_AT + 3 * TREE + 1, 33:34].astype(F32)
        scored.append(cached(query, rope, block, LONG_AT, length))
    top = jnp.max(second, axis=-1, keepdims=True)
    for scores, _ in scored:
        top = jnp.maximum(top, jnp.max(scores, axis=-1, keepdims=True))
    second = jnp.exp(second - top)
    total = jnp.sum(second, axis=-1, keepdims=True)
    acc = dot(second.astype(BF), tree)
    for scores, keys in scored:
        weights = jnp.exp(scores - top)
        total += jnp.sum(weights, axis=-1, keepdims=True)
        acc += dot_t(weights.astype(BF), keys)
    lat[4] = (acc / total).astype(BF)
    column = top + jnp.log(total)
    logs = jnp.zeros((TREE, 128), F32)
    for h in range(SLICE):
        logs = jnp.where(lanes == h, column[TREE * h : TREE * (h + 1)], logs)

    for p in range(SLICE // 2):
        pair = []
        for h in (2 * p, 2 * p + 1):
            rows = jnp.concatenate([lat[k, TREE * h : TREE * (h + 1)] for k in range(5)], axis=0)
            weight = kv[...][:, :, :, KVR:].reshape(SPAN, KVR)[VDIM * h : VDIM * (h + 1)]
            pair.append(dot_t(rows, weight))
        heads = jnp.concatenate(pair, axis=1).astype(BF)
        for d in range(4):
            out[d, 5 * TREE * p : 5 * TREE * (p + 1)] = heads
    base = 5 * TREE * (SLICE // 2)
    for i, part in enumerate(split3(logs)):
        for d in range(4):
            out[d, base + TREE * i : base + TREE * (i + 1)] = part


def project_kernel(got, weight, send, rows):
    base = 5 * TREE * (SLICE // 2)
    logs = sum(got[:, base + TREE * i : base + TREE * (i + 1)].astype(F32) for i in range(3))
    share = jnp.exp(logs - jnp.max(logs, axis=0)[None])
    share = (share / jnp.sum(share, axis=0)[None]).reshape(4 * TREE, 128)
    high = share.astype(BF)
    low = (share - high.astype(F32)).astype(BF)
    for p in range(SLICE // 2):
        at = 5 * TREE * p
        cols = slice(128 * p, 128 * (p + 1))
        for y in range(4):
            rows[4 * TREE * y : 4 * TREE * (y + 1), cols] = got[y, at : at + 4 * TREE]
        owner = lax.broadcasted_iota(jnp.int32, (128, 128), 1) // VDIM + 2 * p
        select = jnp.where(lax.broadcasted_iota(jnp.int32, (128, 128), 0) == owner, 1.0, 0.0).astype(BF)
        wide = (dot(high, select) + dot(low, select)).reshape(4, TREE, 128)
        piece = got[:, at + 4 * TREE : at + 5 * TREE].astype(F32) * wide
        rows[16 * TREE : 17 * TREE, cols] = jnp.sum(piece, axis=0).astype(BF)
    blocks = [weight[:, :, k].reshape(SPAN, 128) for k in range(5)]
    for k in (0, 2):
        both = dot(rows[...], jnp.concatenate(blocks[k : k + 2], axis=1)).astype(BF)
        send[k, :TOKENS] = both[:, :128]
        send[k + 1, :TOKENS] = both[:, 128:]
    rest = dot(rows[...], blocks[4])
    lanes = lax.broadcasted_iota(jnp.int32, (QUARTER, 128), 1) // 32
    for k in range(4):
        packed = jnp.zeros((QUARTER, 128), F32)
        for g in range(4):
            part = rest[QUARTER * g : QUARTER * (g + 1)]
            shift = (32 * (g - k)) % 128
            part = pltpu.roll(part, shift, 1) if shift else part
            packed = jnp.where(lanes == g, part, packed)
        send[k, TOKENS : TOKENS + QUARTER] = packed.astype(BF)
        send[k, TOKENS + QUARTER :] = jnp.zeros((send.shape[1] - TOKENS - QUARTER, 128), BF)


def finish_kernel(got, residual, long_residual, hidden, long_hidden, tail):
    rest = jnp.sum(got[:, TOKENS : TOKENS + QUARTER].astype(F32), axis=0)
    for g in range(4):
        tail[QUARTER * g : QUARTER * (g + 1)] = pltpu.roll(rest, (-32 * g) % 128, 1) if g else rest
    for i in range(17):
        at = slice(TREE * i, TREE * (i + 1))
        main = jnp.sum(got[:, at].astype(F32), axis=0)
        source, target, k = (residual, hidden, i) if i < 16 else (long_residual, long_hidden, 0)
        target[k, :, :128] = (source[k, :, :128].astype(F32) + main).astype(BF)
        target[k, :, 128:160] = (source[k, :, 128:160].astype(F32) + tail[at, :32]).astype(BF)


SMEM = pl.BlockSpec(memory_space=pltpu.SMEM)
VMEM = pl.BlockSpec(memory_space=pltpu.VMEM)
HBM = pl.BlockSpec(memory_space=pltpu.HBM)
COST = pl.CostEstimate(flops=6 * 10**9, transcendentals=10**6, bytes_accessed=18 * 10**6)
PARAMS = pltpu.CompilerParams(vmem_limit_bytes=48 << 20)


def onehot(rows, cols, match):
    row = lax.broadcasted_iota(jnp.int32, (rows, cols), 0)
    col = lax.broadcasted_iota(jnp.int32, (rows, cols), 1)
    return jnp.where(match(row, col), 1.0, 0.0).astype(BF)


def pack_kernel(place, length, length_l, cols, *refs):
    sources, (block, own_q, own_tree, kept, weight), held, (slices, sems) = refs[:9], refs[9:14], refs[14:23], refs[23:]
    copies = [pltpu.make_async_copy(sources[i], held[i], sems.at[i]) for i in range(9)]
    for copy in copies:
        copy.start()
    parents, parents_l, chosen, queries, queries_l, keys, keys_l, tree, tree_l = held
    tails = 0.0
    for k in range(4):
        weight[k] = cols[k, :, :128]
        tails += dot(cols[k, :, 128:], onehot(32, 128, lambda row, col: col == row + 32 * k))
    weight[4] = tails.astype(BF)
    lanes = lax.broadcasted_iota(jnp.int32, (TREE, 128), 1)
    tile4 = onehot(TREE, 128, lambda row, col: col % 32 == row)
    widen = onehot(TREE, 128, lambda row, col: col == row)
    above = lax.broadcasted_iota(jnp.int32, (TREE, TREE), 0)
    same = above == lax.broadcasted_iota(jnp.int32, (TREE, TREE), 1)
    extras = []
    for copy in copies[:2]:
        copy.wait()
    for i, ids in enumerate((parents, parents_l)):
        reach = jnp.where(same | (above == ids[...]), 1.0, 0.0).astype(BF)
        for _ in range((TREE - 1).bit_length()):
            reach = jnp.minimum(dot(reach, reach), 1.0).astype(BF)
        extra = lax.dot_general(reach, widen, (((0,), (0,)), ((), ())), preferred_element_type=F32)
        if i == 1:
            extra = jnp.where(place[1] == 0, extra, 0.0)
        extra = jnp.where(lanes == 32, length[0, 0].astype(F32), extra)
        extras.append(jnp.where(lanes == 33, length_l[0, 0].astype(F32), extra).astype(BF))
    for copy in copies[2:]:
        copy.wait()
    count = chosen.shape[1]
    pick = jnp.where(lax.broadcasted_iota(jnp.int32, (TREE, count), 0) == chosen[...], 1.0, 0.0).astype(BF)
    kept[...] = lax.dot_general(pick, tree[...], (((0,), (0,)), ((), ())), preferred_element_type=F32).astype(BF)
    for d in range(4):
        block[d, 0:288] = keys[:, :128]
        block[d, 288:576] = keys[:, 128:]
        block[d, 576:864] = keys_l[:, :128]
        block[d, 864:1152] = keys_l[:, 128:]
    for i, rows in enumerate((tree, tree_l)):
        parts = (rows[:, :128], rows[:, 128:KVR], dot(rows[:, KVR:], tile4).astype(BF), extras[i])
        for k, part in enumerate(parts):
            at = slice(TREE * k, TREE * (k + 1))
            if i == 0:
                for d in range(4):
                    block[d, TREE_AT + at.start : TREE_AT + at.stop] = part
            else:
                own_tree[at] = part

    def source(col):
        nope = 96 * (col // NOPE) + col % NOPE
        rope = 96 * ((col - 256) // ROPE) + NOPE + (col - 256) % ROPE
        return jnp.where(col < 256, nope, rope)

    sort = onehot(384, 384, lambda row, col: source(col) == row)
    windows = [slice(384 * w, 384 * (w + 1)) for w in range(HEADS // 4)]
    sorted_all = dot(jnp.concatenate([q[:, cols] for cols in windows for q in (queries, queries_l)], axis=0), sort)
    rope = []
    for w in range(HEADS // 4):
        moved = sorted_all[2 * TREE * w : 2 * TREE * (w + 1)]
        rope.append(moved[:, 256:])
        for half in range(2):
            s, p = divmod(2 * w + half, SLICE // 2)
            part = moved[:, 128 * half : 128 * (half + 1)].astype(BF)
            block[s, QUERY_AT + TREE * p : QUERY_AT + TREE * (p + 1)] = part[:TREE]
            slices[s, TREE * p : TREE * (p + 1)] = part[TREE:]
    wide = lax.broadcasted_iota(jnp.int32, (2 * TREE, 128), 1)
    for s in range(4):
        first = SLICE * s // 4
        for k in range(3):
            if s % 2 == 0:
                part = rope[first + k]
            else:
                after = pltpu.roll(rope[first + k + 1], 64, 1) if k < 2 else jnp.zeros((2 * TREE, 128), F32)
                part = jnp.where(wide < 64, pltpu.roll(rope[first + k], 64, 1), after)
            part = part.astype(BF)
            at = TREE * (5 + k)
            block[s, QUERY_AT + at : QUERY_AT + at + TREE] = part[:TREE]
            slices[s, at : at + TREE] = part[TREE:]
    own_q[...] = slices[place[0]]


def on_device(
    queries, tree_latent, parents, cache, cache_lengths, accepted, residual,
    long_queries, long_tree_latent, long_parents, long_cache, long_plan, long_residual,
    key_up, value_up, out_weight,
):
    y, x = lax.axis_index("y"), lax.axis_index("x")
    place = jnp.stack([x, y]).astype(jnp.int32)
    pairs = [(r * 16 + z, ((z % 4) * 4 + z // 4) * 16 + (z + r) % 16) for r in range(16) for z in range(16)]
    kv, place = lax.optimization_barrier((jnp.concatenate([key_up, value_up], axis=1), place))
    kv = lax.ppermute(kv, ("y", "x", "a", "b"), pairs)
    rows = 8 * TREE
    cols = lax.all_gather(out_weight, "x")
    block, query_l, tree_l, accepted_cache, out_rows = pl.pallas_call(
        pack_kernel,
        out_shape=(
            jax.ShapeDtypeStruct((4, BLOCK, 128), BF),
            jax.ShapeDtypeStruct((rows, 128), BF),
            jax.ShapeDtypeStruct((4 * TREE, 128), BF),
            jax.ShapeDtypeStruct((accepted.shape[2], KVR + ROPE), BF),
            jax.ShapeDtypeStruct((5, out_weight.shape[0], 128), BF),
        ),
        in_specs=[SMEM] * 3 + [VMEM] + [HBM] * 9,
        out_specs=(VMEM,) * 5,
        scratch_shapes=[pltpu.VMEM((1, TREE), jnp.int32)] * 2
        + [pltpu.VMEM((1, accepted.shape[2]), jnp.int32)]
        + [pltpu.VMEM((TREE, HEADS * (NOPE + ROPE)), BF)] * 2
        + [pltpu.VMEM((KVR + ROPE, 256), BF)] * 2
        + [pltpu.VMEM((TREE, KVR + ROPE), BF)] * 2
        + [pltpu.VMEM((4, rows, 128), BF), pltpu.SemaphoreType.DMA((9,))],
        compiler_params=PARAMS,
        cost_estimate=COST,
    )(
        place, cache_lengths, long_plan, cols,
        *[
            pltpu.with_memory_space_constraint(value, pltpu.HBM)
            for value in (
                parents[0], long_parents, accepted[0], queries[0], long_queries[0], cache[0, 0].T, long_cache[0].T,
                tree_latent[0], long_tree_latent[0],
            )
        ],
    )
    block, kv, out_rows = lax.optimization_barrier((block, kv, out_rows))
    got = lax.all_to_all(block, "x", 0, 0)
    out_rows = lax.ppermute(out_rows, ("x", "a"), [(4 * i + j, 4 * j + i) for i in range(4) for j in range(4)])
    kv = lax.all_gather(kv, ("y", "c"))
    kv, out_rows = lax.optimization_barrier((kv, out_rows))
    kv = kv.reshape((4, 2) + kv.shape[1:])

    heads = pl.pallas_call(
        attend_kernel,
        out_shape=jax.ShapeDtypeStruct((4, 5 * TREE * (SLICE // 2) + 3 * TREE, 128), BF),
        in_specs=[VMEM] * 4,
        out_specs=VMEM,
        scratch_shapes=[pltpu.VMEM((5, SLICE * TREE, KVR), BF)],
        compiler_params=PARAMS,
        cost_estimate=COST,
    )(got, query_l, tree_l, kv)
    shared = lax.all_to_all(heads, "y", 0, 0)
    out_rows = lax.all_gather(out_rows, ("b", "c"))
    out_rows = out_rows.reshape((4, 2) + out_rows.shape[1:])
    send = pl.pallas_call(
        project_kernel,
        out_shape=jax.ShapeDtypeStruct((4, 688, 128), BF),
        in_specs=[VMEM, VMEM],
        out_specs=VMEM,
        scratch_shapes=[pltpu.VMEM((TOKENS, SPAN), BF)],
        compiler_params=PARAMS,
    )(shared, out_rows)
    back = lax.all_to_all(send, "x", 0, 0)
    hidden, long_hidden = pl.pallas_call(
        finish_kernel,
        out_shape=(
            jax.ShapeDtypeStruct(residual.shape, BF),
            jax.ShapeDtypeStruct(long_residual.shape, BF),
        ),
        in_specs=[VMEM, VMEM, VMEM],
        out_specs=(VMEM, VMEM),
        scratch_shapes=[pltpu.VMEM((TOKENS, 128), F32)],
        compiler_params=PARAMS,
    )(back, residual, long_residual)
    return hidden, accepted_cache[None, None], long_hidden


def solution(mesh):
    split = Mesh(mesh.devices.reshape(4, 4, 4, 4, 2), ("y", "x", "a", "b", "c"))
    return jax.shard_map(
        on_device,
        mesh=split,
        in_specs=(
            P(ROWS, COLS, None),
            P(ROWS, COLS, None),
            P(ROWS, COLS, None),
            P(ROWS, COLS, None, None),
            P(ROWS, COLS),
            P(ROWS, COLS, None),
            P(None, COLS, ROWS),
            P(COLS, None, None),
            P(COLS, None, None),
            P(COLS, None),
            P(COLS, ROWS, None),
            P(COLS, ROWS),
            P(COLS, None, ROWS),
            P(COLS, None),
            P(COLS, None),
            P(COLS, ROWS),
        ),
        out_specs=(P(None, COLS, ROWS), P(ROWS, COLS, None, None), P(COLS, None, ROWS)),
        check_vma=False,
    )
```
